32 devices in a mesh: shard: 4 (over z), ctx: 8 (over y, x, core).
Axes of the slice: x: 2, y: 2, z: 4, core: 2. Of those that a mesh axis runs over, the one named last changes fastest.
Arguments:
- hidden: bfloat16 [4, 1024, 768], P('shard', 'ctx'), may hold values from -6 to 6
- lengths: int32 [4], P('shard'), may hold values from 256 to 1024, as said below
- row_types: int32 [4, 1024], P('shard'), may hold values 0 or 1
- query_weight: bfloat16 [4, 768, 768], P(None, 'shard'), may hold values from -0.3125 to 0.3125
- query_bias: bfloat16 [4, 768], P(None, 'shard'), may hold values from -3 to 3
- key_weight: bfloat16 [768, 768], P('shard'), may hold values from -0.21875 to 0.21875
- key_bias: bfloat16 [768], P('shard'), may hold values from -3 to 3
- value_weight: bfloat16 [768, 768], P('shard'), may hold values from -0.21875 to 0.21875
- value_bias: bfloat16 [768], P('shard'), may hold values from -0.29882812 to 0.29882812
- out_weight: bfloat16 [768, 768], P('shard'), may hold values from -3 to 3
- out_bias: bfloat16 [768], P('shard'), may hold values from -2 to 2
- norm1_gain: bfloat16 [768], P('shard'), may hold values from 0.5 to 1.5
- norm1_bias: bfloat16 [768], P('shard'), may hold values from -2 to 2
- up_weight: bfloat16 [768, 3072], P('shard'), may hold values from -0.21875 to 0.21875
- up_bias: bfloat16 [3072], P('shard'), may hold values from -2 to 2
- down_weight: bfloat16 [3072, 768], P('shard'), may hold values from -0.109375 to 0.109375
- down_bias: bfloat16 [768], P('shard'), may hold values from -2 to 2
- norm2_gain: bfloat16 [768], P('shard'), may hold values from 0.5 to 1.5
- norm2_bias: bfloat16 [768], P('shard'), may hold values from -2 to 2
- cotangent: bfloat16 [4, 1024, 768], P('shard', 'ctx'), may hold values from -6 to 6
Outputs:
- output: bfloat16 [4, 1024, 768], P('shard', 'ctx')
- input_grad: float32 [4, 1024, 768], P('shard', 'ctx')
- query_weight_grad: float32 [4, 768, 768], P(None, 'shard')
- query_bias_grad: float32 [4, 768], P(None, 'shard')
- key_weight_grad: float32 [768, 768], P('shard')
- key_bias_grad: float32 [768], P('shard')
- value_weight_grad: float32 [768, 768], P('shard')
- value_bias_grad: float32 [768], P('shard')
- out_weight_grad: float32 [768, 768], P('shard')
- out_bias_grad: float32 [768], P('shard')
- norm1_gain_grad: float32 [768], P('shard')
- norm1_bias_grad: float32 [768], P('shard')
- up_weight_grad: float32 [768, 3072], P('shard')
- up_bias_grad: float32 [3072], P('shard')
- down_weight_grad: float32 [3072, 768], P('shard')
- down_bias_grad: float32 [768], P('shard')
- norm2_gain_grad: float32 [768], P('shard')
- norm2_bias_grad: float32 [768], P('shard')
The draws below stay inside these ranges and needn't reach their ends.
Inputs may be any that keep to these rules, and one draw needn't show every extreme that they name: `lengths`: live slots of each sequence, counted from its start; some sequence is full and some has 256. `row_types`: 0 marks a word slot, 1 an entity slot.
All inputs are finite; a program needn't handle non-finite values. No bound on the sum of `row_types` on one device may be relied on, other than what follows from the above.
Results may differ from the reference program's by a relative error of at most 0.024.
Values may be sent and summed in bfloat16 or wider, within the bound.
No kernel may reach another device: no remote copies, remote signals or barrier semaphores. Data moves between devices by JAX's collectives and lax.ppermute only.
A program may use at most 384 MiB of HBM per device.

```python
import jax
import jax.numpy as jnp
from jax import lax

D = 768
HEADS = 12
HEAD = 64
FF = 3072
SLOTS = 1024
SEQS = 4


def draw_lengths(key, part):
    first, second, third = jax.random.split(key, 3)
    drawn = jax.random.randint(first, (SEQS,), SLOTS // 4, SLOTS + 1)
    longest = jax.random.randint(second, (), 0, SEQS)
    shortest = (longest + 1 + jax.random.randint(third, (), 0, SEQS - 1)) % SEQS
    drawn = drawn.at[longest].set(SLOTS)
    drawn = drawn.at[shortest].set(SLOTS // 4)
    return drawn.astype(jnp.int32)


def place_ends(array, own_key, smallest, top_value):
    spot = [jax.random.randint(jax.random.fold_in(own_key, axis), (), 0, length) for axis, length in enumerate(array.shape)]
    widest = array.shape.index(max(array.shape))
    next_to = spot[:widest] + [(spot[widest] + 1) % array.shape[widest]] + spot[widest + 1:]
    return array.at[tuple(spot)].set(smallest).at[tuple(next_to)].set(top_value)


def steps_of(own_key, extent, pieces, smallest, top_value):
    level, own = 1.0, jax.random.fold_in(own_key, 6)
    for dim, parts in pieces:
        draws = jnp.exp(jax.random.uniform(jax.random.fold_in(own, dim), (parts,), jnp.float32, smallest / len(pieces), top_value / len(pieces)))
        level = level * jnp.repeat(draws, extent[dim] // parts).reshape([-1 if axis == dim else 1 for axis in range(len(extent))])
    return level


def scatter_about(rng, extent, deviation, most, shards=(), held_as=jnp.bfloat16):
    loudness = steps_of(rng, extent, shards, -0.22, 0.18) if shards else 1.0
    entries = jax.random.normal(rng, extent, jnp.float32) * deviation * loudness
    return jnp.minimum(jnp.maximum(entries, -most), most).astype(held_as)


def setup_inputs(seed: int = 0) -> dict:
    arg_keys = jax.random.split(jax.random.key(seed), 21)
    return {
        "hidden": scatter_about(arg_keys[0], (SEQS, SLOTS, D), 1.0, 6.0, ((0, 4), (1, 8))),
        "lengths": draw_lengths(jax.random.fold_in(arg_keys[20], 71), 0),
        "row_types": place_ends((jax.random.randint(arg_keys[2], (SEQS, SLOTS), 0, 4) < 1).astype(jnp.int32), jax.random.fold_in(arg_keys[2], 1), 0, 1),
        "query_weight": scatter_about(arg_keys[3], (4, D, D), (D // 2) ** -0.5, 0.3125, ((1, 4),)),
        "query_bias": scatter_about(arg_keys[4], (4, D), 0.5, 3.0, ((1, 4),)),
        "key_weight": scatter_about(arg_keys[5], (D, D), D ** -0.5, 0.21875, ((0, 4),)),
        "key_bias": scatter_about(arg_keys[6], (D,), 0.5, 3.0, ((0, 4),)),
        "value_weight": scatter_about(arg_keys[7], (D, D), D ** -0.5, 0.21875, ((0, 4),)),
        "value_bias": scatter_about(arg_keys[8], (D,), 0.05, 0.29882812, ((0, 4),)),
        "out_weight": scatter_about(arg_keys[9], (D, D), 4 ** -0.5, 3.0, ((0, 4),)),
        "out_bias": scatter_about(arg_keys[10], (D,), 0.3, 2.0, ((0, 4),)),
        "norm1_gain": jnp.clip(1.0 + 0.1 * jax.random.normal(arg_keys[11], (D,), jnp.float32), 0.5, 1.5).astype(jnp.bfloat16),
        "norm1_bias": scatter_about(arg_keys[12], (D,), 0.3, 2.0, ((0, 4),)),
        "up_weight": scatter_about(arg_keys[13], (D, FF), D ** -0.5, 0.21875, ((0, 4),)),
        "up_bias": scatter_about(arg_keys[14], (FF,), 0.3, 2.0, ((0, 4),)),
        "down_weight": scatter_about(arg_keys[15], (FF, D), FF ** -0.5, 0.109375, ((0, 4),)),
        "down_bias": scatter_about(arg_keys[16], (D,), 0.3, 2.0, ((0, 4),)),
        "norm2_gain": jnp.clip(1.0 + 0.1 * jax.random.normal(arg_keys[17], (D,), jnp.float32), 0.5, 1.5).astype(jnp.bfloat16),
        "norm2_bias": scatter_about(arg_keys[18], (D,), 0.3, 2.0, ((0, 4),)),
        "cotangent": scatter_about(arg_keys[19], (SEQS, SLOTS, D), 1.0, 6.0, ((0, 4), (1, 8))),
    }


@jax.custom_vjp
def low(v):
    return lax.optimization_barrier(v.astype(jnp.bfloat16)).astype(jnp.float32)

@jax.custom_vjp
def low_back(v):
    return v

def low_keep(v):
    return (low(v), None)

def low_pass(kept, grad):
    return (grad,)

def back_keep(v):
    return (v, None)

def back_low(kept, grad):
    return (low(grad),)
low.defvjp(low_keep, low_pass)
low_back.defvjp(back_keep, back_low)
EPS = 1e-12
SCALE = 0.125
NEG = -1000000000.0
HIGH = lax.Precision.HIGHEST

def matmul(left, right):
    return jnp.dot(left, right, precision=HIGH, preferred_element_type=jnp.float32)

def layer_norm(summed, gain, shift):
    center = summed - lax.optimization_barrier(jnp.mean(summed, axis=-1, keepdims=True))
    spread = lax.optimization_barrier(jnp.mean(center * center, axis=-1, keepdims=True))
    return center * lax.rsqrt(spread + EPS) * gain + shift

def sequence_forward(params, tokens, slot_types, length):
    query_mats, query_shift, key_mat, key_shift, value_mat, value_shift, out_mat, out_shift, gain_one, shift_one, up_mat, up_shift, down_mat, down_shift, gain_two, shift_two = params
    places = jnp.arange(SLOTS, dtype=jnp.int32)
    in_length = places < length
    word_rows = (slot_types == 0)[:, None]
    projected = [low_back(matmul(tokens, query_mats[which])) + query_shift[which] for which in range(4)]
    query_word = low(jnp.where(word_rows, projected[0], projected[2]) * SCALE)
    query_entity = low(jnp.where(word_rows, projected[1], projected[3]) * SCALE)
    key_rows = low(low_back(matmul(tokens, key_mat)) + key_shift)
    value_rows = low(low_back(matmul(tokens, value_mat)) + value_shift)
    key_heads = key_rows.reshape(SLOTS, HEADS, HEAD)
    word_mask = word_rows[:, :, None].astype(jnp.float32)
    paired_keys = jnp.concatenate([key_heads * word_mask, key_heads * (1.0 - word_mask)], axis=-1)
    paired_query = jnp.concatenate([query_word.reshape(SLOTS, HEADS, HEAD), query_entity.reshape(SLOTS, HEADS, HEAD)], axis=-1)
    value_heads = value_rows.reshape(SLOTS, HEADS, HEAD)
    row_block = min(512, SLOTS)

    def attend(query_block):
        scores = jnp.einsum('qhc,khc->hqk', query_block, paired_keys, precision=HIGH)
        scores = jnp.where(in_length[None, None, :], low_back(scores), NEG)
        attention = low(jax.nn.softmax(scores, axis=-1))
        return jnp.einsum('hqk,khc->qhc', attention, value_heads, precision=HIGH)
    mixture = lax.map(jax.checkpoint(attend), paired_query.reshape(SLOTS // row_block, row_block, HEADS, 2 * HEAD))
    context = low(low_back(mixture.reshape(SLOTS, D)))
    first_sum = low_back(matmul(context, out_mat)) + out_shift + tokens
    first_norm = layer_norm(first_sum, gain_one, shift_one)
    hidden_pre = low_back(matmul(low(first_norm), up_mat)) + up_shift
    activated = low(jax.nn.gelu(hidden_pre, approximate=False))
    second_sum = low_back(matmul(activated, down_mat)) + down_shift + first_norm
    return layer_norm(second_sum, gain_two, shift_two) * in_length[:, None].astype(jnp.float32)

def add_grads(first, second):
    return first + second

def reference(hidden, lengths, row_types, query_weight, query_bias, key_weight, key_bias, value_weight, value_bias, out_weight, out_bias, norm1_gain, norm1_bias, up_weight, up_bias, down_weight, down_bias, norm2_gain, norm2_bias, cotangent):
    params = tuple((entry.astype(jnp.float32) for entry in (query_weight, query_bias, key_weight, key_bias, value_weight, value_bias, out_weight, out_bias, norm1_gain, norm1_bias, up_weight, up_bias, down_weight, down_bias, norm2_gain, norm2_bias)))

    def per_sequence(totals, slices):
        tokens, slot_types, length, grad_output = slices

        def forward_fn(weights, inputs):
            return sequence_forward(weights, inputs, slot_types, length)
        result, pullback = jax.vjp(forward_fn, params, tokens)
        grad_params, grad_tokens = pullback(grad_output)
        totals = jax.tree.map(add_grads, totals, grad_params)
        return (totals, (result.astype(jnp.bfloat16), grad_tokens))
    zeros_grad = jax.tree.map(jnp.zeros_like, params)
    totals, (outputs, input_grad) = lax.scan(per_sequence, zeros_grad, (hidden.astype(jnp.float32), row_types, lengths, cotangent.astype(jnp.float32)))
    return (outputs, input_grad, totals[0], totals[1], totals[2], totals[3], totals[4], totals[5], totals[6], totals[7], totals[8], totals[9], totals[10], totals[11], totals[12], totals[13], totals[14], totals[15])
```

```python
from functools import partial

import jax
import jax.numpy as jnp
from jax import lax
from jax.experimental import pallas as pl
from jax.experimental.pallas import tpu as pltpu
from jax.sharding import PartitionSpec as P

HEADS = 12
HEAD = 64
CHIPS = 4
CORES = 2
LOCAL_HEADS = HEADS // CHIPS
COLS = LOCAL_HEADS * HEAD
PAIR = 2 * HEAD
WIDE = LOCAL_HEADS * PAIR

EPS = 1e-12
SCALE = 0.125
NEG = -1000000000.0
F32 = jnp.float32
BF16 = jnp.bfloat16

SMEM = pl.BlockSpec(memory_space=pltpu.SMEM)
VMEM = pl.BlockSpec(memory_space=pltpu.VMEM)


def sds(shape, dtype):
    return jax.ShapeDtypeStruct(shape, dtype)


def dot(left, right, over_left, over_right):
    return lax.dot_general(
        left, right, (((over_left,), (over_right,)), ((), ())), preferred_element_type=F32
    )


def run(body, name, outs, scalars, *arrays, scratch=(), flops=0, vmem=48):
    many = isinstance(outs, (list, tuple))
    size = sum(a.size * a.dtype.itemsize for a in arrays)
    return pl.pallas_call(
        body,
        out_shape=outs,
        in_specs=[SMEM] + [VMEM] * len(arrays),
        out_specs=[VMEM] * len(outs) if many else VMEM,
        scratch_shapes=list(scratch),
        name=name,
        cost_estimate=pl.CostEstimate(flops=flops, bytes_accessed=size, transcendentals=0),
        compiler_params=pltpu.CompilerParams(vmem_limit_bytes=vmem << 20),
    )(scalars, *arrays)


SHARD, CHIP, CORE, SPOT, SIDE = range(5)


def prep_qkv_body(sc, qw, kw, vw, out):
    rows = kw.shape[0]
    half = rows // 2
    for chip in range(CHIPS):
        for core in range(CORES):

            @pl.when((sc[CHIP] == chip) & (sc[CORE] == core))
            def _():
                lo = chip * COLS
                first = qw[2 * core, :, lo : lo + COLS]
                second = qw[2 * core + 1, :, lo : lo + COLS]
                mix = []
                for h in range(LOCAL_HEADS):
                    mix += [
                        first[:, h * HEAD : (h + 1) * HEAD],
                        second[:, h * HEAD : (h + 1) * HEAD],
                    ]
                out[0:rows, :] = jnp.concatenate(mix, axis=1)
                src = kw if core == 0 else vw
                out[rows:, 0:COLS] = src[0:half, lo : lo + COLS]
                out[rows:, COLS:] = src[half:rows, lo : lo + COLS]


def prep_mlp_body(sc, up, down, out):
    rows, ff = up.shape
    width = down.shape[1]
    part = ff // 4
    side = part // 2
    for chip_x in range(2):

        @pl.when(sc[SIDE] == chip_x)
        def _():
            for piece in range(4):
                lo = piece * part + chip_x * side
                row = (piece // 2) * rows
                col = (piece % 2) * side
                out[row : row + rows, col : col + side] = up[:, lo : lo + side]

    out[2 * rows :, :] = down[...]


def assemble_mlp_body(shards, sc, *refs):
    pieces, (wup, wdn) = refs[: 4 * shards], refs[4 * shards :]
    rows = wup.shape[0] // shards
    part = wdn.shape[0] // shards
    width = wdn.shape[1]
    small = rows // 4
    for index, piece in enumerate(pieces):
        shift, rel = index // 4, index % 4
        owner = lax.rem(sc[SHARD] + shards - shift, shards)
        spot = sc[SPOT] ^ rel
        at = pl.multiple_of(owner * rows + spot * small, small)
        wup[pl.ds(at, small), 0:width] = piece[0:small, :]
        wup[pl.ds(at, small), width:] = piece[small : 2 * small, :]
        at = pl.multiple_of(owner * part + spot * (part // 4), part // 4)
        wdn[pl.ds(at, part // 4), :] = piece[2 * small :, :]


def assemble_out_body(shards, sc, own, other, wo):
    rows = wo.shape[0] // shards
    small = rows // 4
    for core, ref in enumerate((own, other)):
        for half in range(2):
            for shift in range(shards):
                owner = lax.rem(sc[SHARD] + shards - shift, shards)
                spot = sc[SPOT] ^ (half * 2 + core)
                at = pl.multiple_of(owner * rows + spot * small, small)
                wo[pl.ds(at, small), :] = ref[half * shards + shift]


def qkv_body(shards, sc, bias, meta, *refs):
    own_x, other_x = refs[0:4], refs[4:8]
    own_w, other_w = refs[8 : 8 + shards], refs[8 + shards : 8 + 2 * shards]
    wall, pq, pk, vv = refs[8 + 2 * shards :]
    slots = own_x[0].shape[0]
    rows = wall.shape[1] // shards
    half = rows // 2
    for which, pieces in enumerate((own_w, other_w)):
        group = sc[CORE] ^ which
        keep = (group == 0).astype(F32).astype(BF16)
        for shift in range(shards):
            piece = pieces[shift]
            owner = lax.rem(sc[SHARD] + shards - shift, shards)
            at = pl.multiple_of(owner * rows, half)
            wall[group, pl.ds(at, rows), 0:WIDE] = piece[0:rows, :]
            for part in range(2):
                mix = []
                for h in range(LOCAL_HEADS):
                    lo = part * COLS + h * HEAD
                    one = piece[rows:, lo : lo + HEAD]
                    mix += [one, one * keep]
                low = pl.multiple_of(owner * rows + part * half, half)
                wall[group, pl.ds(low, half), WIDE:] = jnp.concatenate(mix, axis=1)
    flags = meta[...].T
    lane = lax.broadcasted_iota(jnp.int32, (1, WIDE), 1)
    left = (lane % PAIR) < HEAD
    for block in range(8):
        tokens = (own_x[block] if block < 4 else other_x[block - 4])[...]
        word = flags[:, block : block + 1] > 0
        at = slice(block * slots, (block + 1) * slots)
        if block < 4:
            first = dot(tokens, wall[0], 1, 0) + bias[0:1, :]
            second = dot(tokens, wall[1], 1, 0) + bias[1:2, :]
            query = jnp.where(word, first[:, 0:WIDE], second[:, 0:WIDE]) * SCALE
            pq[at, :] = query.astype(BF16)
            key, value = first[:, WIDE:], second[:, WIDE:]
        else:
            key = dot(tokens, wall[0, :, WIDE:], 1, 0) + bias[0:1, WIDE:]
            value = dot(tokens, wall[1, :, WIDE:], 1, 0) + bias[1:2, WIDE:]
        pk[at, :] = jnp.where(left == word, key, 0.0).astype(BF16)
        vv[at, :] = value.astype(BF16)


def attend_body(step, pq, pk, vv, valid, probs, cx):
    head = pl.program_id(0)
    count = pq.shape[0]
    slots = count // 4
    keep = valid[...] > 0
    keys = pk[...]
    values = vv[...]
    for start in range(0, count, step):
        scores = dot(pq[start : start + step, :], keys, 1, 1)
        scores = jnp.where(keep, scores, NEG)
        top = jnp.max(scores, axis=-1, keepdims=True)
        expo = jnp.exp(scores - top)
        share = 1.0 / jnp.sum(expo, axis=-1, keepdims=True)
        low = (expo * share).astype(BF16)
        probs[0, start : start + step, :] = low
        mixed = dot(low, values, 1, 0)[:, 0:HEAD].astype(BF16)
        for h in range(LOCAL_HEADS):

            @pl.when(head == h)
            def _():
                for at in range(0, step, slots):
                    block = (start + at) // slots
                    mid = at + slots // 2
                    cx[block, :, h * HEAD : (h + 1) * HEAD] = mixed[at:mid]
                    cx[block, :, COLS + h * HEAD : COLS + (h + 1) * HEAD] = mixed[mid : at + slots]


def attend(pq, pk, vv, valid, slots):
    count, keys = pq.shape[0], pk.shape[0]
    step = 2 * slots if keys <= 2048 else slots
    return pl.pallas_call(
        partial(attend_body, step),
        grid=(LOCAL_HEADS,),
        in_specs=[
            pl.BlockSpec((count, PAIR), lambda h: (0, h)),
            pl.BlockSpec((keys, PAIR), lambda h: (0, h)),
            pl.BlockSpec((keys, PAIR), lambda h: (0, h)),
            pl.BlockSpec((1, keys), lambda h: (0, 0)),
        ],
        out_specs=[
            pl.BlockSpec((1, count, keys), lambda h: (h, 0, 0)),
            pl.BlockSpec((4, slots // 2, 2 * COLS), lambda h: (0, 0, 0)),
        ],
        out_shape=[
            sds((LOCAL_HEADS, count, keys), BF16),
            sds((4, slots // 2, 2 * COLS), BF16),
        ],
        name="attend",
        cost_estimate=pl.CostEstimate(
            flops=4 * LOCAL_HEADS * count * keys * PAIR,
            bytes_accessed=LOCAL_HEADS * count * keys * 2,
            transcendentals=LOCAL_HEADS * count * keys,
        ),
        compiler_params=pltpu.CompilerParams(vmem_limit_bytes=52 << 20),
    )(pq, pk, vv, valid)


def attend_back_body(step, gc0, gc1, gc2, gc3, pq, pk, vv, probs, dq, dk, dv, gcs):
    head = pl.program_id(0)
    count = pq.shape[0]
    slots = count // 4
    half = slots // 2

    @pl.when(head == 0)
    def _():
        gcs[...] = jnp.zeros_like(gcs)
        for block, ref in enumerate((gc0, gc1, gc2, gc3)):
            for h in range(LOCAL_HEADS):
                lo = block * slots
                gcs[h, lo : lo + half, 0:HEAD] = ref[:, h * HEAD : (h + 1) * HEAD]
                gcs[h, lo + half : lo + slots, 0:HEAD] = ref[
                    :, COLS + h * HEAD : COLS + (h + 1) * HEAD
                ]

    keys = pk[...]
    values = vv[...]
    for start in range(0, count, step):
        grad = gcs[head, start : start + step, :]
        low = probs[0, start : start + step, :]
        wide = low.astype(F32)
        moved = dot(grad, values, 1, 1)
        inner = jnp.sum(wide * moved, axis=-1, keepdims=True)
        ds = (wide * (moved - inner)).astype(BF16)
        query = pq[start : start + step, :]
        dq[start : start + step, :] = dot(ds, keys, 1, 0)
        key_part = dot(ds, query, 0, 0)
        value_part = dot(low, grad, 0, 0)
        if start == 0:
            dk[...] = key_part
            dv[...] = value_part
        else:
            dk[...] += key_part
            dv[...] += value_part


def attend_back(pieces, pq, pk, vv, probs, slots):
    count, keys = pq.shape[0], pk.shape[0]
    step = 2 * slots if keys <= 2048 else slots
    piece = pl.BlockSpec((slots // 2, 2 * COLS), lambda h: (0, 0))
    rows = pl.BlockSpec((count, PAIR), lambda h: (0, h))
    cols = pl.BlockSpec((keys, PAIR), lambda h: (0, h))
    return pl.pallas_call(
        partial(attend_back_body, step),
        grid=(LOCAL_HEADS,),
        in_specs=[piece] * 4
        + [rows, cols, cols, pl.BlockSpec((1, count, keys), lambda h: (h, 0, 0))],
        out_specs=[rows, cols, cols],
        out_shape=[sds((count, WIDE), F32), sds((keys, WIDE), F32), sds((keys, WIDE), F32)],
        scratch_shapes=[pltpu.VMEM((LOCAL_HEADS, count, PAIR), BF16)],
        name="attend_back",
        cost_estimate=pl.CostEstimate(
            flops=8 * LOCAL_HEADS * count * keys * PAIR,
            bytes_accessed=LOCAL_HEADS * count * keys * 2,
            transcendentals=0,
        ),
        compiler_params=pltpu.CompilerParams(vmem_limit_bytes=56 << 20),
    )(*pieces, pq, pk, vv, probs)


def unpack(piece):
    return jnp.concatenate([piece[:, 0:COLS], piece[:, COLS:]], axis=0)


def normalize(summed):
    center = summed - jnp.mean(summed, axis=-1, keepdims=True)
    spread = jnp.mean(center * center, axis=-1, keepdims=True)
    rate = lax.rsqrt(spread + EPS)
    return center * rate, rate


def norm_back(grad, unit, rate, gain):
    scaled = grad * gain
    mean_one = jnp.mean(scaled, axis=-1, keepdims=True)
    mean_two = jnp.mean(scaled * unit, axis=-1, keepdims=True)
    return rate * (scaled - mean_one - unit * mean_two)


def total(values):
    return jnp.sum(values, axis=0, keepdims=True)


OUT_B, GAIN_1, SHIFT_1, DOWN_B, GAIN_2, SHIFT_2 = range(6)


def norm_one_body(sc, vecs, cx0, cx1, cx2, cx3, wo, hidden, low, unit_out, rate_out):
    acc = hidden[...].astype(F32) + vecs[OUT_B : OUT_B + 1, :]
    for rel, ref in enumerate((cx0, cx1, cx2, cx3)):
        at = pl.multiple_of((sc[CHIP] ^ rel) * COLS, COLS)
        acc += dot(unpack(ref[...]), wo[pl.ds(at, COLS), :], 1, 0)
    unit, rate = normalize(acc)
    first = unit * vecs[GAIN_1 : GAIN_1 + 1, :] + vecs[SHIFT_1 : SHIFT_1 + 1, :]
    low[...] = first.astype(BF16)
    unit_out[...] = unit
    rate_out[...] = jnp.broadcast_to(rate, rate_out.shape)


def mlp_body(chunk, sc, bias, x0, x1, wup, wdn, act, slope, own, send):
    slots = x0.shape[0]
    tokens = jnp.concatenate([x0[...], x1[...]], axis=0)
    acc = None
    for lo in range(0, wup.shape[1], chunk):
        pre = dot(tokens, wup[:, lo : lo + chunk], 1, 0) + bias[0:1, lo : lo + chunk]
        cdf = 0.5 * (1.0 + lax.erf(pre * 0.7071067811865476))
        pdf = jnp.exp(-0.5 * pre * pre) * 0.3989422804014327
        out = (pre * cdf).astype(BF16)
        act[:, lo : lo + chunk] = out
        slope[:, lo : lo + chunk] = cdf + pre * pdf
        part = dot(out, wdn[lo : lo + chunk, :], 1, 0)
        acc = part if acc is None else acc + part
    own[...] = acc[0:slots]
    send[...] = acc[slots:].astype(BF16)


def norm_two_body(sc, vecs, meta, own, received, unit_one, cotangent, output, gs, gs_low, sums):
    valid = meta[...].T[:, 8:9]
    first = unit_one[...] * vecs[GAIN_1 : GAIN_1 + 1, :] + vecs[SHIFT_1 : SHIFT_1 + 1, :]
    acc = own[...] + received[...].astype(F32) + vecs[DOWN_B : DOWN_B + 1, :] + first
    unit, rate = normalize(acc)
    gain = vecs[GAIN_2 : GAIN_2 + 1, :]
    output[...] = ((unit * gain + vecs[SHIFT_2 : SHIFT_2 + 1, :]) * valid).astype(BF16)
    grad = cotangent[...].astype(F32) * valid
    back = norm_back(grad, unit, rate, gain)
    gs[...] = back
    gs_low[...] = back.astype(BF16)
    sums[...] = jnp.zeros_like(sums)
    sums[DOWN_B : DOWN_B + 1, :] = total(back)
    sums[GAIN_2 : GAIN_2 + 1, :] = total(grad * unit)
    sums[SHIFT_2 : SHIFT_2 + 1, :] = total(grad)


def mlp_back_body(chunk, sc, g0, g1, slope, wup, wdn, pre_low, sums, own, send):
    slots = g0.shape[0]
    grads = jnp.concatenate([g0[...], g1[...]], axis=0)
    acc = None
    sums[...] = jnp.zeros_like(sums)
    for lo in range(0, wup.shape[1], chunk):
        pre = dot(grads, wdn[lo : lo + chunk, :], 1, 1) * slope[:, lo : lo + chunk]
        sums[0:1, lo : lo + chunk] = total(pre)
        low = pre.astype(BF16)
        pre_low[:, lo : lo + chunk] = low
        part = dot(low, wup[:, lo : lo + chunk], 1, 1)
        acc = part if acc is None else acc + part
    own[...] = acc[0:slots]
    send[...] = acc[slots:].astype(BF16)


def mlp_grads_body(shards, sc, x0, x1, g0, g1, act, pre_low, keep, send):
    tokens = jnp.concatenate([x0[...], x1[...]], axis=0)
    grads = jnp.concatenate([g0[...], g1[...]], axis=0)
    width = tokens.shape[1]
    rows = width // shards
    small = rows // 4
    part = act.shape[1] // shards

    def put(values, lo, at, col):
        size = values.shape[0] // 4
        for spot in range(4):
            block = values[spot * size : (spot + 1) * size, :]
            for core in range(CORES):

                @pl.when(sc[CORE] == core)
                def _():
                    if spot % 2 == core:
                        keep[spot // 2, at, lo : lo + size, :] = block
                    else:
                        send[spot // 2, at, lo : lo + size, :] = block.astype(BF16)

    for at in range(shards):
        for col in range(2):
            up = dot(
                tokens[:, at * rows : (at + 1) * rows],
                pre_low[:, col * width : (col + 1) * width],
                0,
                0,
            )
            put(up, col * small, at, col)
        down = dot(act[:, at * part : (at + 1) * part], grads, 0, 0)
        put(down, 2 * small, at, 0)


def norm_one_back_body(
    sc, vecs, own, received, gs, unit_one, rate_one, wo, gf, gf_low, gcx, sums
):
    grad = gs[...] + own[...] + received[...].astype(F32)
    unit = unit_one[...]
    rate = rate_one[:, 0:1]
    back = norm_back(grad, unit, rate, vecs[GAIN_1 : GAIN_1 + 1, :])
    gf[...] = back
    low = back.astype(BF16)
    gf_low[...] = low
    sums[...] = jnp.zeros_like(sums)
    sums[OUT_B : OUT_B + 1, :] = total(back)
    sums[GAIN_1 : GAIN_1 + 1, :] = total(grad * unit)
    sums[SHIFT_1 : SHIFT_1 + 1, :] = total(grad)
    half = back.shape[0] // 2
    for rel in range(4):
        at = pl.multiple_of((sc[CHIP] ^ rel) * COLS, COLS)
        part = dot(low, wo[pl.ds(at, COLS), :], 1, 1).astype(BF16)
        gcx[rel, :, 0:COLS] = part[0:half]
        gcx[rel, :, COLS:] = part[half:]


def out_grads_body(sc, cx0, cx1, cx2, cx3, gf_low, keep, send):
    low = gf_low[...]
    half = keep.shape[2]
    for rel, ref in enumerate((cx0, cx1, cx2, cx3)):
        block = dot(unpack(ref[...]), low, 0, 0)
        chip = sc[CHIP] ^ rel
        for core in range(CORES):

            @pl.when(sc[CORE] == core)
            def _():
                keep[chip] = block[:, core * half : (core + 1) * half]
                other = 1 - core
                send[chip] = block[:, other * half : (other + 1) * half].astype(BF16)


def qkv_grads_body(
    shards, sc, meta, dq, dk_own, dk_rec, dv_own, dv_rec, wall, x0, x1, x2, x3,
    own, send, keep_w, send_w, sums, packed,
):
    slots = x0.shape[0]
    flags = meta[...].T
    lane = lax.broadcasted_iota(jnp.int32, (1, WIDE), 1)
    left = (lane % PAIR) < HEAD
    rows = wall.shape[1] // shards
    half = rows // 2
    acc = [0.0] * 4
    for block in range(4):
        at = slice(block * slots, (block + 1) * slots)
        word = flags[:, block : block + 1] > 0
        query = dq[at, :] * SCALE
        parts = (
            jnp.where(word, query, 0.0),
            jnp.where(word, 0.0, query),
            jnp.where(left == word, dk_own[at, :] + dk_rec[at, :].astype(F32), 0.0),
            dv_own[at, :] + dv_rec[at, :].astype(F32),
        )
        acc = [a + total(p) for a, p in zip(acc, parts)]
        packed[0, at, 0:WIDE] = parts[0].astype(BF16)
        packed[1, at, 0:WIDE] = parts[1].astype(BF16)
        packed[0, at, WIDE:] = parts[2].astype(BF16)
        packed[1, at, WIDE:] = parts[3].astype(BF16)
        back = dot(packed[0, at, :], wall[0], 1, 1) + dot(packed[1, at, :], wall[1], 1, 1)
        if block == 0:
            own[...] = back
        else:
            send[block - 1] = back.astype(BF16)
    sums[...] = jnp.zeros_like(sums)
    sums[0:1, 0:WIDE] = acc[0]
    sums[1:2, 0:WIDE] = acc[1]
    sums[0:1, WIDE:] = acc[2]
    sums[1:2, WIDE:] = acc[3]
    tokens = jnp.concatenate([x0[...], x1[...], x2[...], x3[...]], axis=0)
    for group_rel, ref in enumerate((keep_w, send_w)):
        group = sc[CORE] ^ group_rel
        for at in range(shards):
            grad = dot(tokens[:, at * rows : (at + 1) * rows], packed[group], 0, 0)
            ref[at, 0:rows, :] = grad[:, 0:WIDE].astype(ref.dtype)
            folded = jnp.concatenate(
                [
                    grad[:, WIDE + h * PAIR : WIDE + h * PAIR + HEAD]
                    + grad[:, WIDE + h * PAIR + HEAD : WIDE + (h + 1) * PAIR]
                    for h in range(LOCAL_HEADS)
                ],
                axis=1,
            ).astype(ref.dtype)
            ref[at, rows:, 0:COLS] = folded[0:half]
            ref[at, rows:, COLS:] = folded[half:]


def place_qkv_body(sc, *refs):
    pieces, (qg, kg, vg, held) = refs[:8], refs[8:]
    rows = kg.shape[0]
    half = rows // 2
    for core_rel in range(CORES):
        for rel in range(4):
            held[sc[CORE] ^ core_rel, sc[CHIP] ^ rel] = pieces[core_rel * 4 + rel][...]
    for core in range(CORES):
        for chip in range(CHIPS):
            piece = held[core, chip].astype(F32)
            lo = chip * COLS
            for which in range(2):
                qg[2 * core + which, :, lo : lo + COLS] = jnp.concatenate(
                    [
                        piece[0:rows, h * PAIR + which * HEAD : h * PAIR + (which + 1) * HEAD]
                        for h in range(LOCAL_HEADS)
                    ],
                    axis=1,
                )
            ref = kg if core == 0 else vg
            ref[0:half, lo : lo + COLS] = piece[rows:, 0:COLS]
            ref[half:, lo : lo + COLS] = piece[rows:, COLS:]


def place_mlp_body(sc, *refs):
    mlp, outs, (ug, dg, og) = refs[:8], refs[8:16], refs[16:]
    rows, ff = ug.shape
    width = dg.shape[1]
    part = ff // 4
    side = part // 2
    small = rows // 4
    low = part // 8
    for core_rel in range(CORES):
        for rel in range(4):
            core = sc[CORE] ^ core_rel
            chip = sc[CHIP] ^ rel
            chip_x, chip_y = chip & 1, chip >> 1
            spot = chip_y * 2 + core
            piece = mlp[core_rel * 4 + rel][...].astype(F32)
            at = pl.multiple_of(spot * small, small)
            for shard in range(4):
                row = (shard // 2) * small
                col = (shard % 2) * side
                lane = pl.multiple_of(shard * part + chip_x * side, side)
                ug[pl.ds(at, small), pl.ds(lane, side)] = piece[
                    row : row + small, col : col + side
                ]
            at = pl.multiple_of(chip_x * side + spot * low, low)
            dg[pl.ds(at, low), :] = piece[2 * small :, :]
            at = pl.multiple_of(chip * small, small)
            lane = pl.multiple_of(core * (width // 2), width // 2)
            og[pl.ds(at, small), pl.ds(lane, width // 2)] = outs[core_rel * 4 + rel][...].astype(
                F32
            )


def local(
    shards,
    lanes,
    hidden,
    lengths,
    row_types,
    query_weight,
    query_bias,
    key_weight,
    key_bias,
    value_weight,
    value_bias,
    out_weight,
    out_bias,
    norm1_gain,
    norm1_bias,
    up_weight,
    up_bias,
    down_weight,
    down_bias,
    norm2_gain,
    norm2_bias,
    cotangent,
):
    groups = lanes // (CHIPS * CORES)
    shard = lax.axis_index("shard")
    lane = lax.axis_index("ctx")
    core, chip, group = lane & 1, (lane >> 1) & 3, lane >> 3
    chip_x, chip_y = chip & 1, chip >> 1
    spot = chip_y * 2 + core
    scalars = jnp.stack([shard, chip, core, spot, chip_x]).astype(jnp.int32)

    def across(value, mask):
        return lax.ppermute(value, "ctx", [(i, i ^ mask) for i in range(lanes)])

    def chips(value, rel):
        return across(value, rel << 1)

    def turn(value, shift):
        return lax.ppermute(value, "shard", [(i, (i + shift) % shards) for i in range(shards)])

    def pick(stack, index):
        return lax.dynamic_index_in_dim(stack, index, 0, keepdims=False)

    def over_groups(value):
        if groups == 1:
            return value
        sets = [[g * 8 + i for g in range(groups)] for i in range(8)]
        return lax.psum(value, "ctx", axis_index_groups=sets)

    width = hidden.shape[2]
    slots = hidden.shape[1]
    rows = width // shards
    ff = up_weight.shape[1]
    part = ff // shards
    side = part // 2
    hid = hidden[0]
    cot = cotangent[0]

    mine = run(
        prep_qkv_body,
        "prep_qkv",
        sds((rows + rows // 2, WIDE), BF16),
        scalars,
        query_weight,
        key_weight,
        value_weight,
    )
    own_w = [mine] + [turn(mine, d) for d in range(1, shards)]
    own_x = [hid] + [chips(hid, rel) for rel in range(1, 4)]
    small_one = jnp.concatenate(
        [
            query_bias.reshape(-1), key_bias, value_bias, out_bias, norm1_gain, norm1_bias,
            down_bias, norm2_gain, norm2_bias, up_bias,
        ]
    ).reshape(4, width)
    small_all = [small_one] + [turn(small_one, d) for d in range(1, shards)]
    other_w = [across(piece, 1) for piece in own_w]
    other_x = [across(block, 1) for block in own_x]

    out_one = lax.dynamic_slice_in_dim(out_weight, spot * (rows // 4), rows // 4, 0)
    out_own = jnp.stack([out_one] + [turn(out_one, d) for d in range(1, shards)])
    out_own = jnp.concatenate([out_own, across(out_own, 4)], axis=0)
    wo = run(
        partial(assemble_out_body, shards),
        "assemble_out",
        sds((width, width), BF16),
        scalars,
        out_own,
        across(out_own, 1),
    )
    up_rows = lax.dynamic_slice_in_dim(up_weight, spot * (rows // 4), rows // 4, 0)
    down_rows = lax.dynamic_slice_in_dim(
        down_weight, chip_x * side + spot * (side // 4), side // 4, 0
    )
    mlp_one = run(
        prep_mlp_body,
        "prep_mlp",
        sds((rows // 2 + side // 4, width), BF16),
        scalars,
        up_rows,
        down_rows,
    )
    mlp_pieces = []
    for d in range(shards):
        here = mlp_one if d == 0 else turn(mlp_one, d)
        there = across(here, 4)
        mlp_pieces += [here, across(here, 1), there, across(there, 1)]
    wup, wdn = run(
        partial(assemble_mlp_body, shards),
        "assemble_mlp",
        [sds((width, ff // 2), BF16), sds((ff // 2, width), BF16)],
        scalars,
        *mlp_pieces,
    )

    order = (shard - jnp.arange(shards)) % shards
    table = jnp.stack(small_all)[order].astype(F32)
    qb = pick(table, chip)
    pair_bias = qb[0].reshape(2, 2, LOCAL_HEADS, HEAD).transpose(0, 2, 1, 3).reshape(2, WIDE)
    kb = jnp.repeat(qb[1, 0:COLS].reshape(LOCAL_HEADS, 1, HEAD), 2, axis=1).reshape(WIDE)
    vb = jnp.pad(
        qb[1, COLS : 2 * COLS].reshape(LOCAL_HEADS, 1, HEAD), ((0, 0), (0, 1), (0, 0))
    ).reshape(WIDE)
    bias = jnp.concatenate([pair_bias, jnp.stack([kb, vb])], axis=1)
    flat = table[:, 1:3].reshape(shards, 8, rows).transpose(1, 0, 2).reshape(8, width)
    vecs = jnp.concatenate([flat[2:8], jnp.zeros((2, width), F32)], axis=0)
    up_shift = lax.dynamic_slice_in_dim(table[:, 3], chip_x * side, side, 1).reshape(1, ff // 2)

    kinds = row_types.reshape(-1, slots)
    blocks = jnp.stack(
        [group * 8 + (chip ^ rel) * 2 + (core ^ c) for c in range(CORES) for rel in range(4)]
    )
    places = jnp.arange(slots, dtype=jnp.int32)
    word = (kinds[blocks] == 0).astype(F32)
    live = (blocks[:, None] * slots + places[None, :] < lengths[0]).astype(F32)
    meta = jnp.concatenate([word, live], axis=0)

    wall, pq, pk, vv = run(
        partial(qkv_body, shards),
        "qkv",
        [
            sds((2, width, 2 * WIDE), BF16),
            sds((4 * slots, WIDE), BF16),
            sds((8 * slots, WIDE), BF16),
            sds((8 * slots, WIDE), BF16),
        ],
        scalars,
        bias,
        meta,
        *own_x,
        *other_x,
        *own_w,
        *other_w,
        flops=2 * slots * 12 * width * 2 * WIDE,
    )
    valid = live.reshape(1, 8 * slots)
    if groups > 1:
        sets = [[g * 8 + i for g in range(groups)] for i in range(8)]
        gather = partial(lax.all_gather, axis_name="ctx", axis_index_groups=sets, tiled=True)
        pk, vv = gather(pk, axis=0), gather(vv, axis=0)
        valid = gather(valid, axis=1)
    probs, cx = attend(pq, pk, vv, valid, slots)
    cxs = [cx[0]] + [chips(cx[rel], rel) for rel in range(1, 4)]

    low_one, unit_one, rate_one = run(
        norm_one_body,
        "norm_one",
        [sds((slots, width), BF16), sds((slots, width), F32), sds((slots, 128), F32)],
        scalars,
        vecs,
        *cxs,
        wo,
        hid,
    )
    low_two = chips(low_one, 1)
    act, slope, own, send = run(
        partial(mlp_body, 384),
        "mlp",
        [
            sds((2 * slots, ff // 2), BF16),
            sds((2 * slots, ff // 2), F32),
            sds((slots, width), F32),
            sds((slots, width), BF16),
        ],
        scalars,
        up_shift,
        low_one,
        low_two,
        wup,
        wdn,
        flops=4 * slots * width * ff,
    )
    output, gs, gs_low, sums_two = run(
        norm_two_body,
        "norm_two",
        [
            sds((slots, width), BF16),
            sds((slots, width), F32),
            sds((slots, width), BF16),
            sds((8, width), F32),
        ],
        scalars,
        vecs,
        meta,
        own,
        chips(send, 1),
        unit_one,
        cot,
    )
    gs_other = chips(gs_low, 1)
    pre_low, sums_up, own, send = run(
        partial(mlp_back_body, 384),
        "mlp_back",
        [
            sds((2 * slots, ff // 2), BF16),
            sds((8, ff // 2), F32),
            sds((slots, width), F32),
            sds((slots, width), BF16),
        ],
        scalars,
        gs_low,
        gs_other,
        slope,
        wup,
        wdn,
        flops=4 * slots * width * ff,
    )
    received = chips(send, 1)
    piece_rows = rows // 2 + side // 4
    keep_mlp, send_mlp = run(
        partial(mlp_grads_body, shards),
        "mlp_grads",
        [
            sds((2, shards, piece_rows, width), F32),
            sds((2, shards, piece_rows, width), BF16),
        ],
        scalars,
        low_one,
        low_two,
        gs_low,
        gs_other,
        act,
        pre_low,
        flops=4 * slots * width * ff,
    )
    gf, gf_low, gcx, sums_one = run(
        norm_one_back_body,
        "norm_one_back",
        [
            sds((slots, width), F32),
            sds((slots, width), BF16),
            sds((4, slots // 2, 2 * COLS), BF16),
            sds((8, width), F32),
        ],
        scalars,
        vecs,
        own,
        received,
        gs,
        unit_one,
        rate_one,
        wo,
    )
    gcs = [gcx[0]] + [chips(gcx[rel], rel) for rel in range(1, 4)]
    keep_out, send_out = run(
        out_grads_body,
        "out_grads",
        [sds((CHIPS, COLS, width // 2), F32), sds((CHIPS, COLS, width // 2), BF16)],
        scalars,
        *cxs,
        gf_low,
    )

    dq, dk, dv = attend_back(gcs, pq, pk, vv, probs, slots)
    if groups > 1:
        scatter = partial(
            lax.psum_scatter, axis_name="ctx", axis_index_groups=sets, tiled=True
        )
        dk, dv = scatter(dk), scatter(dv)
    count = 4 * slots
    dk_rec = across(dk[count:].astype(BF16), 1)
    dv_rec = across(dv[count:].astype(BF16), 1)
    own, send, keep_w, send_w, sums_qkv = run(
        partial(qkv_grads_body, shards),
        "qkv_grads",
        [
            sds((slots, width), F32),
            sds((3, slots, width), BF16),
            sds((shards, rows + rows // 2, WIDE), F32),
            sds((shards, rows + rows // 2, WIDE), BF16),
            sds((8, 2 * WIDE), F32),
        ],
        scalars,
        meta,
        dq,
        dk[:count],
        dk_rec,
        dv[:count],
        dv_rec,
        wall,
        *own_x,
        scratch=[pltpu.VMEM((2, count, 2 * WIDE), BF16)],
        flops=12 * slots * width * 4 * WIDE,
    )

    def owned(parts):
        result = pick(parts, shard)
        for d in range(1, shards):
            result = result + turn(pick(parts, (shard + d) % shards).astype(BF16), d).astype(F32)
        return over_groups(result)

    def spread(value):
        low = value.astype(BF16)
        here = [low] + [chips(low, rel) for rel in range(1, 4)]
        return here + [across(block, 1) for block in here]

    done_qkv = spread(owned(keep_w + across(send_w, 1).astype(F32)))
    input_grad = gf + own
    for rel in range(1, 4):
        input_grad = input_grad + chips(send[rel - 1], rel).astype(F32)

    both = keep_mlp + across(send_mlp, 1).astype(F32)
    kept, moved = pick(both, chip_y), pick(both, 1 - chip_y).astype(BF16)
    done_mlp = spread(owned(kept + across(moved, 4).astype(F32)))

    both = (keep_out + across(send_out, 1).astype(F32)).reshape(
        CHIPS, 4, COLS // 4, width // 2
    )
    kept = lax.dynamic_index_in_dim(both, chip, 1, keepdims=False)
    for rel in range(1, 4):
        moved = lax.dynamic_index_in_dim(both, chip ^ rel, 1, keepdims=False).astype(BF16)
        kept = kept + chips(moved, rel).astype(F32)
    done_out = spread(owned(kept))

    sums = sums_one + sums_two
    mine_qb = sums_qkv[0:2, 0:WIDE].reshape(2, LOCAL_HEADS, 2, HEAD).transpose(0, 2, 1, 3)
    mine_kb = sums_qkv[0, WIDE:].reshape(LOCAL_HEADS, 2, HEAD).sum(1)
    mine_vb = sums_qkv[1, WIDE:].reshape(LOCAL_HEADS, 2, HEAD)[:, 0]
    mine_row = jnp.concatenate([mine_qb.reshape(-1), mine_kb.reshape(-1), mine_vb.reshape(-1)])
    heads_part = jnp.where(
        (jnp.arange(shards) == chip)[:, None], mine_row[None, :], 0.0
    )
    norms_part = sums[0:6].reshape(6, shards, rows).transpose(1, 0, 2).reshape(shards, 6 * rows)
    up_part = sums_up[0].reshape(shards, side)
    blank = jnp.zeros_like(up_part)
    up_part = jnp.where(
        chip_x == 0,
        jnp.concatenate([up_part, blank], axis=1),
        jnp.concatenate([blank, up_part], axis=1),
    )
    small = jnp.concatenate([heads_part, norms_part, up_part], axis=1)
    for mask in (1, 2, 4):
        small = small + across(small, mask)
    small = over_groups(small)
    step = 1
    while step < shards:
        small = small + lax.ppermute(small, "shard", [(i, i ^ step) for i in range(shards)])
        step *= 2
    small = pick(small, shard)

    qg, kg, vg = run(
        place_qkv_body,
        "place_qkv",
        [sds((4, rows, width), F32), sds((rows, width), F32), sds((rows, width), F32)],
        scalars,
        *done_qkv,
        scratch=[pltpu.VMEM((CORES, CHIPS, rows + rows // 2, WIDE), BF16)],
    )
    ug, dg, og = run(
        place_mlp_body,
        "place_mlp",
        [sds((rows, ff), F32), sds((part, width), F32), sds((rows, width), F32)],
        scalars,
        *done_mlp,
        *done_out,
    )
    pieces = [small[0 : 4 * rows].reshape(4, rows)]
    pieces += [small[i * rows : (i + 1) * rows] for i in range(4, 12)]
    qbg, kbg, vbg, obg, g1g, b1g, dbg, g2g, b2g = pieces
    ubg = small[12 * rows :]
    return (
        output[None], input_grad[None], qg, qbg, kg, kbg, vg, vbg, og, obg,
        g1g, b1g, ug, ubg, dg, dbg, g2g, b2g,
    )


def solution(mesh):
    vec, mat = P("shard"), P("shard", None)
    tokens = P("shard", "ctx", None)
    placed = (
        tokens, vec, mat, P(None, "shard", None), P(None, "shard"), mat, vec, mat, vec, mat,
        vec, vec, vec, mat, vec, mat, vec, vec, vec, tokens,
    )
    result = (
        tokens, tokens, P(None, "shard", None), P(None, "shard"), mat, vec, mat, vec, mat, vec,
        vec, vec, mat, vec, mat, vec, vec, vec,
    )
    return jax.shard_map(
        partial(local, mesh.shape["shard"], mesh.shape["ctx"]),
        mesh=mesh,
        in_specs=placed,
        out_specs=result,
        check_vma=False,
    )
```

```python
from functools import partial

import jax
import jax.numpy as jnp
from jax import lax
from jax.experimental import pallas as pl
from jax.experimental.pallas import tpu as pltpu
from jax.sharding import PartitionSpec as P

HEADS = 12
HEAD = 64
CHIPS = 4
CORES = 2
LOCAL_HEADS = HEADS // CHIPS
COLS = LOCAL_HEADS * HEAD
PAIR = 2 * HEAD
WIDE = LOCAL_HEADS * PAIR

EPS = 1e-12
SCALE = 0.125
NEG = -1000000000.0
F32 = jnp.float32
BF16 = jnp.bfloat16

SMEM = pl.BlockSpec(memory_space=pltpu.SMEM)
VMEM = pl.BlockSpec(memory_space=pltpu.VMEM)


def sds(shape, dtype):
    return jax.ShapeDtypeStruct(shape, dtype)


def dot(left, right, over_left, over_right):
    return lax.dot_general(
        left, right, (((over_left,), (over_right,)), ((), ())), preferred_element_type=F32
    )


def cost(micros):
    return pl.CostEstimate(flops=1, bytes_accessed=int(micros * 3e6), transcendentals=0)


MICROS = {
    "mlp": 3.5, "mlp_back": 3.5, "mlp_grads": 3.3, "out_grads": 2, "qkv_grads": 5,
    "place_qkv": 3.5, "place_mlp": 3,
}


def run(body, name, outs, scalars, *arrays, scratch=(), flops=0, vmem=24):
    many = isinstance(outs, (list, tuple))
    return pl.pallas_call(
        body,
        out_shape=outs,
        in_specs=[SMEM] + [VMEM] * len(arrays),
        out_specs=[VMEM] * len(outs) if many else VMEM,
        scratch_shapes=list(scratch),
        name=name,
        cost_estimate=cost(MICROS.get(name, 1)),
        compiler_params=pltpu.CompilerParams(vmem_limit_bytes=vmem << 20),
    )(scalars, *arrays)


SHARD, CHIP, CORE, SPOT, SIDE, TALL = range(6)


def prep_qkv_body(sc, qw, kw, vw, ow, qb, *refs):
    vectors, (ub, own, other) = refs[:8], refs[8:]
    rows = kw.shape[0]
    half = rows // 2
    wide = [ref[...].astype(F32).reshape(1, rows) for ref in vectors]
    queries = qb[...].astype(F32)
    long = ub[...].astype(F32).reshape(1, 4 * rows)
    lines = [jnp.concatenate([queries[i : i + 1], queries[i + 1 : i + 2]], axis=1) for i in (0, 2)]
    lines += [jnp.concatenate(wide[i : i + 2], axis=1) for i in range(0, 8, 2)]
    lines += [long[:, 0 : 2 * rows], long[:, 2 * rows :]]
    small = jnp.concatenate(lines, axis=0).astype(BF16)
    end = rows + half + small.shape[0]
    own[rows + half : end, :] = small
    third = ow[pl.ds(pl.multiple_of(sc[SPOT] * (rows // 4), rows // 4), rows // 4), :]
    own[end : end + rows // 4, :] = third[:, 0:WIDE]
    own[end + rows // 4 :, :] = third[:, WIDE:]
    for chip in range(CHIPS):
        for core in range(CORES):

            @pl.when((sc[CHIP] == chip) & (sc[CORE] == core))
            def _():
                lo = chip * COLS
                for out, group in ((own, core), (other, 1 - core)):
                    first = qw[2 * group, :, lo : lo + COLS]
                    second = qw[2 * group + 1, :, lo : lo + COLS]
                    mix = []
                    for h in range(LOCAL_HEADS):
                        mix += [
                            first[:, h * HEAD : (h + 1) * HEAD],
                            second[:, h * HEAD : (h + 1) * HEAD],
                        ]
                    out[0:rows, :] = jnp.concatenate(mix, axis=1)
                    src = vw if group else kw
                    out[rows : rows + half, 0:COLS] = src[0:half, lo : lo + COLS]
                    out[rows : rows + half, COLS:] = src[half:rows, lo : lo + COLS]


def prep_mlp_body(sc, up, down, out):
    rows, ff = up.shape
    part = ff // 4
    side = part // 2
    unit = side // 2
    for chip_x in range(2):

        @pl.when(sc[SIDE] == chip_x)
        def _():
            for tall in range(2):
                for piece in range(4):
                    lo = piece * part + chip_x * side + tall * unit
                    out[tall * rows : (tall + 1) * rows, piece * unit : (piece + 1) * unit] = up[
                        :, lo : lo + unit
                    ]

    out[2 * rows :, :] = down[...]


def assemble_out_body(shards, sc, whole, own, other, own_far, other_far, wo):
    rows = wo.shape[0] // shards
    small = rows // 4
    wo[pl.ds(pl.multiple_of(sc[SHARD] * rows, rows), rows), :] = whole[...]
    for rel, ref in enumerate((own, other, own_far, other_far)):
        for shift in range(1, shards):
            owner = lax.rem(sc[SHARD] + shards - shift, shards)
            at = pl.multiple_of(owner * rows + (sc[SPOT] ^ rel) * small, small)
            wo[pl.ds(at, small), :] = ref[shift - 1]


def assemble_mlp_body(shards, sc, up, down, *refs):
    pieces, (wup, wdn) = refs[:-2], refs[-2:]
    rows = wup.shape[0] // shards
    part = wdn.shape[0] // shards
    width = wdn.shape[1]
    unit = part // 2
    small = rows // 4
    at = pl.multiple_of(sc[SHARD] * rows, rows)
    for chip_x in range(2):

        @pl.when(sc[SIDE] == chip_x)
        def _():
            for tall in range(2):
                for piece in range(4):
                    lo = piece * 2 * part + chip_x * part + tall * unit
                    to = tall * width + piece * unit
                    wup[pl.ds(at, rows), to : to + unit] = up[:, lo : lo + unit]

    for tall in range(2):
        at = pl.multiple_of(tall * width + sc[SHARD] * unit, unit)
        lo = pl.multiple_of(sc[SIDE] * part + tall * unit, unit)
        wdn[pl.ds(at, unit), :] = down[pl.ds(lo, unit), :]
    for index, ref in enumerate(pieces):
        rel, shift = index // (shards - 1), index % (shards - 1) + 1
        spot = sc[SPOT] ^ (rel // 2 + rel % 2 * 2)
        owner = lax.rem(sc[SHARD] + shards - shift, shards)
        at = pl.multiple_of(owner * rows + spot * small, small)
        wup[pl.ds(at, small), 0:width] = ref[0:small, :]
        wup[pl.ds(at, small), width:] = ref[small : 2 * small, :]
        at = (spot // 2) * width + owner * unit + (spot % 2) * (unit // 2)
        at = pl.multiple_of(at, unit // 2)
        wdn[pl.ds(at, unit // 2), :] = ref[2 * small :, :]


def split_pairs(line):
    pieces = [
        jnp.concatenate(
            [line[:, h * PAIR + t * HEAD : h * PAIR + (t + 1) * HEAD] for h in range(LOCAL_HEADS)],
            axis=1,
        )
        for t in range(2)
    ]
    return jnp.concatenate(pieces, axis=1)


def join_pairs(left, right):
    mix = []
    for h in range(LOCAL_HEADS):
        mix += [left[:, h * HEAD : (h + 1) * HEAD], right[:, h * HEAD : (h + 1) * HEAD]]
    return jnp.concatenate(mix, axis=1)


def qkv_body(shards, sc, meta, mine, other_mine, own_x, other_x, *refs):
    own_w = [mine] + list(refs[: shards - 1])
    other_w = [other_mine] + list(refs[shards - 1 : 2 * shards - 2])
    wall, pq, pk, vv, vecs, upb, out_own, out_other, held = refs[2 * shards - 2 :]
    slots = own_x.shape[1]
    small = out_own.shape[1]
    width = wall.shape[1]
    rows = width // shards
    half = rows // 2
    unit = rows
    for which in range(CORES):
        group = sc[CORE] ^ which
        keep = (group == 0).astype(F32).astype(BF16)
        for shift in range(shards):
            ref = (other_w if which else own_w)[shift]
            if shift > 0:
                third = out_other if which else out_own
                end = ref.shape[0] - 2 * small
                third[shift - 1, :, 0:WIDE] = ref[end : end + small, :]
                third[shift - 1, :, WIDE:] = ref[end + small :, :]
            owner = lax.rem(sc[SHARD] + shards - shift, shards)
            at = pl.multiple_of(owner * rows, half)
            wall[group, pl.ds(at, rows), 0:WIDE] = ref[0:rows, :]
            if which == 0:
                held[owner] = ref[rows + half : ref.shape[0] - 2 * small, :].astype(F32)
            for part in range(2):
                mix = []
                for h in range(LOCAL_HEADS):
                    lo = part * COLS + h * HEAD
                    one = ref[rows : rows + half, lo : lo + HEAD]
                    mix += [one, one * keep]
                low = pl.multiple_of(owner * rows + part * half, half)
                wall[group, pl.ds(low, half), WIDE:] = jnp.concatenate(mix, axis=1)
    vecs[...] = jnp.zeros_like(vecs)
    for shard in range(shards):
        lo = shard * rows
        for row in range(6):
            line = 3 + row // 2
            col = (row % 2) * rows
            vecs[row : row + 1, lo : lo + rows] = held[shard, line : line + 1, col : col + rows]
        for chip_x in range(2):

            @pl.when(sc[SIDE] == chip_x)
            def _():
                for tall in range(2):
                    to = tall * width + shard * unit
                    upb[0:1, to : to + unit] = held[
                        shard, 6 + chip_x : 7 + chip_x, tall * unit : (tall + 1) * unit
                    ]

    table = held[sc[CHIP]]
    bias = [join_pairs(table[i : i + 1, 0:COLS], table[i : i + 1, COLS:]) for i in range(2)]
    key_bias = join_pairs(table[2:3, 0:COLS], table[2:3, 0:COLS])
    value_bias = join_pairs(table[2:3, COLS:], jnp.zeros((1, COLS), F32))
    flags = meta[...].T
    lane = lax.broadcasted_iota(jnp.int32, (1, WIDE), 1)
    left = (lane % PAIR) < HEAD
    for block in range(8):
        tokens = (own_x if block < 4 else other_x)[sc[CHIP] ^ (block % 4)]
        word = flags[:, block : block + 1] > 0
        at = slice(block * slots, (block + 1) * slots)
        if block < 4:
            first = dot(tokens, wall[0], 1, 0)
            second = dot(tokens, wall[1], 1, 0)
            query = jnp.where(word, first[:, 0:WIDE] + bias[0], second[:, 0:WIDE] + bias[1]) * SCALE
            pq[at, :] = query.astype(BF16)
            key, value = first[:, WIDE:], second[:, WIDE:]
        else:
            key = dot(tokens, wall[0, :, WIDE:], 1, 0)
            value = dot(tokens, wall[1, :, WIDE:], 1, 0)
        pk[at, :] = jnp.where(left == word, key + key_bias, 0.0).astype(BF16)
        vv[at, :] = (value + value_bias).astype(BF16)


def attend_body(step, pq, pk, vv, valid, probs, cx):
    head = pl.program_id(0)
    count = pq.shape[0]
    slots = count // 4
    keep = valid[...] > 0
    keys = pk[...]
    values = vv[...]
    for start in range(0, count, step):
        scores = dot(pq[start : start + step, :], keys, 1, 1)
        scores = jnp.where(keep, scores, NEG)
        top = jnp.max(scores, axis=-1, keepdims=True)
        expo = jnp.exp(scores - top)
        share = 1.0 / jnp.sum(expo, axis=-1, keepdims=True)
        low = (expo * share).astype(BF16)
        probs[0, start : start + step, :] = low
        mixed = dot(low, values, 1, 0)[:, 0:HEAD].astype(BF16)
        for h in range(LOCAL_HEADS):

            @pl.when(head == h)
            def _():
                for at in range(0, step, slots):
                    block = (start + at) // slots
                    mid = at + slots // 2
                    cx[block, :, h * HEAD : (h + 1) * HEAD] = mixed[at:mid]
                    cx[block, :, COLS + h * HEAD : COLS + (h + 1) * HEAD] = mixed[mid : at + slots]


def attend(pq, pk, vv, valid, slots):
    count, keys = pq.shape[0], pk.shape[0]
    step = 2 * slots if keys <= 2048 else slots
    limit = 14 if keys <= 2048 else 56
    return pl.pallas_call(
        partial(attend_body, step),
        grid=(LOCAL_HEADS,),
        in_specs=[
            pl.BlockSpec((count, PAIR), lambda h: (0, h)),
            pl.BlockSpec((keys, PAIR), lambda h: (0, h)),
            pl.BlockSpec((keys, PAIR), lambda h: (0, h)),
            pl.BlockSpec((1, keys), lambda h: (0, 0)),
        ],
        out_specs=[
            pl.BlockSpec((1, count, keys), lambda h: (h, 0, 0)),
            pl.BlockSpec((4, slots // 2, 2 * COLS), lambda h: (0, 0, 0)),
        ],
        out_shape=[
            sds((LOCAL_HEADS, count, keys), BF16),
            sds((4, slots // 2, 2 * COLS), BF16),
        ],
        name="attend",
        cost_estimate=cost(5.5),
        compiler_params=pltpu.CompilerParams(vmem_limit_bytes=limit << 20),
    )(pq, pk, vv, valid)


def attend_back_body(step, split, gc0, gc1, gc2, gc3, pq, pk, vv, probs, dq, *refs):
    head = pl.program_id(0)
    count = pq.shape[0]
    slots = count // 4
    half = slots // 2
    if split:
        dk_own, dv_own, dkv_other, gcs, dk, dv = refs
    else:
        dk, dv, gcs = refs

    @pl.when(head == 0)
    def _():
        gcs[...] = jnp.zeros_like(gcs)
        for block, ref in enumerate((gc0, gc1, gc2, gc3)):
            for h in range(LOCAL_HEADS):
                lo = block * slots
                gcs[h, lo : lo + half, 0:HEAD] = ref[:, h * HEAD : (h + 1) * HEAD]
                gcs[h, lo + half : lo + slots, 0:HEAD] = ref[
                    :, COLS + h * HEAD : COLS + (h + 1) * HEAD
                ]

    keys = pk[...]
    values = vv[...]
    for start in range(0, count, step):
        grad = gcs[head, start : start + step, :]
        low = probs[0, start : start + step, :]
        wide = low.astype(F32)
        moved = dot(grad, values, 1, 1)
        inner = jnp.sum(wide * moved, axis=-1, keepdims=True)
        ds = (wide * (moved - inner)).astype(BF16)
        query = pq[start : start + step, :]
        dq[start : start + step, :] = dot(ds, keys, 1, 0)
        key_part = dot(ds, query, 0, 0)
        value_part = dot(low, grad, 0, 0)
        if start == 0:
            dk[...] = key_part
            dv[...] = value_part
        else:
            dk[...] += key_part
            dv[...] += value_part
    if split:
        dk_own[...] = dk[0:count, :]
        dv_own[...] = dv[0:count, :]
        dkv_other[0] = dk[count:, :].astype(BF16)
        dkv_other[1] = dv[count:, :].astype(BF16)


def attend_back(pieces, pq, pk, vv, probs, slots, split):
    count, keys = pq.shape[0], pk.shape[0]
    step = 2 * slots if keys <= 2048 else slots
    limit = 20 if keys <= 2048 else 58
    piece = pl.BlockSpec((slots // 2, 2 * COLS), lambda h: (0, 0))
    rows = pl.BlockSpec((count, PAIR), lambda h: (0, h))
    cols = pl.BlockSpec((keys, PAIR), lambda h: (0, h))
    scratch = [pltpu.VMEM((LOCAL_HEADS, count, PAIR), BF16)]
    if split:
        specs = [rows, rows, rows, pl.BlockSpec((2, count, PAIR), lambda h: (0, 0, h))]
        shapes = [sds((count, WIDE), F32)] * 3 + [sds((2, count, WIDE), BF16)]
        scratch += [pltpu.VMEM((keys, PAIR), F32), pltpu.VMEM((keys, PAIR), F32)]
    else:
        specs = [rows, cols, cols]
        shapes = [sds((count, WIDE), F32), sds((keys, WIDE), F32), sds((keys, WIDE), F32)]
    return pl.pallas_call(
        partial(attend_back_body, step, split),
        grid=(LOCAL_HEADS,),
        in_specs=[piece] * 4
        + [rows, cols, cols, pl.BlockSpec((1, count, keys), lambda h: (h, 0, 0))],
        out_specs=specs,
        out_shape=shapes,
        scratch_shapes=scratch,
        name="attend_back",
        cost_estimate=cost(6),
        compiler_params=pltpu.CompilerParams(vmem_limit_bytes=limit << 20),
    )(*pieces, pq, pk, vv, probs)


def unpack(piece):
    return jnp.concatenate([piece[:, 0:COLS], piece[:, COLS:]], axis=0)


def normalize(summed):
    center = summed - jnp.mean(summed, axis=-1, keepdims=True)
    spread = jnp.mean(center * center, axis=-1, keepdims=True)
    rate = lax.rsqrt(spread + EPS)
    return center * rate, rate


def norm_back(grad, unit, rate, gain):
    scaled = grad * gain
    mean_one = jnp.mean(scaled, axis=-1, keepdims=True)
    mean_two = jnp.mean(scaled * unit, axis=-1, keepdims=True)
    return rate * (scaled - mean_one - unit * mean_two)


def total(values):
    return jnp.sum(values, axis=0, keepdims=True)


OUT_B, GAIN_1, SHIFT_1, DOWN_B, GAIN_2, SHIFT_2 = range(6)


def norm_one_body(sc, vecs, cx0, cx1, cx2, cx3, wo, hidden, low, unit_out, rate_out):
    acc = hidden[...].astype(F32) + vecs[OUT_B : OUT_B + 1, :]
    for rel, ref in enumerate((cx0, cx1, cx2, cx3)):
        at = pl.multiple_of((sc[CHIP] ^ rel) * COLS, COLS)
        acc += dot(unpack(ref[...]), wo[pl.ds(at, COLS), :], 1, 0)
    unit, rate = normalize(acc)
    first = unit * vecs[GAIN_1 : GAIN_1 + 1, :] + vecs[SHIFT_1 : SHIFT_1 + 1, :]
    low[...] = first.astype(BF16)
    unit_out[...] = unit
    rate_out[...] = jnp.broadcast_to(rate, rate_out.shape)


def mlp_body(chunk, sc, bias, x0, x1, wup, wdn, act, act_send, slope, own, send):
    slots = x0.shape[0]
    width = x0.shape[1]
    tokens = jnp.concatenate([x0[...], x1[...]], axis=0)
    acc = None
    for lo in range(0, wup.shape[1], chunk):
        pre = dot(tokens, wup[:, lo : lo + chunk], 1, 0) + bias[0:1, lo : lo + chunk]
        cdf = 0.5 * (1.0 + lax.erf(pre * 0.7071067811865476))
        pdf = jnp.exp(-0.5 * pre * pre) * 0.3989422804014327
        out = (pre * cdf).astype(BF16)
        slope[:, lo : lo + chunk] = cdf + pre * pdf
        to_quarter(sc, out, lo, width, act, act_send)
        part = dot(out, wdn[lo : lo + chunk, :], 1, 0)
        acc = part if acc is None else acc + part
    own[...] = acc[0:slots]
    send[...] = acc[slots:].astype(BF16)


def to_quarter(sc, values, lo, width, keep, send):
    tall, at = lo // width, lo % width

    @pl.when(sc[TALL] == tall)
    def _():
        keep[:, at : at + values.shape[1]] = values

    @pl.when(sc[TALL] != tall)
    def _():
        send[:, at : at + values.shape[1]] = values


def norm_two_body(sc, vecs, meta, own, received, unit_one, cotangent, output, gs, gs_low, sums):
    valid = meta[...].T[:, 8:9]
    first = unit_one[...] * vecs[GAIN_1 : GAIN_1 + 1, :] + vecs[SHIFT_1 : SHIFT_1 + 1, :]
    acc = own[...] + received[...].astype(F32) + vecs[DOWN_B : DOWN_B + 1, :] + first
    unit, rate = normalize(acc)
    gain = vecs[GAIN_2 : GAIN_2 + 1, :]
    output[...] = ((unit * gain + vecs[SHIFT_2 : SHIFT_2 + 1, :]) * valid).astype(BF16)
    grad = cotangent[...].astype(F32) * valid
    back = norm_back(grad, unit, rate, gain)
    gs[...] = back
    gs_low[...] = back.astype(BF16)
    sums[...] = jnp.zeros_like(sums)
    sums[DOWN_B : DOWN_B + 1, :] = total(back)
    sums[GAIN_2 : GAIN_2 + 1, :] = total(grad * unit)
    sums[SHIFT_2 : SHIFT_2 + 1, :] = total(grad)


def mlp_back_body(chunk, sc, g0, g1, slope, wup, wdn, low_keep, low_send, sums, own, send):
    slots = g0.shape[0]
    width = g0.shape[1]
    grads = jnp.concatenate([g0[...], g1[...]], axis=0)
    acc = None
    sums[...] = jnp.zeros_like(sums)
    for lo in range(0, wup.shape[1], chunk):
        pre = dot(grads, wdn[lo : lo + chunk, :], 1, 1) * slope[:, lo : lo + chunk]
        sums[0:1, lo : lo + chunk] = total(pre)
        low = pre.astype(BF16)
        to_quarter(sc, low, lo, width, low_keep, low_send)
        part = dot(low, wup[:, lo : lo + chunk], 1, 1)
        acc = part if acc is None else acc + part
    own[...] = acc[0:slots]
    send[...] = acc[slots:].astype(BF16)


def mlp_grads_body(
    shards, sc, x0, x1, x2, x3, g0, g1, g2, g3, act, act_r, low, low_r, keep, send
):
    tokens = jnp.concatenate([x0[...], x1[...], x2[...], x3[...]], axis=0)
    grads = jnp.concatenate([g0[...], g1[...], g2[...], g3[...]], axis=0)
    hidden = jnp.concatenate([act[...], act_r[...]], axis=0)
    back = jnp.concatenate([low[...], low_r[...]], axis=0)
    rows = tokens.shape[1] // shards
    for at in range(shards):
        lo = at * rows
        up = dot(tokens[:, lo : lo + rows], back, 0, 0)
        down = dot(hidden[:, lo : lo + rows], grads, 0, 0)

        @pl.when(sc[CORE] == 0)
        def _():
            keep[at] = up
            send[at] = down.astype(BF16)

        @pl.when(sc[CORE] == 1)
        def _():
            keep[at] = down
            send[at] = up.astype(BF16)


def fan_body(shards, sc, keep, received, own, *sends):
    at = sc[SHARD]
    own[...] = keep[at] + received[at].astype(F32)
    for shift in range(1, shards):
        at = lax.rem(sc[SHARD] + shift, shards)
        sends[shift - 1][...] = (keep[at] + received[at].astype(F32)).astype(BF16)


def out_fan_body(sc, keep, received, own, *sends):
    small = own.shape[1]
    for rel in range(4):
        at = pl.multiple_of((sc[CHIP] ^ rel) * small, small)
        value = keep[:, pl.ds(at, small), :] + received[:, pl.ds(at, small), :].astype(F32)
        if rel == 0:
            own[...] = value
        else:
            sends[rel - 1][...] = value.astype(BF16)


def qkv_fan_body(shards, sc, keep, received, own, *sends):
    main = received.shape[1]
    for shift in range(shards):
        at = lax.rem(sc[SHARD] + shift, shards)
        ref = own if shift == 0 else sends[shift - 1]
        ref[0:main, :] = (keep[at, 0:main, :] + received[at].astype(F32)).astype(ref.dtype)
        ref[main:, :] = keep[at, main:, :].astype(ref.dtype)


def out_shards_body(shards, sc, own_all, r1, r2, r3, own, *sends):
    for shift in range(shards):
        at = lax.rem(sc[SHARD] + shift, shards)
        value = own_all[at] + r1[at].astype(F32) + r2[at].astype(F32) + r3[at].astype(F32)
        ref = own if shift == 0 else sends[shift - 1]
        ref[...] = value.astype(ref.dtype)


def gather_sum_body(sc, own, *refs):
    acc = own[...]
    for ref in refs[:-1]:
        acc += ref[...].astype(F32)
    refs[-1][...] = acc.astype(refs[-1].dtype)


def two_sums_body(count, sc, *refs):
    out = refs[-1]
    at = 0
    for part in (refs[:count], refs[count:-1]):
        acc = part[0][...]
        for ref in part[1:]:
            acc += ref[...].astype(F32)
        out[at : at + acc.shape[0], :] = acc.astype(out.dtype)
        at += acc.shape[0]


def input_grad_body(sc, base, own, r1, r2, r3, out):
    out[...] = (
        base[...] + own[...] + r1[...].astype(F32) + r2[...].astype(F32) + r3[...].astype(F32)
    )


def norm_one_back_body(
    sc, vecs, own, received, gs, unit_one, rate_one, wo, gf, gf_low, gcx, sums
):
    grad = gs[...] + own[...] + received[...].astype(F32)
    unit = unit_one[...]
    rate = rate_one[:, 0:1]
    back = norm_back(grad, unit, rate, vecs[GAIN_1 : GAIN_1 + 1, :])
    gf[...] = back
    low = back.astype(BF16)
    gf_low[...] = low
    sums[...] = jnp.zeros_like(sums)
    sums[OUT_B : OUT_B + 1, :] = total(back)
    sums[GAIN_1 : GAIN_1 + 1, :] = total(grad * unit)
    sums[SHIFT_1 : SHIFT_1 + 1, :] = total(grad)
    half = back.shape[0] // 2
    for rel in range(4):
        at = pl.multiple_of((sc[CHIP] ^ rel) * COLS, COLS)
        part = dot(low, wo[pl.ds(at, COLS), :], 1, 1).astype(BF16)
        gcx[rel, :, 0:COLS] = part[0:half]
        gcx[rel, :, COLS:] = part[half:]


def out_grads_body(sc, cx0, cx1, cx2, cx3, gf_low, keep, send):
    low = gf_low[...]
    half = keep.shape[2]
    for rel, ref in enumerate((cx0, cx1, cx2, cx3)):
        block = dot(unpack(ref[...]), low, 0, 0)
        chip = sc[CHIP] ^ rel
        for core in range(CORES):

            @pl.when(sc[CORE] == core)
            def _():
                keep[chip] = block[:, core * half : (core + 1) * half]
                other = 1 - core
                send[chip] = block[:, other * half : (other + 1) * half].astype(BF16)


def qkv_grads_body(
    shards, sc, meta, dq, dk_own, dv_own, dkv_rec, wall, sums_one, sums_two, sums_up,
    x, own, send, keep_w, send_w, packed,
):
    slots = x.shape[1]
    flags = meta[...].T
    lane = lax.broadcasted_iota(jnp.int32, (1, WIDE), 1)
    left = (lane % PAIR) < HEAD
    width = wall.shape[1]
    rows = width // shards
    half = rows // 2
    acc = [0.0] * 4
    for block in range(4):
        at = slice(block * slots, (block + 1) * slots)
        word = flags[:, block : block + 1] > 0
        query = dq[at, :] * SCALE
        parts = (
            jnp.where(word, query, 0.0),
            jnp.where(word, 0.0, query),
            jnp.where(left == word, dk_own[at, :] + dkv_rec[0, at, :].astype(F32), 0.0),
            dv_own[at, :] + dkv_rec[1, at, :].astype(F32),
        )
        acc = [a + total(p) for a, p in zip(acc, parts)]
        packed[0, at, 0:WIDE] = parts[0].astype(BF16)
        packed[1, at, 0:WIDE] = parts[1].astype(BF16)
        packed[0, at, WIDE:] = parts[2].astype(BF16)
        packed[1, at, WIDE:] = parts[3].astype(BF16)
    tokens = jnp.concatenate([x[sc[CHIP] ^ rel] for rel in range(4)], axis=0)
    for group_rel, ref in enumerate((keep_w, send_w)):
        group = sc[CORE] ^ group_rel
        for at in range(shards):
            grad = dot(tokens[:, at * rows : (at + 1) * rows], packed[group], 0, 0)
            ref[at, 0:rows, :] = grad[:, 0:WIDE].astype(ref.dtype)
            folded = jnp.concatenate(
                [
                    grad[:, WIDE + h * PAIR : WIDE + h * PAIR + HEAD]
                    + grad[:, WIDE + h * PAIR + HEAD : WIDE + (h + 1) * PAIR]
                    for h in range(LOCAL_HEADS)
                ],
                axis=1,
            ).astype(ref.dtype)
            ref[at, rows : rows + half, 0:COLS] = folded[0:half]
            ref[at, rows : rows + half, COLS:] = folded[half:]
    for block in range(4):
        at = slice(block * slots, (block + 1) * slots)
        back = dot(packed[0, at, :], wall[0], 1, 1) + dot(packed[1, at, :], wall[1], 1, 1)
        if block == 0:
            own[...] = back
        else:
            send[block - 1] = back.astype(BF16)
    keys = split_pairs(acc[2])
    values = split_pairs(acc[3])
    heads = [
        split_pairs(acc[0]),
        split_pairs(acc[1]),
        jnp.concatenate([keys[:, 0:COLS] + keys[:, COLS:], values[:, 0:COLS]], axis=1),
    ]
    norms = sums_one[...] + sums_two[...]
    for at in range(shards):
        mine = (sc[CHIP] == at).astype(F32)
        lo = at * rows
        lines = [line * mine for line in heads]
        for row in range(0, 6, 2):
            lines.append(
                jnp.concatenate(
                    [norms[row : row + 1, lo : lo + rows], norms[row + 1 : row + 2, lo : lo + rows]],
                    axis=1,
                )
            )
        units = jnp.concatenate(
            [sums_up[0:1, t * width + lo : t * width + lo + rows] for t in range(2)], axis=1
        )
        side = sc[SIDE].astype(F32)
        lines += [units * (1.0 - side), units * side]
        keep_w[at, rows + half :, :] = jnp.concatenate(lines, axis=0)


def place_qkv_body(sc, p0, p1, p2, p3, others, qg, kg, vg, og, qb, *refs):
    vectors, (ub, held) = refs[:8], refs[8:]
    rows = kg.shape[0]
    half = rows // 2
    small = rows // 4
    lines = 0.0
    for core_rel in range(CORES):
        for rel in range(4):
            value = (p0, p1, p2, p3)[rel][...] if core_rel == 0 else others[rel]
            lines += value[rows + half : rows + half + 8, :].astype(F32)
            held[sc[CORE] ^ core_rel, sc[CHIP] ^ rel] = value
    for core in range(CORES):
        for chip in range(CHIPS):
            piece = held[core, chip].astype(F32)
            lo = chip * COLS
            for which in range(2):
                qg[2 * core + which, :, lo : lo + COLS] = jnp.concatenate(
                    [
                        piece[0:rows, h * PAIR + which * HEAD : h * PAIR + (which + 1) * HEAD]
                        for h in range(LOCAL_HEADS)
                    ],
                    axis=1,
                )
            ref = kg if core == 0 else vg
            ref[0:half, lo : lo + COLS] = piece[rows : rows + half, 0:COLS]
            ref[half:, lo : lo + COLS] = piece[rows : rows + half, COLS:]
            og[chip * small : (chip + 1) * small, core * 2 * COLS : (core + 1) * 2 * COLS] = piece[
                rows + half + 8 :, :
            ]
    for which in range(4):
        qb[which : which + 1, :] = lines[
            which // 2 : which // 2 + 1, (which % 2) * COLS : (which % 2 + 1) * COLS
        ]
    for index, ref in enumerate(vectors):
        ref[...] = lines[2 + index // 2, (index % 2) * rows : (index % 2 + 1) * rows]
    ub[...] = jnp.concatenate([lines[6], lines[7]], axis=0)


def place_mlp_body(sc, p0, p1, p2, p3, others, ug, dg, held):
    rows, ff = ug.shape
    part = ff // 4
    side = part // 2
    unit = side // 2
    for core_rel in range(CORES):
        for rel in range(4):
            value = (p0, p1, p2, p3)[rel][...] if core_rel == 0 else others[rel]
            held[sc[CORE] ^ core_rel, sc[CHIP] ^ rel] = value
    for chip in range(CHIPS):
        lo = (chip & 1) * side + (chip >> 1) * unit
        piece = held[0, chip].astype(F32)
        for shard in range(4):
            at = shard * part + lo
            ug[:, at : at + unit] = piece[:, shard * unit : (shard + 1) * unit]
        dg[lo : lo + unit, :] = held[1, chip].astype(F32)


def local(
    shards,
    lanes,
    hidden,
    lengths,
    row_types,
    query_weight,
    query_bias,
    key_weight,
    key_bias,
    value_weight,
    value_bias,
    out_weight,
    out_bias,
    norm1_gain,
    norm1_bias,
    up_weight,
    up_bias,
    down_weight,
    down_bias,
    norm2_gain,
    norm2_bias,
    cotangent,
):
    groups = lanes // (CHIPS * CORES)
    shard = lax.axis_index("shard")
    lane = lax.axis_index("ctx")
    core, chip, group = lane & 1, (lane >> 1) & 3, lane >> 3
    chip_x, chip_y = chip & 1, chip >> 1
    spot = chip_y * 2 + core
    scalars = jnp.stack([shard, chip, core, spot, chip_x, chip_y]).astype(jnp.int32)
    sets = [[g * 8 + i for g in range(groups)] for i in range(8)]

    def across(value, mask, name):
        with jax.named_scope(f"{name}_{mask}"):
            return lax.ppermute(value, "ctx", [(i, i ^ mask) for i in range(lanes)])

    def chips(value, rel, name):
        return across(value, rel << 1, name)

    def turn(value, shift, name):
        with jax.named_scope(f"{name}_z{shift}"):
            return lax.ppermute(value, "shard", [(i, (i + shift) % shards) for i in range(shards)])

    def after(value, *others):
        return lax.optimization_barrier((value,) + others)[0]

    width = hidden.shape[2]
    slots = hidden.shape[1]
    rows = width // shards
    ff = up_weight.shape[1]
    part = ff // shards
    side = part // 2
    hid = hidden[0]
    cot = cotangent[0]
    small_rows = 8
    main = rows + rows // 2

    mine, other_mine = run(
        prep_qkv_body,
        "prep_qkv",
        [sds((main + small_rows + rows // 2, WIDE), BF16), sds((main, WIDE), BF16)],
        scalars,
        query_weight, key_weight, value_weight, out_weight, query_bias,
        key_bias, value_bias, out_bias, norm1_gain, norm1_bias,
        down_bias, norm2_gain, norm2_bias, up_bias,
        vmem=60,
    )
    own_w = [turn(mine, d, "qkvw") for d in range(1, shards)]
    quarter = rows // 4
    mlp_one = run(
        prep_mlp_body,
        "prep_mlp",
        sds((2 * quarter + side // 4, width), BF16),
        scalars,
        lax.dynamic_slice_in_dim(up_weight, spot * quarter, quarter, 0),
        lax.dynamic_slice_in_dim(down_weight, chip_x * side + spot * (side // 4), side // 4, 0),
    )
    mlp_z = [turn(after(mlp_one, mine), d, "mlpw") for d in range(1, shards)]
    planes = [[g * 8 + 2 * j + c for j in range(CHIPS)] for g in range(groups) for c in range(CORES)]
    own_x = lax.all_gather(after(hid, mlp_one), "ctx", axis_index_groups=planes)
    other_x = across(own_x, 1, "hid")
    other_w = [across(piece, 1, "qkvw") for piece in own_w]

    kinds = row_types.reshape(-1, slots)
    blocks = [group * 8 + (chip ^ rel) * 2 + (core ^ c) for c in range(CORES) for rel in range(4)]
    places = jnp.arange(slots, dtype=jnp.int32)
    word = jnp.concatenate([lax.dynamic_slice_in_dim(kinds, b, 1, 0) for b in blocks], axis=0)
    starts = jnp.stack(blocks)[:, None] * slots
    live = (starts + places[None, :] < lengths[0]).astype(F32)
    meta = jnp.concatenate([(word == 0).astype(F32), live], axis=0)

    wall, pq, pk, vv, vecs, up_shift, out_own, out_other = run(
        partial(qkv_body, shards),
        "qkv",
        [
            sds((2, width, 2 * WIDE), BF16),
            sds((4 * slots, WIDE), BF16),
            sds((8 * slots, WIDE), BF16),
            sds((8 * slots, WIDE), BF16),
            sds((8, width), F32),
            sds((1, ff // 2), F32),
            sds((shards - 1, quarter, width), BF16),
            sds((shards - 1, quarter, width), BF16),
        ],
        scalars,
        meta, mine, other_mine, own_x, other_x, *own_w, *other_w,
        scratch=[pltpu.VMEM((shards, small_rows, WIDE), F32)],
    )
    out_far = across(out_own, 4, "outw")
    valid = live.reshape(1, 8 * slots)
    if groups > 1:
        gather = partial(lax.all_gather, axis_name="ctx", axis_index_groups=sets, tiled=True)
        pk, vv = gather(pk, axis=0), gather(vv, axis=0)
        valid = gather(valid, axis=1)
    probs, cx = attend(pq, pk, vv, valid, slots)
    cxs = [cx[0]] + [chips(cx[rel], rel, "cx") for rel in range(1, 4)]
    *cxs, out_far = lax.optimization_barrier((*cxs, out_far))
    wo = run(
        partial(assemble_out_body, shards),
        "assemble_out",
        sds((width, width), BF16),
        scalars,
        out_weight, out_own, out_other, out_far, across(out_far, 1, "outw"),
    )
    mlp_z = after(mlp_z, cx)
    mlp_far = [across(piece, 4, "mlpw") for piece in mlp_z]
    pieces = mlp_z + mlp_far
    wup, wdn = run(
        partial(assemble_mlp_body, shards),
        "assemble_mlp",
        [sds((width, ff // 2), BF16), sds((ff // 2, width), BF16)],
        scalars,
        up_weight, down_weight, *pieces, *[across(piece, 1, "mlpw") for piece in pieces],
    )

    low_one, unit_one, rate_one = run(
        norm_one_body,
        "norm_one",
        [sds((slots, width), BF16), sds((slots, width), F32), sds((slots, 128), F32)],
        scalars,
        vecs, *cxs, wo, hid,
    )
    low_two = chips(low_one, 1, "mlpx")
    low_two, far_one = lax.optimization_barrier((low_two, across(low_one, 4, "mlpy_x1")))
    far_two = across(low_two, 4, "mlpy_x2")
    act, act_send, slope, own, send = run(
        partial(mlp_body, 384),
        "mlp",
        [
            sds((2 * slots, ff // 4), BF16),
            sds((2 * slots, ff // 4), BF16),
            sds((2 * slots, ff // 2), F32),
            sds((slots, width), F32),
            sds((slots, width), BF16),
        ],
        scalars,
        up_shift, low_one, low_two, wup, wdn,
    )
    received, far_two = lax.optimization_barrier((chips(send, 1, "mlpp"), far_two))
    act_far = across(act_send, 4, "mlpy_a")
    output, gs, gs_low, sums_two = run(
        norm_two_body,
        "norm_two",
        [
            sds((slots, width), BF16),
            sds((slots, width), F32),
            sds((slots, width), BF16),
            sds((8, width), F32),
        ],
        scalars,
        vecs, meta, own, received, unit_one, cot,
    )
    gs_other, gs_far_one, act_far = lax.optimization_barrier(
        (chips(gs_low, 1, "mlpg"), across(gs_low, 4, "mlpy_g1"), act_far)
    )
    gs_far_two = across(gs_other, 4, "mlpy_g2")
    low_keep, low_send, sums_up, own, send = run(
        partial(mlp_back_body, 384),
        "mlp_back",
        [
            sds((2 * slots, ff // 4), BF16),
            sds((2 * slots, ff // 4), BF16),
            sds((8, ff // 2), F32),
            sds((slots, width), F32),
            sds((slots, width), BF16),
        ],
        scalars,
        gs_low, gs_other, slope, wup, wdn,
    )
    received, gs_far_two = lax.optimization_barrier((chips(send, 1, "mlpb"), gs_far_two))
    low_far = across(low_send, 4, "mlpy_l")
    gf, gf_low, gcx, sums_one = run(
        norm_one_back_body,
        "norm_one_back",
        [
            sds((slots, width), F32),
            sds((slots, width), BF16),
            sds((4, slots // 2, 2 * COLS), BF16),
            sds((8, width), F32),
        ],
        scalars,
        vecs, own, received, gs, unit_one, rate_one, wo,
    )
    gcs = [gcx[0]] + [chips(gcx[rel], rel, "gcx") for rel in range(1, 4)]
    keep_mlp, send_mlp = run(
        partial(mlp_grads_body, shards),
        "mlp_grads",
        [sds((shards, rows, width), F32), sds((shards, rows, width), BF16)],
        scalars,
        low_one, low_two, far_one, far_two, gs_low, gs_other, gs_far_one, gs_far_two,
        act, act_far, low_keep, low_far,
    )
    *gcs, keep_mlp, send_mlp = lax.optimization_barrier((*gcs, keep_mlp, send_mlp))
    keep_out, send_out = run(
        out_grads_body,
        "out_grads",
        [sds((CHIPS, COLS, width // 2), F32), sds((CHIPS, COLS, width // 2), BF16)],
        scalars,
        *cxs,
        gf_low,
    )

    kind = BF16 if groups == 1 else F32

    def spread(low, name, late=()):
        if groups > 1:
            low = lax.psum(low, "ctx", axis_index_groups=sets).astype(BF16)
        here = [low] + [chips(low, rel, name) for rel in range(1, 4)]
        return here + [across(after(jnp.stack(here), *late), 1, name)]

    if groups == 1:
        dq, dk_own, dv_own, dkv = attend_back(gcs, pq, pk, vv, probs, slots, True)
    else:
        count = 4 * slots
        scatter = partial(lax.psum_scatter, axis_name="ctx", axis_index_groups=sets, tiled=True)
        dq, dk, dv = attend_back(gcs, pq, pk, vv, probs, slots, False)
        dk, dv = scatter(dk), scatter(dv)
        dk_own, dv_own = dk[:count], dv[:count]
        dkv = jnp.stack([dk[count:], dv[count:]]).astype(BF16)
    mlp_parts = run(
        partial(fan_body, shards),
        "fan_mlp",
        [sds((rows, width), F32)] + [sds((rows, width), BF16)] * (shards - 1),
        scalars,
        keep_mlp,
        across(send_mlp, 1, "gm"),
    )
    dkv, *mlp_parts = lax.optimization_barrier((dkv, *mlp_parts))
    mlp_recs = [turn(value, d + 1, "gm") for d, value in enumerate(mlp_parts[1:])]
    dkv_rec, keep_out, send_out = lax.optimization_barrier(
        (across(dkv, 1, "dkv"), keep_out, send_out)
    )
    own, send, keep_w, send_w = run(
        partial(qkv_grads_body, shards),
        "qkv_grads",
        [
            sds((slots, width), F32),
            sds((3, slots, width), BF16),
            sds((shards, main + small_rows, WIDE), F32),
            sds((shards, main, WIDE), BF16),
        ],
        scalars,
        meta, dq, dk_own, dv_own, dkv_rec, wall, sums_one, sums_two, sums_up, own_x,
        scratch=[pltpu.VMEM((2, 4 * slots, 2 * WIDE), BF16)],
    )
    qkv_parts = run(
        partial(qkv_fan_body, shards),
        "fan_qkv",
        [sds((main + small_rows, WIDE), F32)]
        + [sds((main + small_rows, WIDE), BF16)] * (shards - 1),
        scalars,
        keep_w,
        across(send_w, 1, "gq"),
    )
    qkv_recs = [turn(value, d + 1, "gq") for d, value in enumerate(qkv_parts[1:])]

    out_parts = run(
        out_fan_body,
        "fan_out",
        [sds((CHIPS, quarter, width // 2), F32)] + [sds((CHIPS, quarter, width // 2), BF16)] * 3,
        scalars,
        keep_out,
        across(send_out, 1, "go"),
    )
    out_recs = [chips(after(out_parts[rel], qkv_parts), rel, "go") for rel in range(1, 4)]
    out_shards = run(
        partial(out_shards_body, shards),
        "shards_out",
        [sds((quarter, width // 2), F32)] + [sds((quarter, width // 2), BF16)] * (shards - 1),
        scalars,
        out_parts[0],
        *out_recs,
    )
    out_recs = [turn(value, d + 1, "go") for d, value in enumerate(out_shards[1:])]

    mlp_recs = after(mlp_recs, qkv_parts)
    low = run(
        gather_sum_body, "sum_mlp", sds((rows, width), kind), scalars, mlp_parts[0], *mlp_recs
    )
    done_mlp = spread(low, "gm")
    input_grad = run(
        input_grad_body,
        "input_grad",
        sds((slots, width), F32),
        scalars,
        gf,
        own,
        *[chips(send[rel - 1], rel, "ig") for rel in range(1, 4)],
    )
    ug, dg = run(
        place_mlp_body,
        "place_mlp",
        [sds((rows, ff), F32), sds((part, width), F32)],
        scalars,
        *done_mlp,
        scratch=[pltpu.VMEM((CORES, CHIPS, rows, width), BF16)],
    )
    size = main + small_rows + quarter
    qkv_recs, out_recs = after((qkv_recs, out_recs), input_grad)
    low = run(
        partial(two_sums_body, shards),
        "sum_qkv",
        sds((size, WIDE), kind),
        scalars,
        qkv_parts[0], *qkv_recs, out_shards[0], *out_recs,
    )
    done_qkv = spread(low, "gq", (ug, dg))

    vec = sds((rows,), F32)
    qg, kg, vg, og, qbg, kbg, vbg, obg, g1g, b1g, dbg, g2g, b2g, ubg = run(
        place_qkv_body,
        "place_qkv",
        [
            sds((4, rows, width), F32), sds((rows, width), F32), sds((rows, width), F32),
            sds((rows, width), F32), sds((4, rows), F32), vec, vec, vec, vec, vec, vec, vec, vec,
            sds((4 * rows,), F32),
        ],
        scalars,
        *done_qkv,
        scratch=[pltpu.VMEM((CORES, CHIPS, size, WIDE), BF16)],
    )
    return (
        output[None], input_grad[None], qg, qbg, kg, kbg, vg, vbg, og, obg,
        g1g, b1g, ug, ubg, dg, dbg, g2g, b2g,
    )


def solution(mesh):
    vec, mat = P("shard"), P("shard", None)
    tokens = P("shard", "ctx", None)
    placed = (
        tokens, vec, mat, P(None, "shard", None), P(None, "shard"), mat, vec, mat, vec, mat,
        vec, vec, vec, mat, vec, mat, vec, vec, vec, tokens,
    )
    result = (
        tokens, tokens, P(None, "shard", None), P(None, "shard"), mat, vec, mat, vec, mat, vec,
        vec, vec, mat, vec, mat, vec, vec, vec,
    )
    return jax.shard_map(
        partial(local, mesh.shape["shard"], mesh.shape["ctx"]),
        mesh=mesh,
        in_specs=placed,
        out_specs=result,
        check_vma=False,
    )
```

```python
from functools import partial

import jax
import jax.numpy as jnp
from jax import lax
from jax.experimental import pallas as pl
from jax.experimental.pallas import tpu as pltpu
from jax.sharding import PartitionSpec as P

HEADS = 12
HEAD = 64
CHIPS = 4
CORES = 2
LOCAL_HEADS = HEADS // CHIPS
COLS = LOCAL_HEADS * HEAD
PAIR = 2 * HEAD
WIDE = LOCAL_HEADS * PAIR

EPS = 1e-12
SCALE = 0.125
NEG = -1000000000.0
F32 = jnp.float32
BF16 = jnp.bfloat16

SMEM = pl.BlockSpec(memory_space=pltpu.SMEM)
VMEM = pl.BlockSpec(memory_space=pltpu.VMEM)


def sds(shape, dtype):
    return jax.ShapeDtypeStruct(shape, dtype)


def dot(left, right, over_left, over_right):
    return lax.dot_general(
        left, right, (((over_left,), (over_right,)), ((), ())), preferred_element_type=F32
    )


def cost(micros):
    return pl.CostEstimate(flops=1, bytes_accessed=int(micros * 3e6), transcendentals=0)


MICROS = {
    "mlp": 3.5, "mlp_back": 3.5, "mlp_grads": 3.3, "out_grads": 2, "qkv_grads": 5,
    "place_qkv": 3.5, "place_mlp": 3,
}


def run(body, name, outs, scalars, *arrays, scratch=(), flops=0, vmem=24):
    many = isinstance(outs, (list, tuple))
    return pl.pallas_call(
        body,
        out_shape=outs,
        in_specs=[SMEM] + [VMEM] * len(arrays),
        out_specs=[VMEM] * len(outs) if many else VMEM,
        scratch_shapes=list(scratch),
        name=name,
        cost_estimate=cost(MICROS.get(name, 1)),
        compiler_params=pltpu.CompilerParams(vmem_limit_bytes=vmem << 20),
    )(scalars, *arrays)


SHARD, CHIP, CORE, SPOT, SIDE, TALL, PLACE = range(7)


def prep_qkv_body(sc, qw, kw, vw, ow, qb, *refs):
    vectors, (ub, own, other) = refs[:8], refs[8:]
    rows = kw.shape[0]
    half = rows // 2
    wide = [ref[...].astype(F32).reshape(1, rows) for ref in vectors]
    queries = qb[...].astype(F32)
    long = ub[...].astype(F32).reshape(1, 4 * rows)
    lines = [jnp.concatenate([queries[i : i + 1], queries[i + 1 : i + 2]], axis=1) for i in (0, 2)]
    lines += [jnp.concatenate(wide[i : i + 2], axis=1) for i in range(0, 8, 2)]
    lines += [long[:, 0 : 2 * rows], long[:, 2 * rows :]]
    small = jnp.concatenate(lines, axis=0).astype(BF16)
    end = rows + half + small.shape[0]
    own[rows + half : end, :] = small
    third = ow[pl.ds(pl.multiple_of(sc[PLACE] * (rows // 4), rows // 4), rows // 4), :]
    own[end : end + rows // 4, :] = third[:, 0:WIDE]
    own[end + rows // 4 :, :] = third[:, WIDE:]
    for chip in range(CHIPS):
        for core in range(CORES):

            @pl.when((sc[CHIP] == chip) & (sc[CORE] == core))
            def _():
                lo = chip * COLS
                for out, group in ((own, core), (other, 1 - core)):
                    first = qw[2 * group, :, lo : lo + COLS]
                    second = qw[2 * group + 1, :, lo : lo + COLS]
                    mix = []
                    for h in range(LOCAL_HEADS):
                        mix += [
                            first[:, h * HEAD : (h + 1) * HEAD],
                            second[:, h * HEAD : (h + 1) * HEAD],
                        ]
                    out[0:rows, :] = jnp.concatenate(mix, axis=1)
                    src = vw if group else kw
                    out[rows : rows + half, 0:COLS] = src[0:half, lo : lo + COLS]
                    out[rows : rows + half, COLS:] = src[half:rows, lo : lo + COLS]


def prep_mlp_body(sc, up, down, out):
    rows, ff = up.shape
    part = ff // 4
    side = part // 2
    unit = side // 2
    for chip_x in range(2):

        @pl.when(sc[SIDE] == chip_x)
        def _():
            for tall in range(2):
                for piece in range(4):
                    lo = piece * part + chip_x * side + tall * unit
                    out[tall * rows : (tall + 1) * rows, piece * unit : (piece + 1) * unit] = up[
                        :, lo : lo + unit
                    ]

    out[2 * rows :, :] = down[...]


def assemble_out_body(shards, sc, whole, own, other, own_far, other_far, wo):
    rows = wo.shape[0] // shards
    small = rows // 4
    wo[pl.ds(pl.multiple_of(sc[SHARD] * rows, rows), rows), :] = whole[...]
    for rel, ref in enumerate((own, other, own_far, other_far)):
        for shift in range(1, shards):
            owner = sc[SHARD] ^ shift
            at = pl.multiple_of(owner * rows + (sc[PLACE] ^ rel) * small, small)
            wo[pl.ds(at, small), :] = ref[shift - 1]


def assemble_mlp_body(shards, sc, up, down, *refs):
    pieces, (wup, wdn) = refs[:-2], refs[-2:]
    rows = wup.shape[0] // shards
    part = wdn.shape[0] // shards
    width = wdn.shape[1]
    unit = part // 2
    small = rows // 4
    at = pl.multiple_of(sc[SHARD] * rows, rows)
    for chip_x in range(2):

        @pl.when(sc[SIDE] == chip_x)
        def _():
            for tall in range(2):
                for piece in range(4):
                    lo = piece * 2 * part + chip_x * part + tall * unit
                    to = tall * width + piece * unit
                    wup[pl.ds(at, rows), to : to + unit] = up[:, lo : lo + unit]

    for tall in range(2):
        at = pl.multiple_of(tall * width + sc[SHARD] * unit, unit)
        lo = pl.multiple_of(sc[SIDE] * part + tall * unit, unit)
        wdn[pl.ds(at, unit), :] = down[pl.ds(lo, unit), :]
    for index, ref in enumerate(pieces):
        rel, shift = index // (shards - 1), index % (shards - 1) + 1
        spot = sc[SPOT] ^ (rel // 2 + rel % 2 * 2)
        owner = sc[SHARD] ^ shift
        at = pl.multiple_of(owner * rows + spot * small, small)
        wup[pl.ds(at, small), 0:width] = ref[0:small, :]
        wup[pl.ds(at, small), width:] = ref[small : 2 * small, :]
        at = (spot // 2) * width + owner * unit + (spot % 2) * (unit // 2)
        at = pl.multiple_of(at, unit // 2)
        wdn[pl.ds(at, unit // 2), :] = ref[2 * small :, :]


def split_pairs(line):
    pieces = [
        jnp.concatenate(
            [line[:, h * PAIR + t * HEAD : h * PAIR + (t + 1) * HEAD] for h in range(LOCAL_HEADS)],
            axis=1,
        )
        for t in range(2)
    ]
    return jnp.concatenate(pieces, axis=1)


def join_pairs(left, right):
    mix = []
    for h in range(LOCAL_HEADS):
        mix += [left[:, h * HEAD : (h + 1) * HEAD], right[:, h * HEAD : (h + 1) * HEAD]]
    return jnp.concatenate(mix, axis=1)


def qkv_body(shards, sc, meta, mine, other_mine, own_x, other_x, *refs):
    own_w = [mine] + list(refs[: shards - 1])
    other_w = [other_mine] + list(refs[shards - 1 : 2 * shards - 2])
    wall, pq, pk, vv, vecs, upb, out_own, out_other, held = refs[2 * shards - 2 :]
    slots = own_x.shape[1]
    small = out_own.shape[1]
    width = wall.shape[1]
    rows = width // shards
    half = rows // 2
    unit = rows
    for which in range(CORES):
        group = sc[CORE] ^ which
        keep = (group == 0).astype(F32).astype(BF16)
        for shift in range(shards):
            ref = (other_w if which else own_w)[shift]
            if shift > 0:
                third = out_other if which else out_own
                end = ref.shape[0] - 2 * small
                third[shift - 1, :, 0:WIDE] = ref[end : end + small, :]
                third[shift - 1, :, WIDE:] = ref[end + small :, :]
            owner = sc[SHARD] ^ shift
            at = pl.multiple_of(owner * rows, half)
            wall[group, pl.ds(at, rows), 0:WIDE] = ref[0:rows, :]
            if which == 0:
                held[owner] = ref[rows + half : ref.shape[0] - 2 * small, :].astype(F32)
            for part in range(2):
                mix = []
                for h in range(LOCAL_HEADS):
                    lo = part * COLS + h * HEAD
                    one = ref[rows : rows + half, lo : lo + HEAD]
                    mix += [one, one * keep]
                low = pl.multiple_of(owner * rows + part * half, half)
                wall[group, pl.ds(low, half), WIDE:] = jnp.concatenate(mix, axis=1)
    vecs[...] = jnp.zeros_like(vecs)
    for shard in range(shards):
        lo = shard * rows
        for row in range(6):
            line = 3 + row // 2
            col = (row % 2) * rows
            vecs[row : row + 1, lo : lo + rows] = held[shard, line : line + 1, col : col + rows]
        for chip_x in range(2):

            @pl.when(sc[SIDE] == chip_x)
            def _():
                for tall in range(2):
                    to = tall * width + shard * unit
                    upb[0:1, to : to + unit] = held[
                        shard, 6 + chip_x : 7 + chip_x, tall * unit : (tall + 1) * unit
                    ]

    table = held[sc[CHIP]]
    bias = [join_pairs(table[i : i + 1, 0:COLS], table[i : i + 1, COLS:]) for i in range(2)]
    key_bias = join_pairs(table[2:3, 0:COLS], table[2:3, 0:COLS])
    value_bias = join_pairs(table[2:3, COLS:], jnp.zeros((1, COLS), F32))
    flags = meta[...].T
    lane = lax.broadcasted_iota(jnp.int32, (1, WIDE), 1)
    left = (lane % PAIR) < HEAD
    for block in range(8):
        tokens = (own_x if block < 4 else other_x)[block % 4]
        word = flags[:, block : block + 1] > 0
        at = slice(block * slots, (block + 1) * slots)
        if block < 4:
            first = dot(tokens, wall[0], 1, 0)
            second = dot(tokens, wall[1], 1, 0)
            query = jnp.where(word, first[:, 0:WIDE] + bias[0], second[:, 0:WIDE] + bias[1]) * SCALE
            pq[at, :] = query.astype(BF16)
            key, value = first[:, WIDE:], second[:, WIDE:]
        else:
            key = dot(tokens, wall[0, :, WIDE:], 1, 0)
            value = dot(tokens, wall[1, :, WIDE:], 1, 0)
        pk[at, :] = jnp.where(left == word, key + key_bias, 0.0).astype(BF16)
        vv[at, :] = (value + value_bias).astype(BF16)


def attend_body(step, pq, pk, vv, valid, probs, cx):
    head = pl.program_id(0)
    count = pq.shape[0]
    slots = count // 4
    keep = valid[...] > 0
    keys = pk[...]
    values = vv[...]
    for start in range(0, count, step):
        scores = dot(pq[start : start + step, :], keys, 1, 1)
        scores = jnp.where(keep, scores, NEG)
        top = jnp.max(scores, axis=-1, keepdims=True)
        expo = jnp.exp(scores - top)
        share = 1.0 / jnp.sum(expo, axis=-1, keepdims=True)
        low = (expo * share).astype(BF16)
        probs[0, start : start + step, :] = low
        mixed = dot(low, values, 1, 0)[:, 0:HEAD].astype(BF16)
        for h in range(LOCAL_HEADS):

            @pl.when(head == h)
            def _():
                for at in range(0, step, slots):
                    block = (start + at) // slots
                    mid = at + slots // 2
                    cx[block, :, h * HEAD : (h + 1) * HEAD] = mixed[at:mid]
                    cx[block, :, COLS + h * HEAD : COLS + (h + 1) * HEAD] = mixed[mid : at + slots]


def attend(pq, pk, vv, valid, slots):
    count, keys = pq.shape[0], pk.shape[0]
    step = 2 * slots if keys <= 2048 else slots
    limit = 14 if keys <= 2048 else 56
    return pl.pallas_call(
        partial(attend_body, step),
        grid=(LOCAL_HEADS,),
        in_specs=[
            pl.BlockSpec((count, PAIR), lambda h: (0, h)),
            pl.BlockSpec((keys, PAIR), lambda h: (0, h)),
            pl.BlockSpec((keys, PAIR), lambda h: (0, h)),
            pl.BlockSpec((1, keys), lambda h: (0, 0)),
        ],
        out_specs=[
            pl.BlockSpec((1, count, keys), lambda h: (h, 0, 0)),
            pl.BlockSpec((4, slots // 2, 2 * COLS), lambda h: (0, 0, 0)),
        ],
        out_shape=[
            sds((LOCAL_HEADS, count, keys), BF16),
            sds((4, slots // 2, 2 * COLS), BF16),
        ],
        name="attend",
        cost_estimate=cost(5.5),
        compiler_params=pltpu.CompilerParams(vmem_limit_bytes=limit << 20),
    )(pq, pk, vv, valid)


def attend_back_body(step, split, gc0, gc1, gc2, gc3, pq, pk, vv, probs, dq, *refs):
    head = pl.program_id(0)
    count = pq.shape[0]
    slots = count // 4
    half = slots // 2
    if split:
        dk_own, dv_own, dkv_other, gcs, dk, dv = refs
    else:
        dk, dv, gcs = refs

    @pl.when(head == 0)
    def _():
        gcs[...] = jnp.zeros_like(gcs)
        for block, ref in enumerate((gc0, gc1, gc2, gc3)):
            for h in range(LOCAL_HEADS):
                lo = block * slots
                gcs[h, lo : lo + half, 0:HEAD] = ref[:, h * HEAD : (h + 1) * HEAD]
                gcs[h, lo + half : lo + slots, 0:HEAD] = ref[
                    :, COLS + h * HEAD : COLS + (h + 1) * HEAD
                ]

    keys = pk[...]
    values = vv[...]
    for start in range(0, count, step):
        grad = gcs[head, start : start + step, :]
        low = probs[0, start : start + step, :]
        wide = low.astype(F32)
        moved = dot(grad, values, 1, 1)
        inner = jnp.sum(wide * moved, axis=-1, keepdims=True)
        ds = (wide * (moved - inner)).astype(BF16)
        query = pq[start : start + step, :]
        dq[start : start + step, :] = dot(ds, keys, 1, 0)
        key_part = dot(ds, query, 0, 0)
        value_part = dot(low, grad, 0, 0)
        if start == 0:
            dk[...] = key_part
            dv[...] = value_part
        else:
            dk[...] += key_part
            dv[...] += value_part
    if split:
        dk_own[...] = dk[0:count, :]
        dv_own[...] = dv[0:count, :]
        dkv_other[0] = dk[count:, :].astype(BF16)
        dkv_other[1] = dv[count:, :].astype(BF16)


def attend_back(pieces, pq, pk, vv, probs, slots, split):
    count, keys = pq.shape[0], pk.shape[0]
    step = 2 * slots if keys <= 2048 else slots
    limit = 20 if keys <= 2048 else 58
    piece = pl.BlockSpec((slots // 2, 2 * COLS), lambda h: (0, 0))
    rows = pl.BlockSpec((count, PAIR), lambda h: (0, h))
    cols = pl.BlockSpec((keys, PAIR), lambda h: (0, h))
    scratch = [pltpu.VMEM((LOCAL_HEADS, count, PAIR), BF16)]
    if split:
        specs = [rows, rows, rows, pl.BlockSpec((2, count, PAIR), lambda h: (0, 0, h))]
        shapes = [sds((count, WIDE), F32)] * 3 + [sds((2, count, WIDE), BF16)]
        scratch += [pltpu.VMEM((keys, PAIR), F32), pltpu.VMEM((keys, PAIR), F32)]
    else:
        specs = [rows, cols, cols]
        shapes = [sds((count, WIDE), F32), sds((keys, WIDE), F32), sds((keys, WIDE), F32)]
    return pl.pallas_call(
        partial(attend_back_body, step, split),
        grid=(LOCAL_HEADS,),
        in_specs=[piece] * 4
        + [rows, cols, cols, pl.BlockSpec((1, count, keys), lambda h: (h, 0, 0))],
        out_specs=specs,
        out_shape=shapes,
        scratch_shapes=scratch,
        name="attend_back",
        cost_estimate=cost(6),
        compiler_params=pltpu.CompilerParams(vmem_limit_bytes=limit << 20),
    )(*pieces, pq, pk, vv, probs)


def unpack(piece):
    return jnp.concatenate([piece[:, 0:COLS], piece[:, COLS:]], axis=0)


def normalize(summed):
    center = summed - jnp.mean(summed, axis=-1, keepdims=True)
    spread = jnp.mean(center * center, axis=-1, keepdims=True)
    rate = lax.rsqrt(spread + EPS)
    return center * rate, rate


def norm_back(grad, unit, rate, gain):
    scaled = grad * gain
    mean_one = jnp.mean(scaled, axis=-1, keepdims=True)
    mean_two = jnp.mean(scaled * unit, axis=-1, keepdims=True)
    return rate * (scaled - mean_one - unit * mean_two)


def total(values):
    return jnp.sum(values, axis=0, keepdims=True)


OUT_B, GAIN_1, SHIFT_1, DOWN_B, GAIN_2, SHIFT_2 = range(6)


def norm_one_body(sc, vecs, cx0, cx1, cx2, cx3, wo, hidden, low, unit_out, rate_out):
    acc = hidden[...].astype(F32) + vecs[OUT_B : OUT_B + 1, :]
    for rel, ref in enumerate((cx0, cx1, cx2, cx3)):
        at = pl.multiple_of((sc[CHIP] ^ rel) * COLS, COLS)
        acc += dot(unpack(ref[...]), wo[pl.ds(at, COLS), :], 1, 0)
    unit, rate = normalize(acc)
    first = unit * vecs[GAIN_1 : GAIN_1 + 1, :] + vecs[SHIFT_1 : SHIFT_1 + 1, :]
    low[...] = first.astype(BF16)
    unit_out[...] = unit
    rate_out[...] = jnp.broadcast_to(rate, rate_out.shape)


def mlp_body(chunk, sc, bias, x0, x1, wup, wdn, act, act_send, slope, own, send):
    slots = x0.shape[0]
    width = x0.shape[1]
    tokens = jnp.concatenate([x0[...], x1[...]], axis=0)
    acc = None
    for lo in range(0, wup.shape[1], chunk):
        pre = dot(tokens, wup[:, lo : lo + chunk], 1, 0) + bias[0:1, lo : lo + chunk]
        cdf = 0.5 * (1.0 + lax.erf(pre * 0.7071067811865476))
        pdf = jnp.exp(-0.5 * pre * pre) * 0.3989422804014327
        out = (pre * cdf).astype(BF16)
        slope[:, lo : lo + chunk] = cdf + pre * pdf
        to_quarter(sc, out, lo, width, act, act_send)
        part = dot(out, wdn[lo : lo + chunk, :], 1, 0)
        acc = part if acc is None else acc + part
    own[...] = acc[0:slots]
    send[...] = acc[slots:].astype(BF16)


def to_quarter(sc, values, lo, width, keep, send):
    tall, at = lo // width, lo % width

    @pl.when(sc[TALL] == tall)
    def _():
        keep[:, at : at + values.shape[1]] = values

    @pl.when(sc[TALL] != tall)
    def _():
        send[:, at : at + values.shape[1]] = values


def norm_two_body(sc, vecs, meta, own, received, unit_one, cotangent, output, gs, gs_low, sums):
    valid = meta[...].T[:, 8:9]
    first = unit_one[...] * vecs[GAIN_1 : GAIN_1 + 1, :] + vecs[SHIFT_1 : SHIFT_1 + 1, :]
    acc = own[...] + received[...].astype(F32) + vecs[DOWN_B : DOWN_B + 1, :] + first
    unit, rate = normalize(acc)
    gain = vecs[GAIN_2 : GAIN_2 + 1, :]
    output[...] = ((unit * gain + vecs[SHIFT_2 : SHIFT_2 + 1, :]) * valid).astype(BF16)
    grad = cotangent[...].astype(F32) * valid
    back = norm_back(grad, unit, rate, gain)
    gs[...] = back
    gs_low[...] = back.astype(BF16)
    sums[...] = jnp.zeros_like(sums)
    sums[DOWN_B : DOWN_B + 1, :] = total(back)
    sums[GAIN_2 : GAIN_2 + 1, :] = total(grad * unit)
    sums[SHIFT_2 : SHIFT_2 + 1, :] = total(grad)


def mlp_back_body(chunk, sc, g0, g1, slope, wup, wdn, low_keep, low_send, sums, own, send):
    slots = g0.shape[0]
    width = g0.shape[1]
    grads = jnp.concatenate([g0[...], g1[...]], axis=0)
    acc = None
    sums[...] = jnp.zeros_like(sums)
    for lo in range(0, wup.shape[1], chunk):
        pre = dot(grads, wdn[lo : lo + chunk, :], 1, 1) * slope[:, lo : lo + chunk]
        sums[0:1, lo : lo + chunk] = total(pre)
        low = pre.astype(BF16)
        to_quarter(sc, low, lo, width, low_keep, low_send)
        part = dot(low, wup[:, lo : lo + chunk], 1, 1)
        acc = part if acc is None else acc + part
    own[...] = acc[0:slots]
    send[...] = acc[slots:].astype(BF16)


def mlp_grads_body(
    shards, sc, x0, x1, x2, x3, g0, g1, g2, g3, act, act_r, low, low_r, keep, send
):
    tokens = jnp.concatenate([x0[...], x1[...], x2[...], x3[...]], axis=0)
    grads = jnp.concatenate([g0[...], g1[...], g2[...], g3[...]], axis=0)
    hidden = jnp.concatenate([act[...], act_r[...]], axis=0)
    back = jnp.concatenate([low[...], low_r[...]], axis=0)
    rows = tokens.shape[1] // shards
    for at in range(shards):
        lo = at * rows
        up = dot(tokens[:, lo : lo + rows], back, 0, 0)
        down = dot(hidden[:, lo : lo + rows], grads, 0, 0)

        @pl.when(sc[CORE] == 0)
        def _():
            keep[at] = up
            send[at] = down.astype(BF16)

        @pl.when(sc[CORE] == 1)
        def _():
            keep[at] = down
            send[at] = up.astype(BF16)


def fan_body(shards, sc, keep, received, *outs):
    for shift in range(shards):
        at = sc[SHARD] ^ shift
        value = keep[at] + received[at].astype(F32)
        outs[shift][...] = value.astype(outs[shift].dtype)


def relay_body(sc, value, received, out):
    out[...] = (value[...] + received[...].astype(F32)).astype(BF16)


def relay_second_body(sc, value, received, out):
    out[...] = (value[...] + received[1].astype(F32)).astype(BF16)


def qkv_fan_body(shards, sc, keep, received, planes, *outs):
    main = received.shape[1]
    small, half = planes.shape[1:]
    end = keep.shape[1]
    for shift in range(shards):
        at = sc[SHARD] ^ shift
        ref = outs[shift]
        ref[0:main, :] = (keep[at, 0:main, :] + received[at].astype(F32)).astype(ref.dtype)
        ref[main:end, :] = keep[at, main:, :].astype(ref.dtype)
        ref[end:, :] = planes[at].astype(ref.dtype)


def gather_sum_body(sc, own, *refs):
    acc = own[...]
    for ref in refs[:-1]:
        acc += ref[...].astype(F32)
    refs[-1][...] = acc.astype(refs[-1].dtype)


def out_fan_body(sc, keep, received, own, *sends):
    small = own.shape[1]
    for rel in range(4):
        at = pl.multiple_of((sc[CHIP] ^ rel) * small, small)
        value = keep[:, pl.ds(at, small), :] + received[:, pl.ds(at, small), :].astype(F32)
        if rel == 0:
            own[...] = value
        else:
            sends[rel - 1][...] = value.astype(BF16)


def plane_sum_body(sc, own, r1, r2, r3, out):
    out[...] = own[...] + r1[...].astype(F32) + r2[...].astype(F32) + r3[...].astype(F32)


def input_grad_body(sc, base, own, near, far, out):
    out[...] = base[...] + own[...] + near[0].astype(F32) + far[...].astype(F32)


def norm_one_back_body(
    sc, vecs, own, received, gs, unit_one, rate_one, wo, gf, gf_low, gcx, sums
):
    grad = gs[...] + own[...] + received[...].astype(F32)
    unit = unit_one[...]
    rate = rate_one[:, 0:1]
    back = norm_back(grad, unit, rate, vecs[GAIN_1 : GAIN_1 + 1, :])
    gf[...] = back
    low = back.astype(BF16)
    gf_low[...] = low
    sums[...] = jnp.zeros_like(sums)
    sums[OUT_B : OUT_B + 1, :] = total(back)
    sums[GAIN_1 : GAIN_1 + 1, :] = total(grad * unit)
    sums[SHIFT_1 : SHIFT_1 + 1, :] = total(grad)
    half = back.shape[0] // 2
    for rel in range(4):
        at = pl.multiple_of((sc[CHIP] ^ rel) * COLS, COLS)
        part = dot(low, wo[pl.ds(at, COLS), :], 1, 1).astype(BF16)
        gcx[rel, :, 0:COLS] = part[0:half]
        gcx[rel, :, COLS:] = part[half:]


def out_grads_body(sc, cx0, cx1, cx2, cx3, gf_low, keep, send):
    low = gf_low[...]
    half = keep.shape[2]
    for rel, ref in enumerate((cx0, cx1, cx2, cx3)):
        block = dot(unpack(ref[...]), low, 0, 0)
        chip = sc[CHIP] ^ rel
        for core in range(CORES):

            @pl.when(sc[CORE] == core)
            def _():
                keep[chip] = block[:, core * half : (core + 1) * half]
                other = 1 - core
                send[chip] = block[:, other * half : (other + 1) * half].astype(BF16)


def qkv_grads_body(
    shards, sc, meta, dq, dk_own, dv_own, dkv_rec, wall, sums_one, sums_two, sums_up,
    x, own, own_far, send, keep_w, send_w, packed,
):
    slots = x.shape[1]
    flags = meta[...].T
    lane = lax.broadcasted_iota(jnp.int32, (1, WIDE), 1)
    left = (lane % PAIR) < HEAD
    width = wall.shape[1]
    rows = width // shards
    half = rows // 2
    acc = [0.0] * 4
    for block in range(4):
        at = slice(block * slots, (block + 1) * slots)
        word = flags[:, block : block + 1] > 0
        query = dq[at, :] * SCALE
        parts = (
            jnp.where(word, query, 0.0),
            jnp.where(word, 0.0, query),
            jnp.where(left == word, dk_own[at, :] + dkv_rec[0, at, :].astype(F32), 0.0),
            dv_own[at, :] + dkv_rec[1, at, :].astype(F32),
        )
        acc = [a + total(p) for a, p in zip(acc, parts)]
        packed[0, at, 0:WIDE] = parts[0].astype(BF16)
        packed[1, at, 0:WIDE] = parts[1].astype(BF16)
        packed[0, at, WIDE:] = parts[2].astype(BF16)
        packed[1, at, WIDE:] = parts[3].astype(BF16)
    tokens = jnp.concatenate([x[rel] for rel in range(4)], axis=0)
    for group_rel, ref in enumerate((keep_w, send_w)):
        group = sc[CORE] ^ group_rel
        for at in range(shards):
            grad = dot(tokens[:, at * rows : (at + 1) * rows], packed[group], 0, 0)
            ref[at, 0:rows, :] = grad[:, 0:WIDE].astype(ref.dtype)
            folded = jnp.concatenate(
                [
                    grad[:, WIDE + h * PAIR : WIDE + h * PAIR + HEAD]
                    + grad[:, WIDE + h * PAIR + HEAD : WIDE + (h + 1) * PAIR]
                    for h in range(LOCAL_HEADS)
                ],
                axis=1,
            ).astype(ref.dtype)
            ref[at, rows : rows + half, 0:COLS] = folded[0:half]
            ref[at, rows : rows + half, COLS:] = folded[half:]
    for block in range(4):
        at = slice(block * slots, (block + 1) * slots)
        back = dot(packed[0, at, :], wall[0], 1, 1) + dot(packed[1, at, :], wall[1], 1, 1)
        if block == 0:
            own[...] = back
        elif block == 2:
            own_far[...] = back
        else:
            send[block // 2] = back.astype(BF16)
    keys = split_pairs(acc[2])
    values = split_pairs(acc[3])
    heads = [
        split_pairs(acc[0]),
        split_pairs(acc[1]),
        jnp.concatenate([keys[:, 0:COLS] + keys[:, COLS:], values[:, 0:COLS]], axis=1),
    ]
    norms = sums_one[...] + sums_two[...]
    for at in range(shards):
        mine = (sc[CHIP] == at).astype(F32)
        lo = at * rows
        lines = [line * mine for line in heads]
        for row in range(0, 6, 2):
            lines.append(
                jnp.concatenate(
                    [norms[row : row + 1, lo : lo + rows], norms[row + 1 : row + 2, lo : lo + rows]],
                    axis=1,
                )
            )
        units = jnp.concatenate(
            [sums_up[0:1, t * width + lo : t * width + lo + rows] for t in range(2)], axis=1
        )
        side = sc[SIDE].astype(F32)
        lines += [units * (1.0 - side), units * side]
        keep_w[at, rows + half :, :] = jnp.concatenate(lines, axis=0)


def place_qkv_body(sc, p0, p1, p2, p3, others, qg, kg, vg, og, qb, *refs):
    vectors, (ub, held) = refs[:8], refs[8:]
    rows = kg.shape[0]
    half = rows // 2
    small = rows // 4
    lines = 0.0
    for core_rel in range(CORES):
        for rel in range(4):
            value = (p0, p1, p2, p3)[rel][...] if core_rel == 0 else others[rel]
            lines += value[rows + half : rows + half + 8, :].astype(F32)
            held[sc[CORE] ^ core_rel, sc[CHIP] ^ rel] = value
    for core in range(CORES):
        for chip in range(CHIPS):
            piece = held[core, chip].astype(F32)
            lo = chip * COLS
            for which in range(2):
                qg[2 * core + which, :, lo : lo + COLS] = jnp.concatenate(
                    [
                        piece[0:rows, h * PAIR + which * HEAD : h * PAIR + (which + 1) * HEAD]
                        for h in range(LOCAL_HEADS)
                    ],
                    axis=1,
                )
            ref = kg if core == 0 else vg
            ref[0:half, lo : lo + COLS] = piece[rows : rows + half, 0:COLS]
            ref[half:, lo : lo + COLS] = piece[rows : rows + half, COLS:]
            og[chip * small : (chip + 1) * small, core * 2 * COLS : (core + 1) * 2 * COLS] = piece[
                rows + half + 8 :, :
            ]
    for which in range(4):
        qb[which : which + 1, :] = lines[
            which // 2 : which // 2 + 1, (which % 2) * COLS : (which % 2 + 1) * COLS
        ]
    for index, ref in enumerate(vectors):
        ref[...] = lines[2 + index // 2, (index % 2) * rows : (index % 2 + 1) * rows]
    ub[...] = jnp.concatenate([lines[6], lines[7]], axis=0)


def place_mlp_body(sc, p0, p1, p2, p3, others, ug, dg, held):
    rows, ff = ug.shape
    part = ff // 4
    side = part // 2
    unit = side // 2
    for core_rel in range(CORES):
        for rel in range(4):
            value = (p0, p1, p2, p3)[rel][...] if core_rel == 0 else others[rel]
            held[sc[CORE] ^ core_rel, sc[CHIP] ^ rel] = value
    for chip in range(CHIPS):
        lo = (chip & 1) * side + (chip >> 1) * unit
        piece = held[0, chip].astype(F32)
        for shard in range(4):
            at = shard * part + lo
            ug[:, at : at + unit] = piece[:, shard * unit : (shard + 1) * unit]
        dg[lo : lo + unit, :] = held[1, chip].astype(F32)


def local(
    shards,
    lanes,
    hidden,
    lengths,
    row_types,
    query_weight,
    query_bias,
    key_weight,
    key_bias,
    value_weight,
    value_bias,
    out_weight,
    out_bias,
    norm1_gain,
    norm1_bias,
    up_weight,
    up_bias,
    down_weight,
    down_bias,
    norm2_gain,
    norm2_bias,
    cotangent,
):
    groups = lanes // (CHIPS * CORES)
    shard = lax.axis_index("shard")
    lane = lax.axis_index("ctx")
    core, chip, group = lane & 1, (lane >> 1) & 3, lane >> 3
    chip_x, chip_y = chip & 1, chip >> 1
    spot = chip_y * 2 + core
    scalars = jnp.stack([shard, chip, core, spot, chip_x, chip_y, chip_x * 2 + core]).astype(jnp.int32)
    sets = [[g * 8 + i for g in range(groups)] for i in range(8)]

    def across(value, mask, name):
        with jax.named_scope(f"{name}_{mask}"):
            return lax.ppermute(value, "ctx", [(i, i ^ mask) for i in range(lanes)])

    def chips(value, rel, name):
        return across(value, rel << 1, name)

    def turn(value, shift, name):
        with jax.named_scope(f"{name}_z{shift}"):
            return lax.ppermute(value, "shard", [(i, i ^ shift) for i in range(shards)])

    def collect(value, name):
        far = turn(value, 2, name)
        far, near = lax.optimization_barrier((far, turn(value, 1, name)))
        return [near, far, turn(far, 1, name)]

    def reduce(parts, name, *others):
        _, near, far, last = parts
        last = after(turn(last, 1, name), *others)
        near = turn(near, 1, name)
        far = run(relay_body, "relay", sds(far.shape, BF16), scalars, far, last)
        return [near, turn(far, 2, name)], far

    def after(value, *others):
        return lax.optimization_barrier((value,) + others)[0]

    width = hidden.shape[2]
    slots = hidden.shape[1]
    rows = width // shards
    ff = up_weight.shape[1]
    part = ff // shards
    side = part // 2
    hid = hidden[0]
    cot = cotangent[0]
    small_rows = 8
    main = rows + rows // 2

    mine, other_mine = run(
        prep_qkv_body,
        "prep_qkv",
        [sds((main + small_rows + rows // 2, WIDE), BF16), sds((main, WIDE), BF16)],
        scalars,
        query_weight, key_weight, value_weight, out_weight, query_bias,
        key_bias, value_bias, out_bias, norm1_gain, norm1_bias,
        down_bias, norm2_gain, norm2_bias, up_bias,
        vmem=60,
    )
    own_w = collect(mine, "qkvw")
    quarter = rows // 4
    mlp_one = run(
        prep_mlp_body,
        "prep_mlp",
        sds((2 * quarter + side // 4, width), BF16),
        scalars,
        after(lax.dynamic_slice_in_dim(up_weight, spot * quarter, quarter, 0), own_w[1]),
        lax.dynamic_slice_in_dim(down_weight, chip_x * side + spot * (side // 4), side // 4, 0),
    )
    own_x = jnp.stack([hid] + [chips(hid, rel, "hid") for rel in range(1, 4)])
    mlp_z = collect(mlp_one, "mlpw")
    other_x = across(own_x, 1, "hid")
    other_w = [across(after(piece, other_x), 1, "qkvw") for piece in own_w]

    kinds = row_types.reshape(-1, slots)
    blocks = [group * 8 + (chip ^ rel) * 2 + (core ^ c) for c in range(CORES) for rel in range(4)]
    places = jnp.arange(slots, dtype=jnp.int32)
    word = jnp.concatenate([lax.dynamic_slice_in_dim(kinds, b, 1, 0) for b in blocks], axis=0)
    starts = jnp.stack(blocks)[:, None] * slots
    live = (starts + places[None, :] < lengths[0]).astype(F32)
    meta = jnp.concatenate([(word == 0).astype(F32), live], axis=0)

    wall, pq, pk, vv, vecs, up_shift, out_own, out_other = run(
        partial(qkv_body, shards),
        "qkv",
        [
            sds((2, width, 2 * WIDE), BF16),
            sds((4 * slots, WIDE), BF16),
            sds((8 * slots, WIDE), BF16),
            sds((8 * slots, WIDE), BF16),
            sds((8, width), F32),
            sds((1, ff // 2), F32),
            sds((shards - 1, quarter, width), BF16),
            sds((shards - 1, quarter, width), BF16),
        ],
        scalars,
        meta, mine, other_mine, own_x, other_x, *own_w, *other_w,
        scratch=[pltpu.VMEM((shards, small_rows, WIDE), F32)],
    )
    out_far = chips(out_own, 1, "outw")
    valid = live.reshape(1, 8 * slots)
    if groups > 1:
        gather = partial(lax.all_gather, axis_name="ctx", axis_index_groups=sets, tiled=True)
        pk, vv = gather(pk, axis=0), gather(vv, axis=0)
        valid = gather(valid, axis=1)
    mlp_far = [across(piece, 4, "mlpw") for piece in mlp_z]
    mlp_core = [across(piece, 1, "mlpw") for piece in mlp_z[:2]]
    probs, cx = attend(after(pq, mlp_core), pk, vv, valid, slots)
    cx = after(cx, out_far, mlp_far[0])
    cxs = [cx[0]] + [chips(cx[rel], rel, "cx") for rel in range(1, 4)]
    mlp_core += [across(piece, 1, "mlpw") for piece in (mlp_z[2], mlp_far[0], mlp_far[1])]
    cxs = after(cxs, mlp_core)
    *cxs, out_far = lax.optimization_barrier((*cxs, out_far))
    wo = run(
        partial(assemble_out_body, shards),
        "assemble_out",
        sds((width, width), BF16),
        scalars,
        out_weight, out_own, out_other, out_far, across(out_far, 1, "outw"),
    )
    low_one, unit_one, rate_one = run(
        norm_one_body,
        "norm_one",
        [sds((slots, width), BF16), sds((slots, width), F32), sds((slots, 128), F32)],
        scalars,
        vecs, *cxs, wo, hid,
    )
    low_two = chips(low_one, 1, "mlpx")
    low_two, far_one = lax.optimization_barrier((low_two, across(low_one, 4, "mlpy_x1")))
    far_two = chips(far_one, 1, "mlpy_x2")
    pieces = mlp_z + mlp_far
    mlp_core.append(across(after(mlp_far[2], low_two), 1, "mlpw"))
    wup, wdn = run(
        partial(assemble_mlp_body, shards),
        "assemble_mlp",
        [sds((width, ff // 2), BF16), sds((ff // 2, width), BF16)],
        scalars,
        up_weight, down_weight, *pieces, *mlp_core,
    )

    act, act_send, slope, own, send = run(
        partial(mlp_body, 384),
        "mlp",
        [
            sds((2 * slots, ff // 4), BF16),
            sds((2 * slots, ff // 4), BF16),
            sds((2 * slots, ff // 2), F32),
            sds((slots, width), F32),
            sds((slots, width), BF16),
        ],
        scalars,
        up_shift, low_one, low_two, wup, wdn,
    )
    received, far_two = lax.optimization_barrier((chips(send, 1, "mlpp"), far_two))
    act_far = across(act_send, 4, "mlpy_a")
    output, gs, gs_low, sums_two = run(
        norm_two_body,
        "norm_two",
        [
            sds((slots, width), BF16),
            sds((slots, width), F32),
            sds((slots, width), BF16),
            sds((8, width), F32),
        ],
        scalars,
        vecs, meta, own, received, unit_one, cot,
    )
    gs_other, gs_far_one, act_far = lax.optimization_barrier(
        (chips(gs_low, 1, "mlpg"), across(gs_low, 4, "mlpy_g1"), act_far)
    )
    gs_far_two = chips(gs_far_one, 1, "mlpy_g2")
    low_keep, low_send, sums_up, own, send = run(
        partial(mlp_back_body, 384),
        "mlp_back",
        [
            sds((2 * slots, ff // 4), BF16),
            sds((2 * slots, ff // 4), BF16),
            sds((8, ff // 2), F32),
            sds((slots, width), F32),
            sds((slots, width), BF16),
        ],
        scalars,
        gs_low, gs_other, slope, wup, wdn,
    )
    received, gs_far_two = lax.optimization_barrier((chips(send, 1, "mlpb"), gs_far_two))
    low_far = across(low_send, 4, "mlpy_l")
    gf, gf_low, gcx, sums_one = run(
        norm_one_back_body,
        "norm_one_back",
        [
            sds((slots, width), F32),
            sds((slots, width), BF16),
            sds((4, slots // 2, 2 * COLS), BF16),
            sds((8, width), F32),
        ],
        scalars,
        vecs, own, received, gs, unit_one, rate_one, wo,
    )
    gcs = [gcx[0]] + [chips(gcx[rel], rel, "gcx") for rel in range(1, 4)]
    keep_mlp, send_mlp = run(
        partial(mlp_grads_body, shards),
        "mlp_grads",
        [sds((shards, rows, width), F32), sds((shards, rows, width), BF16)],
        scalars,
        low_one, low_two, far_one, far_two, gs_low, gs_other, gs_far_one, gs_far_two,
        act, act_far, after(low_keep, gf_low), low_far,
    )
    keep_out, send_out = run(
        out_grads_body,
        "out_grads",
        [sds((CHIPS, COLS, width // 2), F32), sds((CHIPS, COLS, width // 2), BF16)],
        scalars,
        *cxs,
        after(gf_low, send_mlp),
    )

    kind = BF16 if groups == 1 else F32

    def spread(low, name, late=()):
        if groups > 1:
            low = lax.psum(low, "ctx", axis_index_groups=sets).astype(BF16)
        here = [low] + [chips(low, rel, name) for rel in range(1, 4)]
        return here + [across(after(jnp.stack(here), *late), 1, name)]

    def fan(size):
        return [sds(size, F32), sds(size, BF16), sds(size, F32), sds(size, BF16)]

    mlp_parts = run(
        partial(fan_body, shards),
        "fan_mlp",
        fan((rows, width)),
        scalars,
        keep_mlp,
        across(send_mlp, 1, "gm"),
    )
    out_parts = run(
        out_fan_body,
        "fan_out",
        [sds((CHIPS, quarter, width // 2), F32)] + [sds((CHIPS, quarter, width // 2), BF16)] * 3,
        scalars,
        keep_out,
        across(send_out, 1, "go"),
    )
    gcs, _, (out_own, *out_sends) = lax.optimization_barrier((gcs, mlp_parts[1], out_parts))
    if groups == 1:
        dq, dk_own, dv_own, dkv = attend_back(gcs, pq, pk, vv, probs, slots, True)
    else:
        count = 4 * slots
        scatter = partial(lax.psum_scatter, axis_name="ctx", axis_index_groups=sets, tiled=True)
        dq, dk, dv = attend_back(gcs, pq, pk, vv, probs, slots, False)
        dk, dv = scatter(dk), scatter(dv)
        dk_own, dv_own = dk[:count], dv[:count]
        dkv = jnp.stack([dk[count:], dv[count:]]).astype(BF16)
    planes = run(
        plane_sum_body,
        "plane_out",
        sds((shards, quarter, width // 2), F32),
        scalars,
        after(out_own, dq),
        *[chips(out_sends[rel - 1], rel, "go") for rel in range(1, 4)],
    )
    dkv_rec = across(after(dkv, planes), 1, "dkv")
    own, own_far, send, keep_w, send_w = run(
        partial(qkv_grads_body, shards),
        "qkv_grads",
        [
            sds((slots, width), F32),
            sds((slots, width), F32),
            sds((2, slots, width), BF16),
            sds((shards, main + small_rows, WIDE), F32),
            sds((shards, main, WIDE), BF16),
        ],
        scalars,
        meta, dq, dk_own, dv_own, dkv_rec, wall, sums_one, sums_two, sums_up, own_x,
        scratch=[pltpu.VMEM((2, 4 * slots, 2 * WIDE), BF16)],
    )
    mlp_recs, gm_far = reduce(mlp_parts, "gm", own)
    size = main + small_rows + quarter
    qkv_parts = run(
        partial(qkv_fan_body, shards),
        "fan_qkv",
        fan((size, WIDE)),
        scalars,
        keep_w,
        across(after(send_w, gm_far), 1, "gq"),
        planes,
    )
    qkv_recs, gq_far = reduce(qkv_parts, "gq")

    near = chips(send, 1, "ig")
    far = run(
        relay_second_body, "relay_ig", sds((slots, width), BF16), scalars, own_far, near
    )
    input_grad = run(
        input_grad_body,
        "input_grad",
        sds((slots, width), F32),
        scalars,
        gf, own, near, chips(far, 2, "ig"),
    )

    mlp_recs = after(mlp_recs, gq_far, far)
    low = run(
        gather_sum_body, "sum_mlp", sds((rows, width), kind), scalars, mlp_parts[0], *mlp_recs
    )
    done_mlp = spread(low, "gm", (input_grad, qkv_recs))
    ug, dg = run(
        place_mlp_body,
        "place_mlp",
        [sds((rows, ff), F32), sds((part, width), F32)],
        scalars,
        *done_mlp,
        scratch=[pltpu.VMEM((CORES, CHIPS, rows, width), BF16)],
    )
    low = run(
        gather_sum_body, "sum_qkv", sds((size, WIDE), kind), scalars, qkv_parts[0], *qkv_recs
    )
    done_qkv = spread(low, "gq", (ug, dg))

    vec = sds((rows,), F32)
    qg, kg, vg, og, qbg, kbg, vbg, obg, g1g, b1g, dbg, g2g, b2g, ubg = run(
        place_qkv_body,
        "place_qkv",
        [
            sds((4, rows, width), F32), sds((rows, width), F32), sds((rows, width), F32),
            sds((rows, width), F32), sds((4, rows), F32), vec, vec, vec, vec, vec, vec, vec, vec,
            sds((4 * rows,), F32),
        ],
        scalars,
        *done_qkv,
        scratch=[pltpu.VMEM((CORES, CHIPS, size, WIDE), BF16)],
    )
    return (
        output[None], input_grad[None], qg, qbg, kg, kbg, vg, vbg, og, obg,
        g1g, b1g, ug, ubg, dg, dbg, g2g, b2g,
    )


def solution(mesh):
    vec, mat = P("shard"), P("shard", None)
    tokens = P("shard", "ctx", None)
    placed = (
        tokens, vec, mat, P(None, "shard", None), P(None, "shard"), mat, vec, mat, vec, mat,
        vec, vec, vec, mat, vec, mat, vec, vec, vec, tokens,
    )
    result = (
        tokens, tokens, P(None, "shard", None), P(None, "shard"), mat, vec, mat, vec, mat, vec,
        vec, vec, mat, vec, mat, vec, vec, vec,
    )
    return jax.shard_map(
        partial(local, mesh.shape["shard"], mesh.shape["ctx"]),
        mesh=mesh,
        in_specs=placed,
        out_specs=result,
        check_vma=False,
    )
```

```python
from functools import partial

import jax
import jax.numpy as jnp
from jax import lax
from jax.experimental import pallas as pl
from jax.experimental.pallas import tpu as pltpu
from jax.sharding import PartitionSpec as P

HEADS = 12
HEAD = 64
CHIPS = 4
CORES = 2
LOCAL_HEADS = HEADS // CHIPS
COLS = LOCAL_HEADS * HEAD
PAIR = 2 * HEAD
WIDE = LOCAL_HEADS * PAIR

EPS = 1e-12
SCALE = 0.125
NEG = -1000000000.0
F32 = jnp.float32
BF16 = jnp.bfloat16

SMEM = pl.BlockSpec(memory_space=pltpu.SMEM)
VMEM = pl.BlockSpec(memory_space=pltpu.VMEM)


def sds(shape, dtype):
    return jax.ShapeDtypeStruct(shape, dtype)


def dot(left, right, over_left, over_right):
    return lax.dot_general(
        left, right, (((over_left,), (over_right,)), ((), ())), preferred_element_type=F32
    )


def cost(micros):
    return pl.CostEstimate(flops=1, bytes_accessed=int(micros * 3e6), transcendentals=0)


MICROS = {
    "mlp": 3.5, "mlp_back": 3.5, "mlp_grads": 3.3, "out_grads": 2, "qkv_grads": 5,
    "place_qkv": 3.5, "place_mlp": 3,
}


def run(body, name, outs, scalars, *arrays, scratch=(), flops=0, vmem=24):
    many = isinstance(outs, (list, tuple))
    return pl.pallas_call(
        body,
        out_shape=outs,
        in_specs=[SMEM] + [VMEM] * len(arrays),
        out_specs=[VMEM] * len(outs) if many else VMEM,
        scratch_shapes=list(scratch),
        name=name,
        cost_estimate=cost(MICROS.get(name, 1)),
        compiler_params=pltpu.CompilerParams(vmem_limit_bytes=vmem << 20),
    )(scalars, *arrays)


SHARD, CHIP, CORE, SPOT, SIDE, TALL, PLACE = range(7)


def prep_qkv_body(sc, qw, kw, vw, ow, qb, *refs):
    vectors, (ub, own, other) = refs[:8], refs[8:]
    rows = kw.shape[0]
    half = rows // 2
    wide = [ref[...].astype(F32).reshape(1, rows) for ref in vectors]
    queries = qb[...].astype(F32)
    long = ub[...].astype(F32).reshape(1, 4 * rows)
    lines = [jnp.concatenate([queries[i : i + 1], queries[i + 1 : i + 2]], axis=1) for i in (0, 2)]
    lines += [jnp.concatenate(wide[i : i + 2], axis=1) for i in range(0, 8, 2)]
    lines += [long[:, 0 : 2 * rows], long[:, 2 * rows :]]
    small = jnp.concatenate(lines, axis=0).astype(BF16)
    end = rows + half + small.shape[0]
    own[rows + half : end, :] = small
    third = ow[pl.ds(pl.multiple_of(sc[PLACE] * (rows // 4), rows // 4), rows // 4), :]
    own[end : end + rows // 4, :] = third[:, 0:WIDE]
    own[end + rows // 4 :, :] = third[:, WIDE:]
    for chip in range(CHIPS):
        for core in range(CORES):

            @pl.when((sc[CHIP] == chip) & (sc[CORE] == core))
            def _():
                lo = chip * COLS
                for out, group in ((own, core), (other, 1 - core)):
                    first = qw[2 * group, :, lo : lo + COLS]
                    second = qw[2 * group + 1, :, lo : lo + COLS]
                    mix = []
                    for h in range(LOCAL_HEADS):
                        mix += [
                            first[:, h * HEAD : (h + 1) * HEAD],
                            second[:, h * HEAD : (h + 1) * HEAD],
                        ]
                    out[0:rows, :] = jnp.concatenate(mix, axis=1)
                    src = vw if group else kw
                    out[rows : rows + half, 0:COLS] = src[0:half, lo : lo + COLS]
                    out[rows : rows + half, COLS:] = src[half:rows, lo : lo + COLS]


def prep_mlp_body(sc, up, down, out):
    rows, ff = up.shape
    part = ff // 4
    side = part // 2
    unit = side // 2
    for chip_x in range(2):

        @pl.when(sc[SIDE] == chip_x)
        def _():
            for tall in range(2):
                for piece in range(4):
                    lo = piece * part + chip_x * side + tall * unit
                    out[tall * rows : (tall + 1) * rows, piece * unit : (piece + 1) * unit] = up[
                        :, lo : lo + unit
                    ]

    out[2 * rows :, :] = down[...]


def assemble_out_body(shards, sc, whole, own, other, own_far, other_far, wo):
    rows = wo.shape[0] // shards
    small = rows // 4
    wo[pl.ds(pl.multiple_of(sc[SHARD] * rows, rows), rows), :] = whole[...]
    for rel, ref in enumerate((own, other, own_far, other_far)):
        for shift in range(1, shards):
            owner = sc[SHARD] ^ shift
            at = pl.multiple_of(owner * rows + (sc[PLACE] ^ rel) * small, small)
            wo[pl.ds(at, small), :] = ref[shift - 1]


def assemble_mlp_body(shards, sc, up, down, *refs):
    pieces, (wup, wdn) = refs[:-2], refs[-2:]
    rows = wup.shape[0] // shards
    part = wdn.shape[0] // shards
    width = wdn.shape[1]
    unit = part // 2
    small = rows // 4
    at = pl.multiple_of(sc[SHARD] * rows, rows)
    for chip_x in range(2):

        @pl.when(sc[SIDE] == chip_x)
        def _():
            for tall in range(2):
                for piece in range(4):
                    lo = piece * 2 * part + chip_x * part + tall * unit
                    to = tall * width + piece * unit
                    wup[pl.ds(at, rows), to : to + unit] = up[:, lo : lo + unit]

    for tall in range(2):
        at = pl.multiple_of(tall * width + sc[SHARD] * unit, unit)
        lo = pl.multiple_of(sc[SIDE] * part + tall * unit, unit)
        wdn[pl.ds(at, unit), :] = down[pl.ds(lo, unit), :]
    for index, ref in enumerate(pieces):
        rel, shift = index // (shards - 1), index % (shards - 1) + 1
        spot = sc[SPOT] ^ (rel // 2 + rel % 2 * 2)
        owner = sc[SHARD] ^ shift
        at = pl.multiple_of(owner * rows + spot * small, small)
        wup[pl.ds(at, small), 0:width] = ref[0:small, :]
        wup[pl.ds(at, small), width:] = ref[small : 2 * small, :]
        at = (spot // 2) * width + owner * unit + (spot % 2) * (unit // 2)
        at = pl.multiple_of(at, unit // 2)
        wdn[pl.ds(at, unit // 2), :] = ref[2 * small :, :]


def split_pairs(line):
    pieces = [
        jnp.concatenate(
            [line[:, h * PAIR + t * HEAD : h * PAIR + (t + 1) * HEAD] for h in range(LOCAL_HEADS)],
            axis=1,
        )
        for t in range(2)
    ]
    return jnp.concatenate(pieces, axis=1)


def join_pairs(left, right):
    mix = []
    for h in range(LOCAL_HEADS):
        mix += [left[:, h * HEAD : (h + 1) * HEAD], right[:, h * HEAD : (h + 1) * HEAD]]
    return jnp.concatenate(mix, axis=1)


def qkv_body(shards, sc, meta, mine, other_mine, own_x, other_x, *refs):
    own_w = [mine] + list(refs[: shards - 1])
    other_w = [other_mine] + list(refs[shards - 1 : 2 * shards - 2])
    wall, pq, pk, vv, vecs, upb, out_own, out_other, held = refs[2 * shards - 2 :]
    slots = own_x.shape[1]
    small = out_own.shape[1]
    width = wall.shape[1]
    rows = width // shards
    half = rows // 2
    unit = rows
    for which in range(CORES):
        group = sc[CORE] ^ which
        keep = (group == 0).astype(F32).astype(BF16)
        for shift in range(shards):
            ref = (other_w if which else own_w)[shift]
            if shift > 0:
                third = out_other if which else out_own
                end = ref.shape[0] - 2 * small
                third[shift - 1, :, 0:WIDE] = ref[end : end + small, :]
                third[shift - 1, :, WIDE:] = ref[end + small :, :]
            owner = sc[SHARD] ^ shift
            at = pl.multiple_of(owner * rows, half)
            wall[group, pl.ds(at, rows), 0:WIDE] = ref[0:rows, :]
            if which == 0:
                held[owner] = ref[rows + half : ref.shape[0] - 2 * small, :].astype(F32)
            for part in range(2):
                mix = []
                for h in range(LOCAL_HEADS):
                    lo = part * COLS + h * HEAD
                    one = ref[rows : rows + half, lo : lo + HEAD]
                    mix += [one, one * keep]
                low = pl.multiple_of(owner * rows + part * half, half)
                wall[group, pl.ds(low, half), WIDE:] = jnp.concatenate(mix, axis=1)
    vecs[...] = jnp.zeros_like(vecs)
    for shard in range(shards):
        lo = shard * rows
        for row in range(6):
            line = 3 + row // 2
            col = (row % 2) * rows
            vecs[row : row + 1, lo : lo + rows] = held[shard, line : line + 1, col : col + rows]
        for chip_x in range(2):

            @pl.when(sc[SIDE] == chip_x)
            def _():
                for tall in range(2):
                    to = tall * width + shard * unit
                    upb[0:1, to : to + unit] = held[
                        shard, 6 + chip_x : 7 + chip_x, tall * unit : (tall + 1) * unit
                    ]

    table = held[sc[CHIP]]
    bias = [join_pairs(table[i : i + 1, 0:COLS], table[i : i + 1, COLS:]) for i in range(2)]
    key_bias = join_pairs(table[2:3, 0:COLS], table[2:3, 0:COLS])
    value_bias = join_pairs(table[2:3, COLS:], jnp.zeros((1, COLS), F32))
    flags = meta[...].T
    lane = lax.broadcasted_iota(jnp.int32, (1, WIDE), 1)
    left = (lane % PAIR) < HEAD
    for block in range(8):
        tokens = (own_x if block < 4 else other_x)[block % 4]
        word = flags[:, block : block + 1] > 0
        at = slice(block * slots, (block + 1) * slots)
        if block < 4:
            first = dot(tokens, wall[0], 1, 0)
            second = dot(tokens, wall[1], 1, 0)
            query = jnp.where(word, first[:, 0:WIDE] + bias[0], second[:, 0:WIDE] + bias[1]) * SCALE
            pq[at, :] = query.astype(BF16)
            key, value = first[:, WIDE:], second[:, WIDE:]
        else:
            key = dot(tokens, wall[0, :, WIDE:], 1, 0)
            value = dot(tokens, wall[1, :, WIDE:], 1, 0)
        pk[at, :] = jnp.where(left == word, key + key_bias, 0.0).astype(BF16)
        vv[at, :] = (value + value_bias).astype(BF16)


def attend_body(step, pq, pk, vv, valid, probs, cx):
    head = pl.program_id(0)
    count = pq.shape[0]
    slots = count // 4
    keep = valid[...] > 0
    keys = pk[...]
    values = vv[...]
    for start in range(0, count, step):
        scores = dot(pq[start : start + step, :], keys, 1, 1)
        scores = jnp.where(keep, scores, NEG)
        top = jnp.max(scores, axis=-1, keepdims=True)
        expo = jnp.exp(scores - top)
        share = 1.0 / jnp.sum(expo, axis=-1, keepdims=True)
        low = (expo * share).astype(BF16)
        probs[0, start : start + step, :] = low
        mixed = dot(low, values, 1, 0)[:, 0:HEAD].astype(BF16)
        for h in range(LOCAL_HEADS):

            @pl.when(head == h)
            def _():
                for at in range(0, step, slots):
                    block = (start + at) // slots
                    mid = at + slots // 2
                    cx[block, :, h * HEAD : (h + 1) * HEAD] = mixed[at:mid]
                    cx[block, :, COLS + h * HEAD : COLS + (h + 1) * HEAD] = mixed[mid : at + slots]


def attend(pq, pk, vv, valid, slots):
    count, keys = pq.shape[0], pk.shape[0]
    step = 2 * slots if keys <= 2048 else slots
    limit = 14 if keys <= 2048 else 56
    return pl.pallas_call(
        partial(attend_body, step),
        grid=(LOCAL_HEADS,),
        in_specs=[
            pl.BlockSpec((count, PAIR), lambda h: (0, h)),
            pl.BlockSpec((keys, PAIR), lambda h: (0, h)),
            pl.BlockSpec((keys, PAIR), lambda h: (0, h)),
            pl.BlockSpec((1, keys), lambda h: (0, 0)),
        ],
        out_specs=[
            pl.BlockSpec((1, count, keys), lambda h: (h, 0, 0)),
            pl.BlockSpec((4, slots // 2, 2 * COLS), lambda h: (0, 0, 0)),
        ],
        out_shape=[
            sds((LOCAL_HEADS, count, keys), BF16),
            sds((4, slots // 2, 2 * COLS), BF16),
        ],
        name="attend",
        cost_estimate=cost(5.5),
        compiler_params=pltpu.CompilerParams(vmem_limit_bytes=limit << 20),
    )(pq, pk, vv, valid)


def attend_back_body(step, split, gc0, gc1, gc2, gc3, pq, pk, vv, probs, dq, *refs):
    head = pl.program_id(0)
    count = pq.shape[0]
    slots = count // 4
    half = slots // 2
    if split:
        dk_own, dv_own, dkv_other, gcs, dk, dv = refs
    else:
        dk, dv, gcs = refs

    @pl.when(head == 0)
    def _():
        gcs[...] = jnp.zeros_like(gcs)
        for block, ref in enumerate((gc0, gc1, gc2, gc3)):
            for h in range(LOCAL_HEADS):
                lo = block * slots
                gcs[h, lo : lo + half, 0:HEAD] = ref[:, h * HEAD : (h + 1) * HEAD]
                gcs[h, lo + half : lo + slots, 0:HEAD] = ref[
                    :, COLS + h * HEAD : COLS + (h + 1) * HEAD
                ]

    keys = pk[...]
    values = vv[...]
    for start in range(0, count, step):
        grad = gcs[head, start : start + step, :]
        low = probs[0, start : start + step, :]
        wide = low.astype(F32)
        moved = dot(grad, values, 1, 1)
        inner = jnp.sum(wide * moved, axis=-1, keepdims=True)
        ds = (wide * (moved - inner)).astype(BF16)
        query = pq[start : start + step, :]
        dq[start : start + step, :] = dot(ds, keys, 1, 0)
        key_part = dot(ds, query, 0, 0)
        value_part = dot(low, grad, 0, 0)
        if start == 0:
            dk[...] = key_part
            dv[...] = value_part
        else:
            dk[...] += key_part
            dv[...] += value_part
    if split:
        dk_own[...] = dk[0:count, :]
        dv_own[...] = dv[0:count, :]
        dkv_other[0] = dk[count:, :].astype(BF16)
        dkv_other[1] = dv[count:, :].astype(BF16)


def attend_back(pieces, pq, pk, vv, probs, slots, split):
    count, keys = pq.shape[0], pk.shape[0]
    step = 2 * slots if keys <= 2048 else slots
    limit = 20 if keys <= 2048 else 58
    piece = pl.BlockSpec((slots // 2, 2 * COLS), lambda h: (0, 0))
    rows = pl.BlockSpec((count, PAIR), lambda h: (0, h))
    cols = pl.BlockSpec((keys, PAIR), lambda h: (0, h))
    scratch = [pltpu.VMEM((LOCAL_HEADS, count, PAIR), BF16)]
    if split:
        specs = [rows, rows, rows, pl.BlockSpec((2, count, PAIR), lambda h: (0, 0, h))]
        shapes = [sds((count, WIDE), F32)] * 3 + [sds((2, count, WIDE), BF16)]
        scratch += [pltpu.VMEM((keys, PAIR), F32), pltpu.VMEM((keys, PAIR), F32)]
    else:
        specs = [rows, cols, cols]
        shapes = [sds((count, WIDE), F32), sds((keys, WIDE), F32), sds((keys, WIDE), F32)]
    return pl.pallas_call(
        partial(attend_back_body, step, split),
        grid=(LOCAL_HEADS,),
        in_specs=[piece] * 4
        + [rows, cols, cols, pl.BlockSpec((1, count, keys), lambda h: (h, 0, 0))],
        out_specs=specs,
        out_shape=shapes,
        scratch_shapes=scratch,
        name="attend_back",
        cost_estimate=cost(6),
        compiler_params=pltpu.CompilerParams(vmem_limit_bytes=limit << 20),
    )(*pieces, pq, pk, vv, probs)


def unpack(piece):
    return jnp.concatenate([piece[:, 0:COLS], piece[:, COLS:]], axis=0)


def normalize(summed):
    center = summed - jnp.mean(summed, axis=-1, keepdims=True)
    spread = jnp.mean(center * center, axis=-1, keepdims=True)
    rate = lax.rsqrt(spread + EPS)
    return center * rate, rate


def norm_back(grad, unit, rate, gain):
    scaled = grad * gain
    mean_one = jnp.mean(scaled, axis=-1, keepdims=True)
    mean_two = jnp.mean(scaled * unit, axis=-1, keepdims=True)
    return rate * (scaled - mean_one - unit * mean_two)


def total(values):
    return jnp.sum(values, axis=0, keepdims=True)


OUT_B, GAIN_1, SHIFT_1, DOWN_B, GAIN_2, SHIFT_2 = range(6)


def norm_one_body(sc, vecs, cx0, cx1, cx2, cx3, wo, hidden, low, unit_out, rate_out):
    acc = hidden[...].astype(F32) + vecs[OUT_B : OUT_B + 1, :]
    for rel, ref in enumerate((cx0, cx1, cx2, cx3)):
        at = pl.multiple_of((sc[CHIP] ^ rel) * COLS, COLS)
        acc += dot(unpack(ref[...]), wo[pl.ds(at, COLS), :], 1, 0)
    unit, rate = normalize(acc)
    first = unit * vecs[GAIN_1 : GAIN_1 + 1, :] + vecs[SHIFT_1 : SHIFT_1 + 1, :]
    low[...] = first.astype(BF16)
    unit_out[...] = unit
    rate_out[...] = jnp.broadcast_to(rate, rate_out.shape)


def mlp_body(chunk, sc, bias, x0, x1, wup, wdn, act, act_send, slope, own, send):
    slots = x0.shape[0]
    width = x0.shape[1]
    tokens = jnp.concatenate([x0[...], x1[...]], axis=0)
    acc = None
    for lo in range(0, wup.shape[1], chunk):
        pre = dot(tokens, wup[:, lo : lo + chunk], 1, 0) + bias[0:1, lo : lo + chunk]
        cdf = 0.5 * (1.0 + lax.erf(pre * 0.7071067811865476))
        pdf = jnp.exp(-0.5 * pre * pre) * 0.3989422804014327
        out = (pre * cdf).astype(BF16)
        slope[:, lo : lo + chunk] = cdf + pre * pdf
        to_quarter(sc, out, lo, width, act, act_send)
        part = dot(out, wdn[lo : lo + chunk, :], 1, 0)
        acc = part if acc is None else acc + part
    own[...] = acc[0:slots]
    send[...] = acc[slots:].astype(BF16)


def to_quarter(sc, values, lo, width, keep, send):
    tall, at = lo // width, lo % width

    @pl.when(sc[TALL] == tall)
    def _():
        keep[:, at : at + values.shape[1]] = values

    @pl.when(sc[TALL] != tall)
    def _():
        send[:, at : at + values.shape[1]] = values


def norm_two_body(sc, vecs, meta, own, received, unit_one, cotangent, output, gs, gs_low, sums):
    valid = meta[...].T[:, 8:9]
    first = unit_one[...] * vecs[GAIN_1 : GAIN_1 + 1, :] + vecs[SHIFT_1 : SHIFT_1 + 1, :]
    acc = own[...] + received[...].astype(F32) + vecs[DOWN_B : DOWN_B + 1, :] + first
    unit, rate = normalize(acc)
    gain = vecs[GAIN_2 : GAIN_2 + 1, :]
    output[...] = ((unit * gain + vecs[SHIFT_2 : SHIFT_2 + 1, :]) * valid).astype(BF16)
    grad = cotangent[...].astype(F32) * valid
    back = norm_back(grad, unit, rate, gain)
    gs[...] = back
    gs_low[...] = back.astype(BF16)
    sums[...] = jnp.zeros_like(sums)
    sums[DOWN_B : DOWN_B + 1, :] = total(back)
    sums[GAIN_2 : GAIN_2 + 1, :] = total(grad * unit)
    sums[SHIFT_2 : SHIFT_2 + 1, :] = total(grad)


def mlp_back_body(chunk, sc, g0, g1, slope, wup, wdn, low_keep, low_send, sums, own, send):
    slots = g0.shape[0]
    width = g0.shape[1]
    grads = jnp.concatenate([g0[...], g1[...]], axis=0)
    acc = None
    sums[...] = jnp.zeros_like(sums)
    for lo in range(0, wup.shape[1], chunk):
        pre = dot(grads, wdn[lo : lo + chunk, :], 1, 1) * slope[:, lo : lo + chunk]
        sums[0:1, lo : lo + chunk] = total(pre)
        low = pre.astype(BF16)
        to_quarter(sc, low, lo, width, low_keep, low_send)
        part = dot(low, wup[:, lo : lo + chunk], 1, 1)
        acc = part if acc is None else acc + part
    own[...] = acc[0:slots]
    send[...] = acc[slots:].astype(BF16)


def mlp_grads_body(
    shards, sc, x0, x1, x2, x3, g0, g1, g2, g3, act, act_r, low, low_r, keep, send
):
    tokens = jnp.concatenate([x0[...], x1[...], x2[...], x3[...]], axis=0)
    grads = jnp.concatenate([g0[...], g1[...], g2[...], g3[...]], axis=0)
    hidden = jnp.concatenate([act[...], act_r[...]], axis=0)
    back = jnp.concatenate([low[...], low_r[...]], axis=0)
    rows = tokens.shape[1] // shards
    for at in range(shards):
        lo = at * rows
        up = dot(tokens[:, lo : lo + rows], back, 0, 0)
        down = dot(hidden[:, lo : lo + rows], grads, 0, 0)

        @pl.when(sc[CORE] == 0)
        def _():
            keep[at] = up
            send[at] = down.astype(BF16)

        @pl.when(sc[CORE] == 1)
        def _():
            keep[at] = down
            send[at] = up.astype(BF16)


def fan_body(shards, sc, keep, received, *outs):
    for shift in range(shards):
        at = sc[SHARD] ^ shift
        value = keep[at] + received[at].astype(F32)
        outs[shift][...] = value.astype(outs[shift].dtype)


def relay_body(sc, value, received, out):
    out[...] = (value[...] + received[...].astype(F32)).astype(BF16)


def relay_halves_body(sc, value, received, one, two):
    half = one.shape[0]
    one[...] = (value[0:half, :] + received[0:half, :].astype(F32)).astype(BF16)
    two[...] = (value[half:, :] + received[half:, :].astype(F32)).astype(BF16)


def sum_halves_body(sc, own, near, one, two, out):
    half = one.shape[0]
    value = own[...] + near[...].astype(F32)
    out[0:half, :] = (value[0:half] + one[...].astype(F32)).astype(out.dtype)
    out[half:, :] = (value[half:] + two[...].astype(F32)).astype(out.dtype)


def relay_second_body(sc, value, received, out):
    out[...] = (value[...] + received[1].astype(F32)).astype(BF16)


def qkv_fan_body(shards, sc, keep, received, planes, *outs):
    main = received.shape[1]
    small, half = planes.shape[1:]
    end = keep.shape[1]
    for shift in range(shards):
        at = sc[SHARD] ^ shift
        ref = outs[shift]
        ref[0:main, :] = (keep[at, 0:main, :] + received[at].astype(F32)).astype(ref.dtype)
        ref[main:end, :] = keep[at, main:, :].astype(ref.dtype)
        ref[end:, :] = planes[at].astype(ref.dtype)


def gather_sum_body(sc, own, *refs):
    acc = own[...]
    for ref in refs[:-1]:
        acc += ref[...].astype(F32)
    refs[-1][...] = acc.astype(refs[-1].dtype)


def out_fan_body(sc, keep, received, own, *sends):
    small = own.shape[1]
    for rel in range(4):
        at = pl.multiple_of((sc[CHIP] ^ rel) * small, small)
        value = keep[:, pl.ds(at, small), :] + received[:, pl.ds(at, small), :].astype(F32)
        if rel == 0:
            own[...] = value
        else:
            sends[rel - 1][...] = value.astype(BF16)


def plane_sum_body(sc, own, r1, r2, r3, out):
    out[...] = own[...] + r1[...].astype(F32) + r2[...].astype(F32) + r3[...].astype(F32)


def input_grad_body(sc, base, own, near, far, out):
    out[...] = base[...] + own[...] + near[0].astype(F32) + far[...].astype(F32)


def norm_one_back_body(
    sc, vecs, own, received, gs, unit_one, rate_one, wo, gf, gf_low, gcx, sums
):
    grad = gs[...] + own[...] + received[...].astype(F32)
    unit = unit_one[...]
    rate = rate_one[:, 0:1]
    back = norm_back(grad, unit, rate, vecs[GAIN_1 : GAIN_1 + 1, :])
    gf[...] = back
    low = back.astype(BF16)
    gf_low[...] = low
    sums[...] = jnp.zeros_like(sums)
    sums[OUT_B : OUT_B + 1, :] = total(back)
    sums[GAIN_1 : GAIN_1 + 1, :] = total(grad * unit)
    sums[SHIFT_1 : SHIFT_1 + 1, :] = total(grad)
    half = back.shape[0] // 2
    for rel in range(4):
        at = pl.multiple_of((sc[CHIP] ^ rel) * COLS, COLS)
        part = dot(low, wo[pl.ds(at, COLS), :], 1, 1).astype(BF16)
        gcx[rel, :, 0:COLS] = part[0:half]
        gcx[rel, :, COLS:] = part[half:]


def out_grads_body(sc, cx0, cx1, cx2, cx3, gf_low, keep, send):
    low = gf_low[...]
    half = keep.shape[2]
    for rel, ref in enumerate((cx0, cx1, cx2, cx3)):
        block = dot(unpack(ref[...]), low, 0, 0)
        chip = sc[CHIP] ^ rel
        for core in range(CORES):

            @pl.when(sc[CORE] == core)
            def _():
                keep[chip] = block[:, core * half : (core + 1) * half]
                other = 1 - core
                send[chip] = block[:, other * half : (other + 1) * half].astype(BF16)


def qkv_grads_body(
    shards, sc, meta, dq, dk_own, dv_own, dkv_rec, wall, sums_one, sums_two, sums_up,
    x, own, own_far, send, keep_w, send_w, packed,
):
    slots = x.shape[1]
    flags = meta[...].T
    lane = lax.broadcasted_iota(jnp.int32, (1, WIDE), 1)
    left = (lane % PAIR) < HEAD
    width = wall.shape[1]
    rows = width // shards
    half = rows // 2
    acc = [0.0] * 4
    for block in range(4):
        at = slice(block * slots, (block + 1) * slots)
        word = flags[:, block : block + 1] > 0
        query = dq[at, :] * SCALE
        parts = (
            jnp.where(word, query, 0.0),
            jnp.where(word, 0.0, query),
            jnp.where(left == word, dk_own[at, :] + dkv_rec[0, at, :].astype(F32), 0.0),
            dv_own[at, :] + dkv_rec[1, at, :].astype(F32),
        )
        acc = [a + total(p) for a, p in zip(acc, parts)]
        packed[0, at, 0:WIDE] = parts[0].astype(BF16)
        packed[1, at, 0:WIDE] = parts[1].astype(BF16)
        packed[0, at, WIDE:] = parts[2].astype(BF16)
        packed[1, at, WIDE:] = parts[3].astype(BF16)
    tokens = jnp.concatenate([x[rel] for rel in range(4)], axis=0)
    for group_rel, ref in enumerate((keep_w, send_w)):
        group = sc[CORE] ^ group_rel
        for at in range(shards):
            grad = dot(tokens[:, at * rows : (at + 1) * rows], packed[group], 0, 0)
            ref[at, 0:rows, :] = grad[:, 0:WIDE].astype(ref.dtype)
            folded = jnp.concatenate(
                [
                    grad[:, WIDE + h * PAIR : WIDE + h * PAIR + HEAD]
                    + grad[:, WIDE + h * PAIR + HEAD : WIDE + (h + 1) * PAIR]
                    for h in range(LOCAL_HEADS)
                ],
                axis=1,
            ).astype(ref.dtype)
            ref[at, rows : rows + half, 0:COLS] = folded[0:half]
            ref[at, rows : rows + half, COLS:] = folded[half:]
    for block in range(4):
        at = slice(block * slots, (block + 1) * slots)
        back = dot(packed[0, at, :], wall[0], 1, 1) + dot(packed[1, at, :], wall[1], 1, 1)
        if block == 0:
            own[...] = back
        elif block == 2:
            own_far[...] = back
        else:
            send[block // 2] = back.astype(BF16)
    keys = split_pairs(acc[2])
    values = split_pairs(acc[3])
    heads = [
        split_pairs(acc[0]),
        split_pairs(acc[1]),
        jnp.concatenate([keys[:, 0:COLS] + keys[:, COLS:], values[:, 0:COLS]], axis=1),
    ]
    norms = sums_one[...] + sums_two[...]
    for at in range(shards):
        mine = (sc[CHIP] == at).astype(F32)
        lo = at * rows
        lines = [line * mine for line in heads]
        for row in range(0, 6, 2):
            lines.append(
                jnp.concatenate(
                    [norms[row : row + 1, lo : lo + rows], norms[row + 1 : row + 2, lo : lo + rows]],
                    axis=1,
                )
            )
        units = jnp.concatenate(
            [sums_up[0:1, t * width + lo : t * width + lo + rows] for t in range(2)], axis=1
        )
        side = sc[SIDE].astype(F32)
        lines += [units * (1.0 - side), units * side]
        keep_w[at, rows + half :, :] = jnp.concatenate(lines, axis=0)


def place_qkv_body(sc, p0, p1, p2, p3, others, qg, kg, vg, og, qb, *refs):
    vectors, (ub, held) = refs[:8], refs[8:]
    rows = kg.shape[0]
    half = rows // 2
    small = rows // 4
    lines = 0.0
    for core_rel in range(CORES):
        for rel in range(4):
            value = (p0, p1, p2, p3)[rel][...] if core_rel == 0 else others[rel]
            lines += value[rows + half : rows + half + 8, :].astype(F32)
            held[sc[CORE] ^ core_rel, sc[CHIP] ^ rel] = value
    for core in range(CORES):
        for chip in range(CHIPS):
            piece = held[core, chip].astype(F32)
            lo = chip * COLS
            for which in range(2):
                qg[2 * core + which, :, lo : lo + COLS] = jnp.concatenate(
                    [
                        piece[0:rows, h * PAIR + which * HEAD : h * PAIR + (which + 1) * HEAD]
                        for h in range(LOCAL_HEADS)
                    ],
                    axis=1,
                )
            ref = kg if core == 0 else vg
            ref[0:half, lo : lo + COLS] = piece[rows : rows + half, 0:COLS]
            ref[half:, lo : lo + COLS] = piece[rows : rows + half, COLS:]
            og[chip * small : (chip + 1) * small, core * 2 * COLS : (core + 1) * 2 * COLS] = piece[
                rows + half + 8 :, :
            ]
    for which in range(4):
        qb[which : which + 1, :] = lines[
            which // 2 : which // 2 + 1, (which % 2) * COLS : (which % 2 + 1) * COLS
        ]
    for index, ref in enumerate(vectors):
        ref[...] = lines[2 + index // 2, (index % 2) * rows : (index % 2 + 1) * rows]
    ub[...] = jnp.concatenate([lines[6], lines[7]], axis=0)


def place_mlp_body(sc, p0, p1, p2, p3, others, ug, dg, held):
    rows, ff = ug.shape
    part = ff // 4
    side = part // 2
    unit = side // 2
    for core_rel in range(CORES):
        for rel in range(4):
            value = (p0, p1, p2, p3)[rel][...] if core_rel == 0 else others[rel]
            held[sc[CORE] ^ core_rel, sc[CHIP] ^ rel] = value
    for chip in range(CHIPS):
        lo = (chip & 1) * side + (chip >> 1) * unit
        piece = held[0, chip].astype(F32)
        for shard in range(4):
            at = shard * part + lo
            ug[:, at : at + unit] = piece[:, shard * unit : (shard + 1) * unit]
        dg[lo : lo + unit, :] = held[1, chip].astype(F32)


def local(
    shards,
    lanes,
    hidden,
    lengths,
    row_types,
    query_weight,
    query_bias,
    key_weight,
    key_bias,
    value_weight,
    value_bias,
    out_weight,
    out_bias,
    norm1_gain,
    norm1_bias,
    up_weight,
    up_bias,
    down_weight,
    down_bias,
    norm2_gain,
    norm2_bias,
    cotangent,
):
    groups = lanes // (CHIPS * CORES)
    shard = lax.axis_index("shard")
    lane = lax.axis_index("ctx")
    core, chip, group = lane & 1, (lane >> 1) & 3, lane >> 3
    chip_x, chip_y = chip & 1, chip >> 1
    spot = chip_y * 2 + core
    scalars = jnp.stack([shard, chip, core, spot, chip_x, chip_y, chip_x * 2 + core]).astype(jnp.int32)
    sets = [[g * 8 + i for g in range(groups)] for i in range(8)]

    def across(value, mask, name):
        with jax.named_scope(f"{name}_{mask}"):
            return lax.ppermute(value, "ctx", [(i, i ^ mask) for i in range(lanes)])

    def chips(value, rel, name):
        return across(value, rel << 1, name)

    def turn(value, shift, name):
        with jax.named_scope(f"{name}_z{shift}"):
            return lax.ppermute(value, "shard", [(i, i ^ shift) for i in range(shards)])

    def first_two(value, name):
        far = turn(value, 2, name)
        far, near = lax.optimization_barrier((far, turn(value, 1, name)))
        return [near, far]

    def collect(pair, name):
        return pair + [turn(pair[1], 1, name)]

    def reduce(parts, name):
        _, near, far, last = parts
        last = turn(last, 1, name)
        far = run(relay_body, "relay", sds(far.shape, BF16), scalars, far, last)
        near = turn(after(near, far), 1, name)
        return [near, turn(far, 2, name)], far

    def after(value, *others):
        return lax.optimization_barrier((value,) + others)[0]

    width = hidden.shape[2]
    slots = hidden.shape[1]
    rows = width // shards
    ff = up_weight.shape[1]
    part = ff // shards
    side = part // 2
    hid = hidden[0]
    cot = cotangent[0]
    small_rows = 8
    main = rows + rows // 2

    mine, other_mine = run(
        prep_qkv_body,
        "prep_qkv",
        [sds((main + small_rows + rows // 2, WIDE), BF16), sds((main, WIDE), BF16)],
        scalars,
        query_weight, key_weight, value_weight, out_weight, query_bias,
        key_bias, value_bias, out_bias, norm1_gain, norm1_bias,
        down_bias, norm2_gain, norm2_bias, up_bias,
        vmem=60,
    )
    own_w = collect(first_two(mine, "qkvw"), "qkvw")
    quarter = rows // 4
    mlp_one = run(
        prep_mlp_body,
        "prep_mlp",
        sds((2 * quarter + side // 4, width), BF16),
        scalars,
        after(lax.dynamic_slice_in_dim(up_weight, spot * quarter, quarter, 0), own_w[1]),
        lax.dynamic_slice_in_dim(down_weight, chip_x * side + spot * (side // 4), side // 4, 0),
    )
    own_x = jnp.stack([hid] + [chips(hid, rel, "hid") for rel in range(1, 4)])
    mlp_z = collect(first_two(mlp_one, "mlpw"), "mlpw")
    other_x = across(own_x, 1, "hid")
    other_w = [across(after(piece, other_x), 1, "qkvw") for piece in own_w]

    kinds = row_types.reshape(-1, slots)
    blocks = [group * 8 + (chip ^ rel) * 2 + (core ^ c) for c in range(CORES) for rel in range(4)]
    places = jnp.arange(slots, dtype=jnp.int32)
    word = jnp.concatenate([lax.dynamic_slice_in_dim(kinds, b, 1, 0) for b in blocks], axis=0)
    starts = jnp.stack(blocks)[:, None] * slots
    live = (starts + places[None, :] < lengths[0]).astype(F32)
    meta = jnp.concatenate([(word == 0).astype(F32), live], axis=0)

    wall, pq, pk, vv, vecs, up_shift, out_own, out_other = run(
        partial(qkv_body, shards),
        "qkv",
        [
            sds((2, width, 2 * WIDE), BF16),
            sds((4 * slots, WIDE), BF16),
            sds((8 * slots, WIDE), BF16),
            sds((8 * slots, WIDE), BF16),
            sds((8, width), F32),
            sds((1, ff // 2), F32),
            sds((shards - 1, quarter, width), BF16),
            sds((shards - 1, quarter, width), BF16),
        ],
        scalars,
        meta, mine, other_mine, own_x, other_x, *own_w, *other_w,
        scratch=[pltpu.VMEM((shards, small_rows, WIDE), F32)],
    )
    out_far = chips(out_own, 1, "outw")
    valid = live.reshape(1, 8 * slots)
    if groups > 1:
        gather = partial(lax.all_gather, axis_name="ctx", axis_index_groups=sets, tiled=True)
        pk, vv = gather(pk, axis=0), gather(vv, axis=0)
        valid = gather(valid, axis=1)
    mlp_far = [across(piece, 4, "mlpw") for piece in mlp_z]
    mlp_core = [across(piece, 1, "mlpw") for piece in mlp_z[:2]]
    probs, cx = attend(after(pq, mlp_core), pk, vv, valid, slots)
    cx = after(cx, out_far, mlp_far[0])
    cxs = [cx[0]] + [chips(cx[rel], rel, "cx") for rel in range(1, 4)]
    mlp_core += [across(piece, 1, "mlpw") for piece in [mlp_z[2]] + mlp_far[:2]]
    cxs = after(cxs, mlp_core)
    *cxs, out_far = lax.optimization_barrier((*cxs, out_far))
    wo = run(
        partial(assemble_out_body, shards),
        "assemble_out",
        sds((width, width), BF16),
        scalars,
        out_weight, out_own, out_other, out_far, across(out_far, 1, "outw"),
    )
    low_one, unit_one, rate_one = run(
        norm_one_body,
        "norm_one",
        [sds((slots, width), BF16), sds((slots, width), F32), sds((slots, 128), F32)],
        scalars,
        vecs, *cxs, wo, hid,
    )
    low_two = chips(low_one, 1, "mlpx")
    far_one = across(low_one, 4, "mlpy_x1")
    far_two = across(low_two, 4, "mlpy_x2")
    mlp_core.append(across(after(mlp_far[2], low_two), 1, "mlpw"))
    pieces = mlp_z + mlp_far
    wup, wdn = run(
        partial(assemble_mlp_body, shards),
        "assemble_mlp",
        [sds((width, ff // 2), BF16), sds((ff // 2, width), BF16)],
        scalars,
        up_weight, down_weight, *pieces, *mlp_core,
    )

    act, act_send, slope, own, send = run(
        partial(mlp_body, 384),
        "mlp",
        [
            sds((2 * slots, ff // 4), BF16),
            sds((2 * slots, ff // 4), BF16),
            sds((2 * slots, ff // 2), F32),
            sds((slots, width), F32),
            sds((slots, width), BF16),
        ],
        scalars,
        up_shift, low_one, low_two, wup, wdn,
    )
    received, far_one, far_two = lax.optimization_barrier(
        (chips(send, 1, "mlpp"), far_one, far_two)
    )
    act_far = across(act_send, 4, "mlpy_a")
    output, gs, gs_low, sums_two = run(
        norm_two_body,
        "norm_two",
        [
            sds((slots, width), BF16),
            sds((slots, width), F32),
            sds((slots, width), BF16),
            sds((8, width), F32),
        ],
        scalars,
        vecs, meta, own, received, unit_one, cot,
    )
    gs_other, gs_far_one, act_far = lax.optimization_barrier(
        (chips(gs_low, 1, "mlpg"), across(gs_low, 4, "mlpy_g1"), act_far)
    )
    low_keep, low_send, sums_up, own, send = run(
        partial(mlp_back_body, 384),
        "mlp_back",
        [
            sds((2 * slots, ff // 4), BF16),
            sds((2 * slots, ff // 4), BF16),
            sds((8, ff // 2), F32),
            sds((slots, width), F32),
            sds((slots, width), BF16),
        ],
        scalars,
        gs_low, gs_other, slope, wup, wdn,
    )
    received = chips(send, 1, "mlpb")
    gs_far_two = chips(after(gs_far_one, received), 1, "mlpy_g2")
    low_far = across(low_send, 4, "mlpy_l")
    gf, gf_low, gcx, sums_one = run(
        norm_one_back_body,
        "norm_one_back",
        [
            sds((slots, width), F32),
            sds((slots, width), BF16),
            sds((4, slots // 2, 2 * COLS), BF16),
            sds((8, width), F32),
        ],
        scalars,
        vecs, own, received, gs, unit_one, rate_one, wo,
    )
    gcs = [gcx[0]] + [chips(gcx[rel], rel, "gcx") for rel in range(1, 4)]
    keep_out, send_out = run(
        out_grads_body,
        "out_grads",
        [sds((CHIPS, COLS, width // 2), F32), sds((CHIPS, COLS, width // 2), BF16)],
        scalars,
        *cxs,
        gf_low,
    )
    keep_mlp, send_mlp = run(
        partial(mlp_grads_body, shards),
        "mlp_grads",
        [sds((shards, rows, width), F32), sds((shards, rows, width), BF16)],
        scalars,
        low_one, low_two, far_one, far_two, gs_low, gs_other, gs_far_one, gs_far_two,
        act, act_far, after(low_keep, send_out), low_far,
    )

    kind = BF16 if groups == 1 else F32

    def spread(low, name, late=()):
        if groups > 1:
            low = lax.psum(low, "ctx", axis_index_groups=sets).astype(BF16)
        here = [low] + [chips(low, rel, name) for rel in range(1, 4)]
        return here + [across(after(jnp.stack(here), *late), 1, name)]

    def fan(size):
        return [sds(size, F32), sds(size, BF16), sds(size, F32), sds(size, BF16)]

    mlp_parts = run(
        partial(fan_body, shards),
        "fan_mlp",
        fan((rows, width)),
        scalars,
        keep_mlp,
        across(send_mlp, 1, "gm"),
    )
    out_parts = run(
        out_fan_body,
        "fan_out",
        [sds((CHIPS, quarter, width // 2), F32)] + [sds((CHIPS, quarter, width // 2), BF16)] * 3,
        scalars,
        keep_out,
        across(send_out, 1, "go"),
    )
    gcs, _, (out_own, *out_sends) = lax.optimization_barrier((gcs, mlp_parts[1], out_parts))
    if groups == 1:
        dq, dk_own, dv_own, dkv = attend_back(gcs, pq, pk, vv, probs, slots, True)
    else:
        count = 4 * slots
        scatter = partial(lax.psum_scatter, axis_name="ctx", axis_index_groups=sets, tiled=True)
        dq, dk, dv = attend_back(gcs, pq, pk, vv, probs, slots, False)
        dk, dv = scatter(dk), scatter(dv)
        dk_own, dv_own = dk[:count], dv[:count]
        dkv = jnp.stack([dk[count:], dv[count:]]).astype(BF16)
    planes = run(
        plane_sum_body,
        "plane_out",
        sds((shards, quarter, width // 2), F32),
        scalars,
        after(out_own, dq),
        *[chips(out_sends[rel - 1], rel, "go") for rel in range(1, 4)],
    )
    gm_far = run(
        relay_halves_body,
        "relay_mlp",
        [sds((rows // 2, width), BF16)] * 2,
        scalars,
        mlp_parts[2],
        after(turn(mlp_parts[3], 1, "gm"), dq),
    )
    gm_near = turn(mlp_parts[1], 1, "gm")
    dkv_rec = across(after(dkv, planes, gm_far, gm_near), 1, "dkv")
    gm_far = [turn(value, 2, "gm") for value in gm_far]
    own, own_far, send, keep_w, send_w = run(
        partial(qkv_grads_body, shards),
        "qkv_grads",
        [
            sds((slots, width), F32),
            sds((slots, width), F32),
            sds((2, slots, width), BF16),
            sds((shards, main + small_rows, WIDE), F32),
            sds((shards, main, WIDE), BF16),
        ],
        scalars,
        meta, dq, dk_own, dv_own, dkv_rec, wall, sums_one, sums_two, sums_up, own_x,
        scratch=[pltpu.VMEM((2, 4 * slots, 2 * WIDE), BF16)],
    )
    size = main + small_rows + quarter
    qkv_parts = run(
        partial(qkv_fan_body, shards),
        "fan_qkv",
        fan((size, WIDE)),
        scalars,
        keep_w,
        across(after(send_w, gm_far[0]), 1, "gq"),
        planes,
    )
    qkv_recs, gq_far = reduce(qkv_parts, "gq")

    near = chips(send, 1, "ig")
    far = run(
        relay_second_body, "relay_ig", sds((slots, width), BF16), scalars, own_far, near
    )
    input_grad = run(
        input_grad_body,
        "input_grad",
        sds((slots, width), F32),
        scalars,
        gf, own, near, chips(far, 2, "ig"),
    )

    mlp_recs = after([gm_near] + gm_far, gq_far, far)
    low = run(
        sum_halves_body, "sum_mlp", sds((rows, width), kind), scalars, mlp_parts[0], *mlp_recs
    )
    done_mlp = spread(low, "gm", (input_grad, qkv_recs))
    ug, dg = run(
        place_mlp_body,
        "place_mlp",
        [sds((rows, ff), F32), sds((part, width), F32)],
        scalars,
        *done_mlp,
        scratch=[pltpu.VMEM((CORES, CHIPS, rows, width), BF16)],
    )
    low = run(
        gather_sum_body, "sum_qkv", sds((size, WIDE), kind), scalars, qkv_parts[0], *qkv_recs
    )
    done_qkv = spread(low, "gq")

    vec = sds((rows,), F32)
    qg, kg, vg, og, qbg, kbg, vbg, obg, g1g, b1g, dbg, g2g, b2g, ubg = run(
        place_qkv_body,
        "place_qkv",
        [
            sds((4, rows, width), F32), sds((rows, width), F32), sds((rows, width), F32),
            sds((rows, width), F32), sds((4, rows), F32), vec, vec, vec, vec, vec, vec, vec, vec,
            sds((4 * rows,), F32),
        ],
        scalars,
        *done_qkv,
        scratch=[pltpu.VMEM((CORES, CHIPS, size, WIDE), BF16)],
    )
    return (
        output[None], input_grad[None], qg, qbg, kg, kbg, vg, vbg, og, obg,
        g1g, b1g, ug, ubg, dg, dbg, g2g, b2g,
    )


def solution(mesh):
    vec, mat = P("shard"), P("shard", None)
    tokens = P("shard", "ctx", None)
    placed = (
        tokens, vec, mat, P(None, "shard", None), P(None, "shard"), mat, vec, mat, vec, mat,
        vec, vec, vec, mat, vec, mat, vec, vec, vec, tokens,
    )
    result = (
        tokens, tokens, P(None, "shard", None), P(None, "shard"), mat, vec, mat, vec, mat, vec,
        vec, vec, mat, vec, mat, vec, vec, vec,
    )
    return jax.shard_map(
        partial(local, mesh.shape["shard"], mesh.shape["ctx"]),
        mesh=mesh,
        in_specs=placed,
        out_specs=result,
        check_vma=False,
    )
```

```python
from functools import partial

import jax
import jax.numpy as jnp
from jax import lax
from jax.experimental import pallas as pl
from jax.experimental.pallas import tpu as pltpu
from jax.sharding import PartitionSpec as P

HEADS = 12
HEAD = 64
CHIPS = 4
CORES = 2
LOCAL_HEADS = HEADS // CHIPS
COLS = LOCAL_HEADS * HEAD
PAIR = 2 * HEAD
WIDE = LOCAL_HEADS * PAIR

EPS = 1e-12
SCALE = 0.125
NEG = -1000000000.0
F32 = jnp.float32
BF16 = jnp.bfloat16

SMEM = pl.BlockSpec(memory_space=pltpu.SMEM)
VMEM = pl.BlockSpec(memory_space=pltpu.VMEM)


def sds(shape, dtype):
    return jax.ShapeDtypeStruct(shape, dtype)


def dot(left, right, over_left, over_right):
    return lax.dot_general(
        left, right, (((over_left,), (over_right,)), ((), ())), preferred_element_type=F32
    )


def cost(micros):
    return pl.CostEstimate(flops=1, bytes_accessed=int(micros * 3e6), transcendentals=0)


MICROS = {
    "mlp": 3.5, "mlp_back": 3.5, "mlp_grads": 3.3, "out_grads": 2, "qkv_grads": 5,
    "place_qkv": 3.5, "place_mlp": 3,
}


def run(body, name, outs, scalars, *arrays, scratch=(), flops=0, vmem=24):
    many = isinstance(outs, (list, tuple))
    return pl.pallas_call(
        body,
        out_shape=outs,
        in_specs=[SMEM] + [VMEM] * len(arrays),
        out_specs=[VMEM] * len(outs) if many else VMEM,
        scratch_shapes=list(scratch),
        name=name,
        cost_estimate=cost(MICROS.get(name, 1)),
        compiler_params=pltpu.CompilerParams(vmem_limit_bytes=vmem << 20),
    )(scalars, *arrays)


SHARD, CHIP, CORE, SPOT, SIDE, TALL, PLACE = range(7)


def prep_qkv_body(sc, qw, kw, vw, ow, qb, *refs):
    vectors, (ub, own, other) = refs[:8], refs[8:]
    rows = kw.shape[0]
    half = rows // 2
    wide = [ref[...].astype(F32).reshape(1, rows) for ref in vectors]
    queries = qb[...].astype(F32)
    long = ub[...].astype(F32).reshape(1, 4 * rows)
    lines = [jnp.concatenate([queries[i : i + 1], queries[i + 1 : i + 2]], axis=1) for i in (0, 2)]
    lines += [jnp.concatenate(wide[i : i + 2], axis=1) for i in range(0, 8, 2)]
    lines += [long[:, 0 : 2 * rows], long[:, 2 * rows :]]
    small = jnp.concatenate(lines, axis=0).astype(BF16)
    end = rows + half + small.shape[0]
    own[rows + half : end, :] = small
    third = ow[pl.ds(pl.multiple_of(sc[PLACE] * (rows // 4), rows // 4), rows // 4), :]
    own[end : end + rows // 4, :] = third[:, 0:WIDE]
    own[end + rows // 4 :, :] = third[:, WIDE:]
    for chip in range(CHIPS):
        for core in range(CORES):

            @pl.when((sc[CHIP] == chip) & (sc[CORE] == core))
            def _():
                lo = chip * COLS
                for out, group in ((own, core), (other, 1 - core)):
                    first = qw[2 * group, :, lo : lo + COLS]
                    second = qw[2 * group + 1, :, lo : lo + COLS]
                    mix = []
                    for h in range(LOCAL_HEADS):
                        mix += [
                            first[:, h * HEAD : (h + 1) * HEAD],
                            second[:, h * HEAD : (h + 1) * HEAD],
                        ]
                    out[0:rows, :] = jnp.concatenate(mix, axis=1)
                    src = vw if group else kw
                    out[rows : rows + half, 0:COLS] = src[0:half, lo : lo + COLS]
                    out[rows : rows + half, COLS:] = src[half:rows, lo : lo + COLS]


def prep_mlp_body(sc, up, down, out):
    rows, ff = up.shape
    part = ff // 4
    side = part // 2
    unit = side // 2
    for chip_x in range(2):

        @pl.when(sc[SIDE] == chip_x)
        def _():
            for tall in range(2):
                for piece in range(4):
                    lo = piece * part + chip_x * side + tall * unit
                    out[tall * rows : (tall + 1) * rows, piece * unit : (piece + 1) * unit] = up[
                        :, lo : lo + unit
                    ]

    out[2 * rows :, :] = down[...]


def assemble_out_body(shards, sc, whole, own, other, own_far, other_far, wo):
    rows = wo.shape[0] // shards
    small = rows // 4
    wo[pl.ds(pl.multiple_of(sc[SHARD] * rows, rows), rows), :] = whole[...]
    for rel, ref in enumerate((own, other, own_far, other_far)):
        for shift in range(1, shards):
            owner = sc[SHARD] ^ shift
            at = pl.multiple_of(owner * rows + (sc[PLACE] ^ rel) * small, small)
            wo[pl.ds(at, small), :] = ref[shift - 1]


def assemble_mlp_body(shards, sc, up, down, *refs):
    pieces, (wup, wdn) = refs[:-2], refs[-2:]
    rows = wup.shape[0] // shards
    part = wdn.shape[0] // shards
    width = wdn.shape[1]
    unit = part // 2
    small = rows // 4
    at = pl.multiple_of(sc[SHARD] * rows, rows)
    for chip_x in range(2):

        @pl.when(sc[SIDE] == chip_x)
        def _():
            for tall in range(2):
                for piece in range(4):
                    lo = piece * 2 * part + chip_x * part + tall * unit
                    to = tall * width + piece * unit
                    wup[pl.ds(at, rows), to : to + unit] = up[:, lo : lo + unit]

    for tall in range(2):
        at = pl.multiple_of(tall * width + sc[SHARD] * unit, unit)
        lo = pl.multiple_of(sc[SIDE] * part + tall * unit, unit)
        wdn[pl.ds(at, unit), :] = down[pl.ds(lo, unit), :]
    for index, ref in enumerate(pieces):
        rel, shift = index // (shards - 1), index % (shards - 1) + 1
        spot = sc[SPOT] ^ (rel // 2 + rel % 2 * 2)
        owner = sc[SHARD] ^ shift
        at = pl.multiple_of(owner * rows + spot * small, small)
        wup[pl.ds(at, small), 0:width] = ref[0:small, :]
        wup[pl.ds(at, small), width:] = ref[small : 2 * small, :]
        at = (spot // 2) * width + owner * unit + (spot % 2) * (unit // 2)
        at = pl.multiple_of(at, unit // 2)
        wdn[pl.ds(at, unit // 2), :] = ref[2 * small :, :]


def split_pairs(line):
    pieces = [
        jnp.concatenate(
            [line[:, h * PAIR + t * HEAD : h * PAIR + (t + 1) * HEAD] for h in range(LOCAL_HEADS)],
            axis=1,
        )
        for t in range(2)
    ]
    return jnp.concatenate(pieces, axis=1)


def join_pairs(left, right):
    mix = []
    for h in range(LOCAL_HEADS):
        mix += [left[:, h * HEAD : (h + 1) * HEAD], right[:, h * HEAD : (h + 1) * HEAD]]
    return jnp.concatenate(mix, axis=1)


def qkv_body(shards, sc, meta, mine, other_mine, own_x, other_x, *refs):
    own_w = [mine] + list(refs[: shards - 1])
    other_w = [other_mine] + list(refs[shards - 1 : 2 * shards - 2])
    wall, pq, pk, vv, vecs, upb, out_own, out_other, held = refs[2 * shards - 2 :]
    slots = own_x.shape[1]
    small = out_own.shape[1]
    width = wall.shape[1]
    rows = width // shards
    half = rows // 2
    unit = rows
    for which in range(CORES):
        group = sc[CORE] ^ which
        keep = (group == 0).astype(F32).astype(BF16)
        for shift in range(shards):
            ref = (other_w if which else own_w)[shift]
            if shift > 0:
                third = out_other if which else out_own
                end = ref.shape[0] - 2 * small
                third[shift - 1, :, 0:WIDE] = ref[end : end + small, :]
                third[shift - 1, :, WIDE:] = ref[end + small :, :]
            owner = sc[SHARD] ^ shift
            at = pl.multiple_of(owner * rows, half)
            wall[group, pl.ds(at, rows), 0:WIDE] = ref[0:rows, :]
            if which == 0:
                held[owner] = ref[rows + half : ref.shape[0] - 2 * small, :].astype(F32)
            for part in range(2):
                mix = []
                for h in range(LOCAL_HEADS):
                    lo = part * COLS + h * HEAD
                    one = ref[rows : rows + half, lo : lo + HEAD]
                    mix += [one, one * keep]
                low = pl.multiple_of(owner * rows + part * half, half)
                wall[group, pl.ds(low, half), WIDE:] = jnp.concatenate(mix, axis=1)
    vecs[...] = jnp.zeros_like(vecs)
    for shard in range(shards):
        lo = shard * rows
        for row in range(6):
            line = 3 + row // 2
            col = (row % 2) * rows
            vecs[row : row + 1, lo : lo + rows] = held[shard, line : line + 1, col : col + rows]
        for chip_x in range(2):

            @pl.when(sc[SIDE] == chip_x)
            def _():
                for tall in range(2):
                    to = tall * width + shard * unit
                    upb[0:1, to : to + unit] = held[
                        shard, 6 + chip_x : 7 + chip_x, tall * unit : (tall + 1) * unit
                    ]

    table = held[sc[CHIP]]
    bias = [join_pairs(table[i : i + 1, 0:COLS], table[i : i + 1, COLS:]) for i in range(2)]
    key_bias = join_pairs(table[2:3, 0:COLS], table[2:3, 0:COLS])
    value_bias = join_pairs(table[2:3, COLS:], jnp.zeros((1, COLS), F32))
    flags = meta[...].T
    lane = lax.broadcasted_iota(jnp.int32, (1, WIDE), 1)
    left = (lane % PAIR) < HEAD
    for block in range(8):
        tokens = (own_x if block < 4 else other_x)[block % 4]
        word = flags[:, block : block + 1] > 0
        at = slice(block * slots, (block + 1) * slots)
        if block < 4:
            first = dot(tokens, wall[0], 1, 0)
            second = dot(tokens, wall[1], 1, 0)
            query = jnp.where(word, first[:, 0:WIDE] + bias[0], second[:, 0:WIDE] + bias[1]) * SCALE
            pq[at, :] = query.astype(BF16)
            key, value = first[:, WIDE:], second[:, WIDE:]
        else:
            key = dot(tokens, wall[0, :, WIDE:], 1, 0)
            value = dot(tokens, wall[1, :, WIDE:], 1, 0)
        pk[at, :] = jnp.where(left == word, key + key_bias, 0.0).astype(BF16)
        vv[at, :] = (value + value_bias).astype(BF16)


def attend_body(step, pq, pk, vv, valid, probs, cx):
    head = pl.program_id(0)
    count = pq.shape[0]
    slots = count // 4
    keep = valid[...] > 0
    keys = pk[...]
    values = vv[...]
    for start in range(0, count, step):
        scores = dot(pq[start : start + step, :], keys, 1, 1)
        scores = jnp.where(keep, scores, NEG)
        top = jnp.max(scores, axis=-1, keepdims=True)
        expo = jnp.exp(scores - top)
        share = 1.0 / jnp.sum(expo, axis=-1, keepdims=True)
        low = (expo * share).astype(BF16)
        probs[0, start : start + step, :] = low
        mixed = dot(low, values, 1, 0)[:, 0:HEAD].astype(BF16)
        for h in range(LOCAL_HEADS):

            @pl.when(head == h)
            def _():
                for at in range(0, step, slots):
                    block = (start + at) // slots
                    mid = at + slots // 2
                    cx[block, :, h * HEAD : (h + 1) * HEAD] = mixed[at:mid]
                    cx[block, :, COLS + h * HEAD : COLS + (h + 1) * HEAD] = mixed[mid : at + slots]


def attend(pq, pk, vv, valid, slots):
    count, keys = pq.shape[0], pk.shape[0]
    step = 2 * slots if keys <= 2048 else slots
    limit = 14 if keys <= 2048 else 56
    return pl.pallas_call(
        partial(attend_body, step),
        grid=(LOCAL_HEADS,),
        in_specs=[
            pl.BlockSpec((count, PAIR), lambda h: (0, h)),
            pl.BlockSpec((keys, PAIR), lambda h: (0, h)),
            pl.BlockSpec((keys, PAIR), lambda h: (0, h)),
            pl.BlockSpec((1, keys), lambda h: (0, 0)),
        ],
        out_specs=[
            pl.BlockSpec((1, count, keys), lambda h: (h, 0, 0)),
            pl.BlockSpec((4, slots // 2, 2 * COLS), lambda h: (0, 0, 0)),
        ],
        out_shape=[
            sds((LOCAL_HEADS, count, keys), BF16),
            sds((4, slots // 2, 2 * COLS), BF16),
        ],
        name="attend",
        cost_estimate=cost(5.5),
        compiler_params=pltpu.CompilerParams(vmem_limit_bytes=limit << 20),
    )(pq, pk, vv, valid)


def attend_back_body(step, split, gc0, gc1, gc2, gc3, pq, pk, vv, probs, dq, *refs):
    head = pl.program_id(0)
    count = pq.shape[0]
    slots = count // 4
    half = slots // 2
    if split:
        dk_own, dv_own, dkv_other, gcs, dk, dv = refs
    else:
        dk, dv, gcs = refs

    @pl.when(head == 0)
    def _():
        gcs[...] = jnp.zeros_like(gcs)
        for block, ref in enumerate((gc0, gc1, gc2, gc3)):
            for h in range(LOCAL_HEADS):
                lo = block * slots
                gcs[h, lo : lo + half, 0:HEAD] = ref[:, h * HEAD : (h + 1) * HEAD]
                gcs[h, lo + half : lo + slots, 0:HEAD] = ref[
                    :, COLS + h * HEAD : COLS + (h + 1) * HEAD
                ]

    keys = pk[...]
    values = vv[...]
    for start in range(0, count, step):
        grad = gcs[head, start : start + step, :]
        low = probs[0, start : start + step, :]
        wide = low.astype(F32)
        moved = dot(grad, values, 1, 1)
        inner = jnp.sum(wide * moved, axis=-1, keepdims=True)
        ds = (wide * (moved - inner)).astype(BF16)
        query = pq[start : start + step, :]
        dq[start : start + step, :] = dot(ds, keys, 1, 0)
        key_part = dot(ds, query, 0, 0)
        value_part = dot(low, grad, 0, 0)
        if start == 0:
            dk[...] = key_part
            dv[...] = value_part
        else:
            dk[...] += key_part
            dv[...] += value_part
    if split:
        dk_own[...] = dk[0:count, :]
        dv_own[...] = dv[0:count, :]
        dkv_other[0] = dk[count:, :].astype(BF16)
        dkv_other[1] = dv[count:, :].astype(BF16)


def attend_back(pieces, pq, pk, vv, probs, slots, split):
    count, keys = pq.shape[0], pk.shape[0]
    step = 2 * slots if keys <= 2048 else slots
    limit = 20 if keys <= 2048 else 58
    piece = pl.BlockSpec((slots // 2, 2 * COLS), lambda h: (0, 0))
    rows = pl.BlockSpec((count, PAIR), lambda h: (0, h))
    cols = pl.BlockSpec((keys, PAIR), lambda h: (0, h))
    scratch = [pltpu.VMEM((LOCAL_HEADS, count, PAIR), BF16)]
    if split:
        specs = [rows, rows, rows, pl.BlockSpec((2, count, PAIR), lambda h: (0, 0, h))]
        shapes = [sds((count, WIDE), F32)] * 3 + [sds((2, count, WIDE), BF16)]
        scratch += [pltpu.VMEM((keys, PAIR), F32), pltpu.VMEM((keys, PAIR), F32)]
    else:
        specs = [rows, cols, cols]
        shapes = [sds((count, WIDE), F32), sds((keys, WIDE), F32), sds((keys, WIDE), F32)]
    return pl.pallas_call(
        partial(attend_back_body, step, split),
        grid=(LOCAL_HEADS,),
        in_specs=[piece] * 4
        + [rows, cols, cols, pl.BlockSpec((1, count, keys), lambda h: (h, 0, 0))],
        out_specs=specs,
        out_shape=shapes,
        scratch_shapes=scratch,
        name="attend_back",
        cost_estimate=cost(6),
        compiler_params=pltpu.CompilerParams(vmem_limit_bytes=limit << 20),
    )(*pieces, pq, pk, vv, probs)


def unpack(piece):
    return jnp.concatenate([piece[:, 0:COLS], piece[:, COLS:]], axis=0)


def normalize(summed):
    center = summed - jnp.mean(summed, axis=-1, keepdims=True)
    spread = jnp.mean(center * center, axis=-1, keepdims=True)
    rate = lax.rsqrt(spread + EPS)
    return center * rate, rate


def norm_back(grad, unit, rate, gain):
    scaled = grad * gain
    mean_one = jnp.mean(scaled, axis=-1, keepdims=True)
    mean_two = jnp.mean(scaled * unit, axis=-1, keepdims=True)
    return rate * (scaled - mean_one - unit * mean_two)


def total(values):
    return jnp.sum(values, axis=0, keepdims=True)


OUT_B, GAIN_1, SHIFT_1, DOWN_B, GAIN_2, SHIFT_2 = range(6)


def norm_one_body(sc, vecs, cx0, cx1, cx2, cx3, wo, hidden, low, unit_out, rate_out):
    acc = hidden[...].astype(F32) + vecs[OUT_B : OUT_B + 1, :]
    for rel, ref in enumerate((cx0, cx1, cx2, cx3)):
        at = pl.multiple_of((sc[CHIP] ^ rel) * COLS, COLS)
        acc += dot(unpack(ref[...]), wo[pl.ds(at, COLS), :], 1, 0)
    unit, rate = normalize(acc)
    first = unit * vecs[GAIN_1 : GAIN_1 + 1, :] + vecs[SHIFT_1 : SHIFT_1 + 1, :]
    low[...] = first.astype(BF16)
    unit_out[...] = unit
    rate_out[...] = jnp.broadcast_to(rate, rate_out.shape)


def mlp_body(chunk, sc, bias, x0, x1, wup, wdn, act, act_send, slope, own, send):
    slots = x0.shape[0]
    width = x0.shape[1]
    tokens = jnp.concatenate([x0[...], x1[...]], axis=0)
    acc = None
    for lo in range(0, wup.shape[1], chunk):
        pre = dot(tokens, wup[:, lo : lo + chunk], 1, 0) + bias[0:1, lo : lo + chunk]
        cdf = 0.5 * (1.0 + lax.erf(pre * 0.7071067811865476))
        pdf = jnp.exp(-0.5 * pre * pre) * 0.3989422804014327
        out = (pre * cdf).astype(BF16)
        slope[:, lo : lo + chunk] = cdf + pre * pdf
        to_quarter(sc, out, lo, width, act, act_send)
        part = dot(out, wdn[lo : lo + chunk, :], 1, 0)
        acc = part if acc is None else acc + part
    own[...] = acc[0:slots]
    send[...] = acc[slots:].astype(BF16)


def to_quarter(sc, values, lo, width, keep, send):
    tall, at = lo // width, lo % width

    @pl.when(sc[TALL] == tall)
    def _():
        keep[:, at : at + values.shape[1]] = values

    @pl.when(sc[TALL] != tall)
    def _():
        send[:, at : at + values.shape[1]] = values


def norm_two_body(sc, vecs, meta, own, received, unit_one, cotangent, output, gs, gs_low, sums):
    valid = meta[...].T[:, 8:9]
    first = unit_one[...] * vecs[GAIN_1 : GAIN_1 + 1, :] + vecs[SHIFT_1 : SHIFT_1 + 1, :]
    acc = own[...] + received[...].astype(F32) + vecs[DOWN_B : DOWN_B + 1, :] + first
    unit, rate = normalize(acc)
    gain = vecs[GAIN_2 : GAIN_2 + 1, :]
    output[...] = ((unit * gain + vecs[SHIFT_2 : SHIFT_2 + 1, :]) * valid).astype(BF16)
    grad = cotangent[...].astype(F32) * valid
    back = norm_back(grad, unit, rate, gain)
    gs[...] = back
    gs_low[...] = back.astype(BF16)
    sums[...] = jnp.zeros_like(sums)
    sums[DOWN_B : DOWN_B + 1, :] = total(back)
    sums[GAIN_2 : GAIN_2 + 1, :] = total(grad * unit)
    sums[SHIFT_2 : SHIFT_2 + 1, :] = total(grad)


def mlp_back_body(chunk, sc, g0, g1, slope, wup, wdn, low_keep, low_send, sums, own, send):
    slots = g0.shape[0]
    width = g0.shape[1]
    grads = jnp.concatenate([g0[...], g1[...]], axis=0)
    acc = None
    sums[...] = jnp.zeros_like(sums)
    for lo in range(0, wup.shape[1], chunk):
        pre = dot(grads, wdn[lo : lo + chunk, :], 1, 1) * slope[:, lo : lo + chunk]
        sums[0:1, lo : lo + chunk] = total(pre)
        low = pre.astype(BF16)
        to_quarter(sc, low, lo, width, low_keep, low_send)
        part = dot(low, wup[:, lo : lo + chunk], 1, 1)
        acc = part if acc is None else acc + part
    own[...] = acc[0:slots]
    send[...] = acc[slots:].astype(BF16)


def mlp_grads_body(
    shards, sc, x0, x1, x2, x3, g0, g1, g2, g3, act, act_r, low, low_r, keep, send
):
    tokens = jnp.concatenate([x0[...], x1[...], x2[...], x3[...]], axis=0)
    grads = jnp.concatenate([g0[...], g1[...], g2[...], g3[...]], axis=0)
    hidden = jnp.concatenate([act[...], act_r[...]], axis=0)
    back = jnp.concatenate([low[...], low_r[...]], axis=0)
    rows = tokens.shape[1] // shards
    for at in range(shards):
        lo = at * rows
        up = dot(tokens[:, lo : lo + rows], back, 0, 0)
        down = dot(hidden[:, lo : lo + rows], grads, 0, 0)

        @pl.when(sc[CORE] == 0)
        def _():
            keep[at] = up
            send[at] = down.astype(BF16)

        @pl.when(sc[CORE] == 1)
        def _():
            keep[at] = down
            send[at] = up.astype(BF16)


def fan_body(shards, sc, keep, received, *outs):
    for shift in range(shards):
        at = sc[SHARD] ^ shift
        value = keep[at] + received[at].astype(F32)
        outs[shift][...] = value.astype(outs[shift].dtype)


def relay_body(sc, value, received, out):
    out[...] = (value[...] + received[...].astype(F32)).astype(BF16)


def relay_halves_body(sc, value, received, one, two):
    half = one.shape[0]
    one[...] = (value[0:half, :] + received[0:half, :].astype(F32)).astype(BF16)
    two[...] = (value[half:, :] + received[half:, :].astype(F32)).astype(BF16)


def sum_halves_body(sc, own, near, one, two, out):
    half = one.shape[0]
    value = own[...] + near[...].astype(F32)
    out[0:half, :] = (value[0:half] + one[...].astype(F32)).astype(out.dtype)
    out[half:, :] = (value[half:] + two[...].astype(F32)).astype(out.dtype)


def relay_second_body(sc, value, received, out):
    out[...] = (value[...] + received[1].astype(F32)).astype(BF16)


def qkv_fan_body(shards, sc, keep, received, planes, *outs):
    main = received.shape[1]
    small, half = planes.shape[1:]
    end = keep.shape[1]
    for shift in range(shards):
        at = sc[SHARD] ^ shift
        ref = outs[shift]
        ref[0:main, :] = (keep[at, 0:main, :] + received[at].astype(F32)).astype(ref.dtype)
        ref[main:end, :] = keep[at, main:, :].astype(ref.dtype)
        ref[end:, :] = planes[at].astype(ref.dtype)


def gather_sum_body(sc, own, *refs):
    acc = own[...]
    for ref in refs[:-1]:
        acc += ref[...].astype(F32)
    refs[-1][...] = acc.astype(refs[-1].dtype)


def out_fan_body(sc, keep, received, own, *sends):
    small = own.shape[1]
    for rel in range(4):
        at = pl.multiple_of((sc[CHIP] ^ rel) * small, small)
        value = keep[:, pl.ds(at, small), :] + received[:, pl.ds(at, small), :].astype(F32)
        if rel == 0:
            own[...] = value
        else:
            sends[rel - 1][...] = value.astype(BF16)


def plane_sum_body(sc, own, r1, r2, r3, out):
    out[...] = own[...] + r1[...].astype(F32) + r2[...].astype(F32) + r3[...].astype(F32)


def input_grad_body(sc, base, own, near, far, out):
    out[...] = base[...] + own[...] + near[0].astype(F32) + far[...].astype(F32)


def norm_one_back_body(
    sc, vecs, own, received, gs, unit_one, rate_one, wo, gf, gf_low, gcx, sums
):
    grad = gs[...] + own[...] + received[...].astype(F32)
    unit = unit_one[...]
    rate = rate_one[:, 0:1]
    back = norm_back(grad, unit, rate, vecs[GAIN_1 : GAIN_1 + 1, :])
    gf[...] = back
    low = back.astype(BF16)
    gf_low[...] = low
    sums[...] = jnp.zeros_like(sums)
    sums[OUT_B : OUT_B + 1, :] = total(back)
    sums[GAIN_1 : GAIN_1 + 1, :] = total(grad * unit)
    sums[SHIFT_1 : SHIFT_1 + 1, :] = total(grad)
    half = back.shape[0] // 2
    for rel in range(4):
        at = pl.multiple_of((sc[CHIP] ^ rel) * COLS, COLS)
        part = dot(low, wo[pl.ds(at, COLS), :], 1, 1).astype(BF16)
        gcx[rel, :, 0:COLS] = part[0:half]
        gcx[rel, :, COLS:] = part[half:]


def out_grads_body(sc, cx0, cx1, cx2, cx3, gf_low, keep, send):
    low = gf_low[...]
    half = keep.shape[2]
    for rel, ref in enumerate((cx0, cx1, cx2, cx3)):
        block = dot(unpack(ref[...]), low, 0, 0)
        chip = sc[CHIP] ^ rel
        for core in range(CORES):

            @pl.when(sc[CORE] == core)
            def _():
                keep[chip] = block[:, core * half : (core + 1) * half]
                other = 1 - core
                send[chip] = block[:, other * half : (other + 1) * half].astype(BF16)


def qkv_grads_body(
    shards, sc, meta, dq, dk_own, dv_own, dkv_rec, wall, sums_one, sums_two, sums_up,
    x, own, own_far, send, keep_w, send_w, packed,
):
    slots = x.shape[1]
    flags = meta[...].T
    lane = lax.broadcasted_iota(jnp.int32, (1, WIDE), 1)
    left = (lane % PAIR) < HEAD
    width = wall.shape[1]
    rows = width // shards
    half = rows // 2
    acc = [0.0] * 4
    for block in range(4):
        at = slice(block * slots, (block + 1) * slots)
        word = flags[:, block : block + 1] > 0
        query = dq[at, :] * SCALE
        parts = (
            jnp.where(word, query, 0.0),
            jnp.where(word, 0.0, query),
            jnp.where(left == word, dk_own[at, :] + dkv_rec[0, at, :].astype(F32), 0.0),
            dv_own[at, :] + dkv_rec[1, at, :].astype(F32),
        )
        acc = [a + total(p) for a, p in zip(acc, parts)]
        packed[0, at, 0:WIDE] = parts[0].astype(BF16)
        packed[1, at, 0:WIDE] = parts[1].astype(BF16)
        packed[0, at, WIDE:] = parts[2].astype(BF16)
        packed[1, at, WIDE:] = parts[3].astype(BF16)
    tokens = jnp.concatenate([x[rel] for rel in range(4)], axis=0)
    for group_rel, ref in enumerate((keep_w, send_w)):
        group = sc[CORE] ^ group_rel
        for at in range(shards):
            grad = dot(tokens[:, at * rows : (at + 1) * rows], packed[group], 0, 0)
            ref[at, 0:rows, :] = grad[:, 0:WIDE].astype(ref.dtype)
            folded = jnp.concatenate(
                [
                    grad[:, WIDE + h * PAIR : WIDE + h * PAIR + HEAD]
                    + grad[:, WIDE + h * PAIR + HEAD : WIDE + (h + 1) * PAIR]
                    for h in range(LOCAL_HEADS)
                ],
                axis=1,
            ).astype(ref.dtype)
            ref[at, rows : rows + half, 0:COLS] = folded[0:half]
            ref[at, rows : rows + half, COLS:] = folded[half:]
    for block in range(4):
        at = slice(block * slots, (block + 1) * slots)
        back = dot(packed[0, at, :], wall[0], 1, 1) + dot(packed[1, at, :], wall[1], 1, 1)
        if block == 0:
            own[...] = back
        elif block == 2:
            own_far[...] = back
        else:
            send[block // 2] = back.astype(BF16)
    keys = split_pairs(acc[2])
    values = split_pairs(acc[3])
    heads = [
        split_pairs(acc[0]),
        split_pairs(acc[1]),
        jnp.concatenate([keys[:, 0:COLS] + keys[:, COLS:], values[:, 0:COLS]], axis=1),
    ]
    norms = sums_one[...] + sums_two[...]
    for at in range(shards):
        mine = (sc[CHIP] == at).astype(F32)
        lo = at * rows
        lines = [line * mine for line in heads]
        for row in range(0, 6, 2):
            lines.append(
                jnp.concatenate(
                    [norms[row : row + 1, lo : lo + rows], norms[row + 1 : row + 2, lo : lo + rows]],
                    axis=1,
                )
            )
        units = jnp.concatenate(
            [sums_up[0:1, t * width + lo : t * width + lo + rows] for t in range(2)], axis=1
        )
        side = sc[SIDE].astype(F32)
        lines += [units * (1.0 - side), units * side]
        keep_w[at, rows + half :, :] = jnp.concatenate(lines, axis=0)


def place_qkv_body(sc, p0, p1, p2, p3, others, qg, kg, vg, og, qb, *refs):
    vectors, (ub, held) = refs[:8], refs[8:]
    rows = kg.shape[0]
    half = rows // 2
    small = rows // 4
    lines = 0.0
    for core_rel in range(CORES):
        for rel in range(4):
            value = (p0, p1, p2, p3)[rel][...] if core_rel == 0 else others[rel]
            lines += value[rows + half : rows + half + 8, :].astype(F32)
            held[sc[CORE] ^ core_rel, sc[CHIP] ^ rel] = value
    for core in range(CORES):
        for chip in range(CHIPS):
            piece = held[core, chip].astype(F32)
            lo = chip * COLS
            for which in range(2):
                qg[2 * core + which, :, lo : lo + COLS] = jnp.concatenate(
                    [
                        piece[0:rows, h * PAIR + which * HEAD : h * PAIR + (which + 1) * HEAD]
                        for h in range(LOCAL_HEADS)
                    ],
                    axis=1,
                )
            ref = kg if core == 0 else vg
            ref[0:half, lo : lo + COLS] = piece[rows : rows + half, 0:COLS]
            ref[half:, lo : lo + COLS] = piece[rows : rows + half, COLS:]
            og[chip * small : (chip + 1) * small, core * 2 * COLS : (core + 1) * 2 * COLS] = piece[
                rows + half + 8 :, :
            ]
    for which in range(4):
        qb[which : which + 1, :] = lines[
            which // 2 : which // 2 + 1, (which % 2) * COLS : (which % 2 + 1) * COLS
        ]
    for index, ref in enumerate(vectors):
        ref[...] = lines[2 + index // 2, (index % 2) * rows : (index % 2 + 1) * rows]
    ub[...] = jnp.concatenate([lines[6], lines[7]], axis=0)


def place_mlp_body(sc, p0, p1, p2, p3, others, ug, dg, held):
    rows, ff = ug.shape
    part = ff // 4
    side = part // 2
    unit = side // 2
    for core_rel in range(CORES):
        for rel in range(4):
            value = (p0, p1, p2, p3)[rel][...] if core_rel == 0 else others[rel]
            held[sc[CORE] ^ core_rel, sc[CHIP] ^ rel] = value
    for chip in range(CHIPS):
        lo = (chip & 1) * side + (chip >> 1) * unit
        piece = held[0, chip].astype(F32)
        for shard in range(4):
            at = shard * part + lo
            ug[:, at : at + unit] = piece[:, shard * unit : (shard + 1) * unit]
        dg[lo : lo + unit, :] = held[1, chip].astype(F32)


def local(
    shards,
    lanes,
    hidden,
    lengths,
    row_types,
    query_weight,
    query_bias,
    key_weight,
    key_bias,
    value_weight,
    value_bias,
    out_weight,
    out_bias,
    norm1_gain,
    norm1_bias,
    up_weight,
    up_bias,
    down_weight,
    down_bias,
    norm2_gain,
    norm2_bias,
    cotangent,
):
    groups = lanes // (CHIPS * CORES)
    shard = lax.axis_index("shard")
    lane = lax.axis_index("ctx")
    core, chip, group = lane & 1, (lane >> 1) & 3, lane >> 3
    chip_x, chip_y = chip & 1, chip >> 1
    spot = chip_y * 2 + core
    scalars = jnp.stack([shard, chip, core, spot, chip_x, chip_y, chip_x * 2 + core]).astype(jnp.int32)
    sets = [[g * 8 + i for g in range(groups)] for i in range(8)]

    def across(value, mask, name):
        with jax.named_scope(f"{name}_{mask}"):
            return lax.ppermute(value, "ctx", [(i, i ^ mask) for i in range(lanes)])

    def chips(value, rel, name):
        return across(value, rel << 1, name)

    def turn(value, shift, name):
        with jax.named_scope(f"{name}_z{shift}"):
            return lax.ppermute(value, "shard", [(i, i ^ shift) for i in range(shards)])

    def first_two(value, name):
        far = turn(value, 2, name)
        far, near = lax.optimization_barrier((far, turn(value, 1, name)))
        return [near, far]

    def collect(pair, name):
        return pair + [turn(pair[1], 1, name)]

    def reduce(parts, name):
        _, near, far, last = parts
        last = turn(last, 1, name)
        far = run(relay_body, "relay", sds(far.shape, BF16), scalars, far, last)
        near = turn(after(near, far), 1, name)
        return [near, turn(far, 2, name)], far

    def after(value, *others):
        return lax.optimization_barrier((value,) + others)[0]

    width = hidden.shape[2]
    slots = hidden.shape[1]
    rows = width // shards
    ff = up_weight.shape[1]
    part = ff // shards
    side = part // 2
    hid = hidden[0]
    cot = cotangent[0]
    small_rows = 8
    main = rows + rows // 2

    mine, other_mine = run(
        prep_qkv_body,
        "prep_qkv",
        [sds((main + small_rows + rows // 2, WIDE), BF16), sds((main, WIDE), BF16)],
        scalars,
        query_weight, key_weight, value_weight, out_weight, query_bias,
        key_bias, value_bias, out_bias, norm1_gain, norm1_bias,
        down_bias, norm2_gain, norm2_bias, up_bias,
        vmem=60,
    )
    own_w = collect(first_two(mine, "qkvw"), "qkvw")
    quarter = rows // 4
    mlp_one = run(
        prep_mlp_body,
        "prep_mlp",
        sds((2 * quarter + side // 4, width), BF16),
        scalars,
        after(lax.dynamic_slice_in_dim(up_weight, spot * quarter, quarter, 0), own_w[1]),
        lax.dynamic_slice_in_dim(down_weight, chip_x * side + spot * (side // 4), side // 4, 0),
    )
    own_x = jnp.stack([hid] + [chips(hid, rel, "hid") for rel in range(1, 4)])
    mlp_pair = first_two(after(mlp_one, own_w[2]), "mlpw")
    other_x = across(own_x, 1, "hid")
    other_w = [across(after(piece, other_x), 1, "qkvw") for piece in own_w]

    kinds = row_types.reshape(-1, slots)
    blocks = [group * 8 + (chip ^ rel) * 2 + (core ^ c) for c in range(CORES) for rel in range(4)]
    places = jnp.arange(slots, dtype=jnp.int32)
    word = jnp.concatenate([lax.dynamic_slice_in_dim(kinds, b, 1, 0) for b in blocks], axis=0)
    starts = jnp.stack(blocks)[:, None] * slots
    live = (starts + places[None, :] < lengths[0]).astype(F32)
    meta = jnp.concatenate([(word == 0).astype(F32), live], axis=0)

    wall, pq, pk, vv, vecs, up_shift, out_own, out_other = run(
        partial(qkv_body, shards),
        "qkv",
        [
            sds((2, width, 2 * WIDE), BF16),
            sds((4 * slots, WIDE), BF16),
            sds((8 * slots, WIDE), BF16),
            sds((8 * slots, WIDE), BF16),
            sds((8, width), F32),
            sds((1, ff // 2), F32),
            sds((shards - 1, quarter, width), BF16),
            sds((shards - 1, quarter, width), BF16),
        ],
        scalars,
        meta, mine, other_mine, own_x, other_x, *own_w, *other_w,
        scratch=[pltpu.VMEM((shards, small_rows, WIDE), F32)],
    )
    out_far = chips(out_own, 1, "outw")
    valid = live.reshape(1, 8 * slots)
    if groups > 1:
        gather = partial(lax.all_gather, axis_name="ctx", axis_index_groups=sets, tiled=True)
        pk, vv = gather(pk, axis=0), gather(vv, axis=0)
        valid = gather(valid, axis=1)
    mlp_z = collect(after(mlp_pair, out_far), "mlpw")
    mlp_far = [across(piece, 4, "mlpw") for piece in mlp_z]
    probs, cx = attend(after(pq, mlp_z[:2]), pk, vv, valid, slots)
    cx = after(cx, mlp_far[0])
    mlp_core = [across(piece, 1, "mlpw") for piece in mlp_z[:2]]
    cxs = [cx[0]] + [chips(cx[rel], rel, "cx") for rel in range(1, 4)]
    mlp_core += [across(piece, 1, "mlpw") for piece in [mlp_z[2]] + mlp_far[:2]]
    cxs = after(cxs, mlp_far[1])
    *cxs, out_far = lax.optimization_barrier((*cxs, out_far))
    wo = run(
        partial(assemble_out_body, shards),
        "assemble_out",
        sds((width, width), BF16),
        scalars,
        out_weight, out_own, out_other, out_far, across(out_far, 1, "outw"),
    )
    low_one, unit_one, rate_one = run(
        norm_one_body,
        "norm_one",
        [sds((slots, width), BF16), sds((slots, width), F32), sds((slots, 128), F32)],
        scalars,
        vecs, *cxs, wo, hid,
    )
    low_two = chips(low_one, 1, "mlpx")
    far_one = across(low_one, 4, "mlpy_x1")
    far_two = across(low_two, 4, "mlpy_x2")
    mlp_core.append(across(after(mlp_far[2], low_two), 1, "mlpw"))
    pieces = mlp_z + mlp_far
    wup, wdn = run(
        partial(assemble_mlp_body, shards),
        "assemble_mlp",
        [sds((width, ff // 2), BF16), sds((ff // 2, width), BF16)],
        scalars,
        up_weight, down_weight, *pieces, *mlp_core,
    )

    act, act_send, slope, own, send = run(
        partial(mlp_body, 384),
        "mlp",
        [
            sds((2 * slots, ff // 4), BF16),
            sds((2 * slots, ff // 4), BF16),
            sds((2 * slots, ff // 2), F32),
            sds((slots, width), F32),
            sds((slots, width), BF16),
        ],
        scalars,
        up_shift, low_one, low_two, wup, wdn,
    )
    received, far_one, far_two = lax.optimization_barrier(
        (chips(send, 1, "mlpp"), far_one, far_two)
    )
    act_far = across(act_send, 4, "mlpy_a")
    output, gs, gs_low, sums_two = run(
        norm_two_body,
        "norm_two",
        [
            sds((slots, width), BF16),
            sds((slots, width), F32),
            sds((slots, width), BF16),
            sds((8, width), F32),
        ],
        scalars,
        vecs, meta, own, received, unit_one, cot,
    )
    gs_other, gs_far_one, act_far = lax.optimization_barrier(
        (chips(gs_low, 1, "mlpg"), across(gs_low, 4, "mlpy_g1"), act_far)
    )
    low_keep, low_send, sums_up, own, send = run(
        partial(mlp_back_body, 384),
        "mlp_back",
        [
            sds((2 * slots, ff // 4), BF16),
            sds((2 * slots, ff // 4), BF16),
            sds((8, ff // 2), F32),
            sds((slots, width), F32),
            sds((slots, width), BF16),
        ],
        scalars,
        gs_low, gs_other, slope, wup, wdn,
    )
    received = chips(send, 1, "mlpb")
    gs_far_two = chips(after(gs_far_one, received), 1, "mlpy_g2")
    low_far = across(low_send, 4, "mlpy_l")
    gf, gf_low, gcx, sums_one = run(
        norm_one_back_body,
        "norm_one_back",
        [
            sds((slots, width), F32),
            sds((slots, width), BF16),
            sds((4, slots // 2, 2 * COLS), BF16),
            sds((8, width), F32),
        ],
        scalars,
        vecs, own, received, gs, unit_one, rate_one, wo,
    )
    gcs = [gcx[0]] + [chips(gcx[rel], rel, "gcx") for rel in range(1, 4)]
    keep_out, send_out = run(
        out_grads_body,
        "out_grads",
        [sds((CHIPS, COLS, width // 2), F32), sds((CHIPS, COLS, width // 2), BF16)],
        scalars,
        *cxs,
        gf_low,
    )
    keep_mlp, send_mlp = run(
        partial(mlp_grads_body, shards),
        "mlp_grads",
        [sds((shards, rows, width), F32), sds((shards, rows, width), BF16)],
        scalars,
        low_one, low_two, far_one, far_two, gs_low, gs_other, gs_far_one, gs_far_two,
        act, act_far, after(low_keep, send_out), low_far,
    )

    kind = BF16 if groups == 1 else F32

    def spread(low, name, late=()):
        if groups > 1:
            low = lax.psum(low, "ctx", axis_index_groups=sets).astype(BF16)
        here = [low] + [chips(low, rel, name) for rel in range(1, 4)]
        return here + [across(after(jnp.stack(here), *late), 1, name)]

    def fan(size):
        return [sds(size, F32), sds(size, BF16), sds(size, F32), sds(size, BF16)]

    mlp_parts = run(
        partial(fan_body, shards),
        "fan_mlp",
        fan((rows, width)),
        scalars,
        keep_mlp,
        across(send_mlp, 1, "gm"),
    )
    out_parts = run(
        out_fan_body,
        "fan_out",
        [sds((CHIPS, quarter, width // 2), F32)] + [sds((CHIPS, quarter, width // 2), BF16)] * 3,
        scalars,
        keep_out,
        across(send_out, 1, "go"),
    )
    gcs, _, (out_own, *out_sends) = lax.optimization_barrier((gcs, mlp_parts[1], out_parts))
    if groups == 1:
        dq, dk_own, dv_own, dkv = attend_back(gcs, pq, pk, vv, probs, slots, True)
    else:
        count = 4 * slots
        scatter = partial(lax.psum_scatter, axis_name="ctx", axis_index_groups=sets, tiled=True)
        dq, dk, dv = attend_back(gcs, pq, pk, vv, probs, slots, False)
        dk, dv = scatter(dk), scatter(dv)
        dk_own, dv_own = dk[:count], dv[:count]
        dkv = jnp.stack([dk[count:], dv[count:]]).astype(BF16)
    planes = run(
        plane_sum_body,
        "plane_out",
        sds((shards, quarter, width // 2), F32),
        scalars,
        after(out_own, dq),
        *[chips(out_sends[rel - 1], rel, "go") for rel in range(1, 4)],
    )
    gm_far = run(
        relay_halves_body,
        "relay_mlp",
        [sds((rows // 2, width), BF16)] * 2,
        scalars,
        mlp_parts[2],
        after(turn(mlp_parts[3], 1, "gm"), dq),
    )
    gm_near = turn(mlp_parts[1], 1, "gm")
    dkv_rec = across(after(dkv, planes, gm_far, gm_near), 1, "dkv")
    gm_far = [turn(value, 2, "gm") for value in gm_far]
    own, own_far, send, keep_w, send_w = run(
        partial(qkv_grads_body, shards),
        "qkv_grads",
        [
            sds((slots, width), F32),
            sds((slots, width), F32),
            sds((2, slots, width), BF16),
            sds((shards, main + small_rows, WIDE), F32),
            sds((shards, main, WIDE), BF16),
        ],
        scalars,
        meta, dq, dk_own, dv_own, dkv_rec, wall, sums_one, sums_two, sums_up, own_x,
        scratch=[pltpu.VMEM((2, 4 * slots, 2 * WIDE), BF16)],
    )
    size = main + small_rows + quarter
    qkv_parts = run(
        partial(qkv_fan_body, shards),
        "fan_qkv",
        fan((size, WIDE)),
        scalars,
        keep_w,
        across(after(send_w, gm_far[0]), 1, "gq"),
        planes,
    )
    qkv_recs, gq_far = reduce(qkv_parts, "gq")

    near = chips(send, 1, "ig")
    far = run(
        relay_second_body, "relay_ig", sds((slots, width), BF16), scalars, own_far, near
    )
    input_grad = run(
        input_grad_body,
        "input_grad",
        sds((slots, width), F32),
        scalars,
        gf, own, near, chips(far, 2, "ig"),
    )

    mlp_recs = after([gm_near] + gm_far, gq_far, far)
    low = run(
        sum_halves_body, "sum_mlp", sds((rows, width), kind), scalars, mlp_parts[0], *mlp_recs
    )
    done_mlp = spread(low, "gm", (input_grad, qkv_recs))
    ug, dg = run(
        place_mlp_body,
        "place_mlp",
        [sds((rows, ff), F32), sds((part, width), F32)],
        scalars,
        *done_mlp,
        scratch=[pltpu.VMEM((CORES, CHIPS, rows, width), BF16)],
    )
    low = run(
        gather_sum_body, "sum_qkv", sds((size, WIDE), kind), scalars, qkv_parts[0], *qkv_recs
    )
    done_qkv = spread(low, "gq")

    vec = sds((rows,), F32)
    qg, kg, vg, og, qbg, kbg, vbg, obg, g1g, b1g, dbg, g2g, b2g, ubg = run(
        place_qkv_body,
        "place_qkv",
        [
            sds((4, rows, width), F32), sds((rows, width), F32), sds((rows, width), F32),
            sds((rows, width), F32), sds((4, rows), F32), vec, vec, vec, vec, vec, vec, vec, vec,
            sds((4 * rows,), F32),
        ],
        scalars,
        *done_qkv,
        scratch=[pltpu.VMEM((CORES, CHIPS, size, WIDE), BF16)],
    )
    return (
        output[None], input_grad[None], qg, qbg, kg, kbg, vg, vbg, og, obg,
        g1g, b1g, ug, ubg, dg, dbg, g2g, b2g,
    )


def solution(mesh):
    vec, mat = P("shard"), P("shard", None)
    tokens = P("shard", "ctx", None)
    placed = (
        tokens, vec, mat, P(None, "shard", None), P(None, "shard"), mat, vec, mat, vec, mat,
        vec, vec, vec, mat, vec, mat, vec, vec, vec, tokens,
    )
    result = (
        tokens, tokens, P(None, "shard", None), P(None, "shard"), mat, vec, mat, vec, mat, vec,
        vec, vec, mat, vec, mat, vec, vec, vec,
    )
    return jax.shard_map(
        partial(local, mesh.shape["shard"], mesh.shape["ctx"]),
        mesh=mesh,
        in_specs=placed,
        out_specs=result,
        check_vma=False,
    )
```
